128 devices in a mesh: feat: 4 (over z), trainer: 32 (over x, y, core).
Axes of the slice: x: 4, y: 4, z: 4, core: 2. Of those that a mesh axis runs over, the one named last changes fastest.
Arguments:
- features: bfloat16 [128, 131072], P('feat', 'trainer'), may hold values from -6 to 6
- first_adjacent: int32 [65536, 15], P('trainer'), may hold values from 0 to 4095
- first_center: int32 [65536], P('trainer'), may hold values from 0 to 4095
- first_count: int32 [65536], P('trainer'), may hold values from 1 to 15
- owner_map: int32 [65536], P('trainer'), may hold values from 0 to 127, as said below
- first_root: bfloat16 [128, 1024], P('feat'), may hold values from -0.5 to 0.5
- first_near: bfloat16 [128, 1024], P('feat'), may hold values from -0.5 to 0.5
- first_bias: float32 [1024], replicated, may hold values from -3 to 3
- second_adjacent: int32 [65536, 10], P(('feat', 'trainer')), may hold values from 0 to 1023, as said below
- second_center: int32 [65536], P(('feat', 'trainer')), may hold values from 0 to 1023, as said below
- second_count: int32 [65536], P(('feat', 'trainer')), may hold values from 1 to 10
- second_root: bfloat16 [1024, 1024], replicated, may hold values from -0.1875 to 0.1875
- second_near: bfloat16 [1024, 1024], replicated, may hold values from -0.1875 to 0.1875
- second_bias: float32 [1024], replicated, may hold values from -3 to 3
- upstream: bfloat16 [65536, 1024], P(('feat', 'trainer')), may hold values from -0.0234375 to 0.0234375
Outputs:
- layer_output: bfloat16 [65536, 1024], P(('feat', 'trainer'))
- rootgrad_two: float32 [1024, 1024], replicated
- neargrad_two: float32 [1024, 1024], replicated
- biasgrad_two: float32 [1024], replicated
- rootgrad_one: float32 [128, 1024], P('feat')
- neargrad_one: float32 [128, 1024], P('feat')
- biasgrad_one: float32 [1024], replicated
The draws below stay inside these ranges and needn't reach their ends.
Inputs may be any that keep to these rules, and one draw needn't show every extreme that they name: `owner_map`: among the 2048 layer-one nodes of one trainer block at most 32 name any one owner; in every draw some owner is named by exactly 32 nodes of every block, and every owner is named by some node. `second_adjacent`: every entry names a filled row of the owner's table: row s * 32 + c with c smaller than the number of nodes of block s that name this owner. `second_center`: every entry names a filled row of the owner's table, as for second_adjacent.
All inputs are finite; a program needn't handle non-finite values.
Results may differ from the reference program's by a relative error of at most 0.025.
Values may be sent and summed in bfloat16 or wider, within the bound.
No kernel may reach another device: no remote copies, remote signals or barrier semaphores. Data moves between devices by JAX's collectives and lax.ppermute only.
A program may use at most 128 MiB of HBM per device.

```python
import jax
import jax.numpy as jnp
from jax import lax

FEAT_IN = 128
HID = 1024
FAN1 = 15
FAN2 = 10
CAP = 32
IN_DEV = 4096
L2_DEV = 512
NOWN = 128
L1_DEV = 2048
SLOTS = 1024
L1_TOTAL = 65536
IN_TOTAL = 131072
L2_TOTAL = 65536
N_FEAT = 4
N_TRAINER = 32


def owner_blocks(base_key):
    slot_count = NOWN * CAP
    popular = jax.random.randint(jax.random.fold_in(base_key, 11), (NOWN,), 0, 4)
    chosen_owner = jax.random.randint(jax.random.fold_in(base_key, 12), (), 0, NOWN)
    slot_ids = jnp.arange(slot_count, dtype=jnp.int32)
    slot_owner = slot_ids // CAP
    slot_place = slot_ids % CAP

    def one_source(source):
        source_key = jax.random.fold_in(jax.random.fold_in(base_key, 13), source)
        priority = jax.random.randint(source_key, (slot_count,), 0, 4096) + (3 - popular[slot_owner]) * 1024
        forced = (slot_owner == chosen_owner) | (slot_owner % N_TRAINER == source) & (slot_place == 0)
        priority = jnp.where(forced, -1, priority)
        ranking = jnp.argsort(priority * slot_count + slot_ids, stable=True)
        picked = ranking[:L1_DEV]
        shuffle = jax.random.permutation(jax.random.fold_in(source_key, 1), L1_DEV)
        return slot_owner[picked][shuffle]
    return jax.vmap(one_source)(jnp.arange(N_TRAINER, dtype=jnp.int32))


def second_slots(key):
    owners = owner_blocks(jax.random.fold_in(key, 7))
    owner_ids = jnp.arange(NOWN, dtype=jnp.int32)
    load_table = jnp.sum((owners[:, :, None] == owner_ids[None, None, :]).astype(jnp.int32), axis=1)
    load_ends = jnp.cumsum(load_table, axis=0).T
    load_starts = load_ends - load_table.T
    totals = load_ends[:, -1]
    random_bits = jax.random.randint(jax.random.fold_in(key, 21), (NOWN, L2_DEV * (FAN2 + 1)), 0, 1 << 30)
    chosen = random_bits % totals[:, None]
    source = jnp.sum((load_ends[:, None, :] <= chosen[:, :, None]).astype(jnp.int32), axis=2)
    place = chosen - jnp.take_along_axis(load_starts, source, axis=1)
    return (source * CAP + place).reshape(NOWN, L2_DEV, FAN2 + 1)


def draw_owner_map(key, part):
    return owner_blocks(jax.random.fold_in(key, 7)).reshape(-1).astype(jnp.int32)


def draw_second_adjacent(key, part):
    return second_slots(key)[:, :, :FAN2].reshape(NOWN * L2_DEV, FAN2).astype(jnp.int32)


def draw_second_center(key, part):
    return second_slots(key)[:, :, FAN2].reshape(-1).astype(jnp.int32)


def place_ends(entries, rng, low, largest):
    longest = entries.shape.index(max(entries.shape))
    spots = []
    for shift in (0, 1):
        where = [jax.random.randint(jax.random.fold_in(rng, axis), (), 0, length) for axis, length in enumerate(entries.shape)]
        where[longest] = (where[longest] + shift) % entries.shape[longest]
        spots.append(tuple(where))
    return entries.at[spots[0]].set(low).at[spots[1]].set(largest)


def block_levels(rng, shape, shards, least, high):
    level = 1.0
    for dim, blocks in shards:
        steps = jax.random.uniform(jax.random.fold_in(jax.random.fold_in(rng, 6), dim), (blocks,), jnp.float32, least / len(shards), high / len(shards))
        level = level * jnp.repeat(jnp.exp(steps), shape[dim] // blocks).reshape((-1,) + (1,) * (len(shape) - 1 - dim))
    return level


def gaussian(own_key, dims, deviation, reach, shards=(), kind=jnp.bfloat16):
    factor_of = block_levels(own_key, dims, shards, -0.22, 0.18) if shards else 1.0
    drawn = jax.random.normal(own_key, dims, jnp.float32) * deviation * factor_of
    return jnp.minimum(jnp.maximum(drawn, -reach), reach).astype(kind)


def setup_inputs(seed: int = 0) -> dict:
    keys = jax.random.split(jax.random.key(seed), 16)
    return {
        "features": gaussian(keys[0], (FEAT_IN, IN_TOTAL), 1.0, 6.0, ((0, 4), (1, 32))),
        "first_adjacent": place_ends(jax.random.randint(keys[1], (L1_TOTAL, FAN1), 0, IN_DEV), jax.random.fold_in(keys[1], 1), 0, IN_DEV - 1).astype(jnp.int32),
        "first_center": place_ends(jax.random.randint(keys[2], (L1_TOTAL,), 0, IN_DEV), jax.random.fold_in(keys[2], 1), 0, IN_DEV - 1).astype(jnp.int32),
        "first_count": place_ends(jax.random.randint(keys[3], (L1_TOTAL,), 1, FAN1 + 1), jax.random.fold_in(keys[3], 1), 1, FAN1).astype(jnp.int32),
        "owner_map": draw_owner_map(jax.random.fold_in(keys[15], 71), 0),
        "first_root": gaussian(keys[5], (FEAT_IN, HID), FEAT_IN ** -0.5, 0.5, ((0, 4),)),
        "first_near": gaussian(keys[6], (FEAT_IN, HID), FEAT_IN ** -0.5, 0.5, ((0, 4),)),
        "first_bias": gaussian(keys[7], (HID,), 0.5, 3.0, (), jnp.float32),
        "second_adjacent": draw_second_adjacent(jax.random.fold_in(keys[15], 71), 0),
        "second_center": draw_second_center(jax.random.fold_in(keys[15], 71), 0),
        "second_count": place_ends(jax.random.randint(keys[10], (L2_TOTAL,), 1, FAN2 + 1), jax.random.fold_in(keys[10], 1), 1, FAN2).astype(jnp.int32),
        "second_root": gaussian(keys[11], (HID, HID), HID ** -0.5, 0.1875),
        "second_near": gaussian(keys[12], (HID, HID), HID ** -0.5, 0.1875),
        "second_bias": gaussian(keys[13], (HID,), 0.5, 3.0, (), jnp.float32),
        "upstream": gaussian(keys[14], (L2_TOTAL, HID), (1.0 / L2_TOTAL ** 0.5), 0.0234375, ((0, 128),)),
    }


def reference(features, first_adjacent, first_center, first_count, owner_map, first_root, first_near, first_bias, second_adjacent, second_center, second_count, second_root, second_near, second_bias, upstream):
    block_width = FEAT_IN // N_FEAT
    node_ids = jnp.arange(L1_TOTAL, dtype=jnp.int32)
    sources = node_ids // L1_DEV
    columns = features.T
    offsets = sources * IN_DEV
    center_rows = jnp.take(columns, offsets + first_center, axis=0)
    near_total = jnp.zeros((L1_TOTAL, FEAT_IN), jnp.float32)
    for column in range(FAN1):
        picked = jnp.take(columns, offsets + first_adjacent[:, column], axis=0).astype(jnp.float32)
        near_total = near_total + jnp.where((column < first_count)[:, None], picked, jnp.float32(0.0))
    near_rows = (near_total / first_count.astype(jnp.float32)[:, None]).astype(jnp.bfloat16)
    pre_one = jnp.zeros((L1_TOTAL, HID), jnp.float32) + first_bias
    for quarter in range(N_FEAT):
        low = quarter * block_width
        high = low + block_width
        part = jnp.dot(center_rows[:, low:high], first_root[low:high], preferred_element_type=jnp.float32)
        part = part + jnp.dot(near_rows[:, low:high], first_near[low:high], preferred_element_type=jnp.float32)
        pre_one = pre_one + part.astype(jnp.bfloat16).astype(jnp.float32)
    hidden_one = jax.nn.softplus(pre_one).astype(jnp.bfloat16)
    empty_row = jax.nn.softplus(first_bias).astype(jnp.bfloat16)[None, :]
    hidden_pad = jnp.concatenate([hidden_one, empty_row], axis=0)
    onehot = (owner_map.reshape(N_TRAINER, L1_DEV, 1) == jnp.arange(NOWN, dtype=jnp.int32)[None, None, :]).astype(jnp.int32)
    slot_rank = jnp.sum((jnp.cumsum(onehot, axis=1) - onehot) * onehot, axis=2).reshape(-1)
    position = sources * CAP + slot_rank
    table_index = jnp.full((NOWN, SLOTS), L1_TOTAL, jnp.int32).at[owner_map, position].set(node_ids)

    def owner_step(totals, inputs):
        index_row, adjacent, center, count, grad_out = inputs
        hidden_table = jnp.take(hidden_pad, index_row, axis=0)
        root_rows = jnp.take(hidden_table, center, axis=0)
        near_sum = jnp.zeros((L2_DEV, HID), jnp.float32)
        for column in range(FAN2):
            picked = jnp.take(hidden_table, adjacent[:, column], axis=0).astype(jnp.float32)
            near_sum = near_sum + jnp.where((column < count)[:, None], picked, jnp.float32(0.0))
        divisor = count.astype(jnp.float32)[:, None]
        near_two = (near_sum / divisor).astype(jnp.bfloat16)
        pre_two = jnp.dot(root_rows, second_root, preferred_element_type=jnp.float32)
        pre_two = pre_two + jnp.dot(near_two, second_near, preferred_element_type=jnp.float32) + second_bias
        gate = jax.nn.sigmoid(pre_two)
        output_rows = (pre_two * gate).astype(jnp.bfloat16)
        slope_two = (grad_out.astype(jnp.float32) * gate * (1.0 + pre_two * (1.0 - gate))).astype(jnp.bfloat16)
        root_grad = jnp.dot(root_rows.T, slope_two, preferred_element_type=jnp.float32)
        near_grad = jnp.dot(near_two.T, slope_two, preferred_element_type=jnp.float32)
        bias_grad = jnp.sum(slope_two.astype(jnp.float32), axis=0)
        back_root = jnp.dot(slope_two, second_root.T, preferred_element_type=jnp.float32).astype(jnp.bfloat16)
        back_near = (jnp.dot(slope_two, second_near.T, preferred_element_type=jnp.float32) / divisor).astype(jnp.bfloat16)
        table_grad = jnp.zeros((SLOTS, HID), jnp.float32).at[center].add(back_root.astype(jnp.float32))
        usable = jnp.arange(FAN2, dtype=jnp.int32)[None, :] < count[:, None]
        targets = jnp.where(usable, adjacent, SLOTS).reshape(-1)
        spread = jnp.broadcast_to(back_near.astype(jnp.float32)[:, None, :], (L2_DEV, FAN2, HID)).reshape(L2_DEV * FAN2, HID)
        table_grad = table_grad.at[targets].add(spread, mode="drop")
        pre_grad = (table_grad * (1.0 - jnp.exp(-hidden_table.astype(jnp.float32)))).astype(jnp.bfloat16)
        totals = (totals[0] + root_grad, totals[1] + near_grad, totals[2] + bias_grad)
        return totals, (output_rows, pre_grad)

    start = (jnp.zeros((HID, HID), jnp.float32), jnp.zeros((HID, HID), jnp.float32), jnp.zeros((HID,), jnp.float32))
    inputs = (table_index, second_adjacent.reshape(NOWN, L2_DEV, FAN2), second_center.reshape(NOWN, L2_DEV), second_count.reshape(NOWN, L2_DEV), upstream.reshape(NOWN, L2_DEV, HID))
    totals, stacked = lax.scan(owner_step, start, inputs)
    layer_output = stacked[0].reshape(L2_TOTAL, HID)
    node_grad = stacked[1][owner_map, position]
    rootgrad_one = jnp.dot(center_rows.T, node_grad, preferred_element_type=jnp.float32)
    neargrad_one = jnp.dot(near_rows.T, node_grad, preferred_element_type=jnp.float32)
    biasgrad_one = jnp.sum(node_grad.astype(jnp.float32), axis=0)
    return layer_output, totals[0], totals[1], totals[2], rootgrad_one, neargrad_one, biasgrad_one
```

```python
import jax
import jax.numpy as jnp
from jax import lax
from jax.experimental import pallas as pl
from jax.experimental.pallas import tpu as pltpu
from jax.sharding import Mesh, PartitionSpec as P

CAP = 32
LANES = 128
AXES = ("z", "x", "y", "core")
CHIPS = ("z", "x", "y")
CHUNK = 152
VMEM = pl.BlockSpec(memory_space=pltpu.VMEM)
SMEM = pl.BlockSpec(memory_space=pltpu.SMEM)


def lanes_at(at, size=LANES):
    return pl.ds(pl.multiple_of(at * size, size), size)


def across(left, right):
    return lax.dot_general(
        left, right, (((0,), (0,)), ((), ())), preferred_element_type=jnp.float32
    )


def along(left, right):
    return lax.dot_general(
        left, right, (((1,), (1,)), ((), ())), preferred_element_type=jnp.float32
    )


def matmul(left, right):
    return jnp.dot(left, right, preferred_element_type=jnp.float32)


def aggregate_kernel(feat_ref, adj_ref, count_ref, owner_ref, out_ref, table, rows, places, stage):
    width, inputs = feat_ref.shape
    nodes = owner_ref.shape[1]
    owners = out_ref.shape[0]
    fan = adj_ref.shape[0] - 1
    chunks = inputs // LANES
    groups = nodes // LANES
    parts = width // 8
    for c in range(chunks):
        table[c] = feat_ref[:, c * LANES : (c + 1) * LANES].astype(jnp.float32)

    def one_group(g, carry):
        count = count_ref[:, lanes_at(g)]
        total = [jnp.zeros((8, LANES), jnp.float32) for _ in range(parts)]
        for k in range(fan + 1):
            index = jnp.broadcast_to(adj_ref[k : k + 1, lanes_at(g)], (8, LANES))
            high = lax.shift_right_logical(index, 7)
            low = lax.bitwise_and(index, LANES - 1)
            found = [jnp.zeros((8, LANES), jnp.float32) for _ in range(parts)]
            for c in range(chunks):
                here = high == c
                for v in range(parts):
                    got = jnp.take_along_axis(
                        table[c, v * 8 : (v + 1) * 8, :], low, axis=1, mode="promise_in_bounds"
                    )
                    found[v] = jnp.where(here, got, found[v])
            if k < fan:
                valid = jnp.broadcast_to(k < count, (8, LANES))
                total = [a + jnp.where(valid, b, 0.0) for a, b in zip(total, found)]
            else:
                for v in range(parts):
                    rows[v * 8 : (v + 1) * 8, lanes_at(g)] = found[v]
        divisor = jnp.broadcast_to(count.astype(jnp.float32), (8, LANES))
        for v in range(parts):
            rows[width + v * 8 : width + (v + 1) * 8, lanes_at(g)] = total[v] / divisor
        return carry

    lax.fori_loop(0, groups, one_group, 0)

    span = 256
    before = (
        lax.broadcasted_iota(jnp.int32, (span, span), 0)
        < lax.broadcasted_iota(jnp.int32, (span, span), 1)
    ).astype(jnp.bfloat16)
    owner_ids = lax.broadcasted_iota(jnp.int32, (owners, span), 0)
    ranks = lax.broadcasted_iota(jnp.int32, (CAP, span), 0)
    seen = jnp.zeros((owners, 1), jnp.float32)
    found_at = jnp.zeros((3 * CAP, owners), jnp.float32)
    for b in range(nodes // span):
        hit = owner_ids == owner_ref[:, b * span : (b + 1) * span]
        picked = hit.astype(jnp.bfloat16)
        earlier = matmul(picked, before) + seen
        rank = jnp.sum(jnp.where(hit, earlier, 0.0), axis=0, keepdims=True).astype(jnp.int32)
        seen = seen + jnp.sum(jnp.where(hit, 1.0, 0.0), axis=1, keepdims=True)
        node = lax.broadcasted_iota(jnp.int32, (CAP, span), 1) + b * span
        mine = ranks == rank
        weights = jnp.concatenate(
            [
                jnp.where(mine, lax.shift_right_logical(node, 7), 0).astype(jnp.float32),
                jnp.where(mine, lax.bitwise_and(node, LANES - 1), 0).astype(jnp.float32),
                jnp.where(mine, 1.0, 0.0),
            ],
            axis=0,
        ).astype(jnp.bfloat16)
        found_at = found_at + along(weights, picked)
    places[...] = found_at.astype(jnp.int32)

    half = 2 * width
    for pair in range(CAP // 2):
        for j in range(2):
            r = pair * 2 + j
            high = jnp.broadcast_to(places[r : r + 1, :], (8, owners))
            low = jnp.broadcast_to(places[CAP + r : CAP + r + 1, :], (8, owners))
            filled = jnp.broadcast_to(places[2 * CAP + r : 2 * CAP + r + 1, :], (8, owners)) > 0
            for v in range(half // 8):
                found = jnp.zeros((8, owners), jnp.float32)
                for g in range(groups):
                    got = jnp.take_along_axis(
                        rows[v * 8 : (v + 1) * 8, g * LANES : (g + 1) * LANES],
                        low,
                        axis=1,
                        mode="promise_in_bounds",
                    )
                    found = jnp.where(high == g, got, found)
                stage[j * half + v * 8 : j * half + (v + 1) * 8, :] = jnp.where(filled, found, 0.0)
        out_ref[:, pair * LANES : (pair + 1) * LANES] = stage[...].T.astype(out_ref.dtype)


def aggregate(features, adjacent, count, owner, owners):
    width, inputs = features.shape
    nodes = owner.shape[1]
    return pl.pallas_call(
        aggregate_kernel,
        out_shape=jax.ShapeDtypeStruct((owners, CAP * 2 * width), jnp.bfloat16),
        in_specs=[VMEM] * 4,
        out_specs=VMEM,
        scratch_shapes=[
            pltpu.VMEM((inputs // LANES, width, LANES), jnp.float32),
            pltpu.VMEM((2 * width, nodes), jnp.float32),
            pltpu.VMEM((3 * CAP, owners), jnp.int32),
            pltpu.VMEM((4 * width, owners), jnp.float32),
        ],
        name="aggregate",
        cost_estimate=pl.CostEstimate(flops=40_000_000, bytes_accessed=3_000_000, transcendentals=0),
    )(features, adjacent, count, owner)


def picks_kernel(adj_ref, center_ref, count_ref, out_ref, flip_ref):
    nodes, fan = adj_ref.shape
    slots = out_ref.shape[1]

    def table_row(slot):
        return lax.bitwise_and(slot, CAP - 1) * (slots // CAP) + lax.shift_right_logical(slot, 5)

    def one_tile(t, carry):
        at = pl.ds(pl.multiple_of(t * 16, 16), 16)
        number = lax.broadcasted_iota(jnp.int32, (16, fan), 1)
        adjacent = jnp.where(number < count_ref[at, :], table_row(adj_ref[at, :]), -1)
        center = jnp.broadcast_to(table_row(center_ref[at, :]), (16, LANES))
        spread = [jnp.broadcast_to(adjacent[:, k : k + 1], (16, LANES)) for k in range(fan)]
        for c in range(slots // LANES):
            ids = lax.broadcasted_iota(jnp.int32, (16, LANES), 1) + c * LANES
            total = jnp.zeros((16, LANES), jnp.float32)
            for k in range(fan):
                total = total + jnp.where(spread[k] == ids, 1.0, 0.0)
            out_ref[at, c * LANES : (c + 1) * LANES] = jnp.where(center == ids, 1.0, 0.0).astype(
                out_ref.dtype
            )
            low = pl.ds(pl.multiple_of(nodes + t * 16, 16), 16)
            out_ref[low, c * LANES : (c + 1) * LANES] = total.astype(out_ref.dtype)
        return carry

    lax.fori_loop(0, nodes // 16, one_tile, 0)

    def one_flip(t, carry):
        flip_ref[:, lanes_at(t)] = out_ref[lanes_at(t), :].T
        return carry

    lax.fori_loop(0, 2 * nodes // LANES, one_flip, 0)


def picks(adjacent, center, count, slots):
    nodes = adjacent.shape[0]
    return pl.pallas_call(
        picks_kernel,
        out_shape=(
            jax.ShapeDtypeStruct((2 * nodes, slots), jnp.bfloat16),
            jax.ShapeDtypeStruct((slots, 2 * nodes), jnp.bfloat16),
        ),
        in_specs=[VMEM] * 3,
        out_specs=(VMEM, VMEM),
        name="picks",
        cost_estimate=pl.CostEstimate(flops=20_000_000, bytes_accessed=5_000_000, transcendentals=0),
    )(adjacent, center, count)


def owner_kernel(
    core_ref, arrived_ref, first_ref, bias_one_ref, picks_ref, flip_ref, count_ref, root_ref,
    near_ref, bias_two_ref, upstream_ref, out_ref, kept_ref, sent_ref, inputs, inputs_flip,
    hidden, rows, slope, back, bias_grads,
):
    core = core_ref[0]
    slots, depth = inputs.shape
    hidden_width = hidden.shape[1]
    nodes = slope.shape[0]
    quarter = depth // 4
    sources = slots // CAP
    tile = 256
    for r in range(CAP):
        pieces = [
            arrived_ref[f * sources : (f + 1) * sources, r * quarter : (r + 1) * quarter]
            for f in range(4)
        ]
        inputs[r * sources : (r + 1) * sources, :] = jnp.concatenate(pieces, axis=1)
    for t in range(slots // tile):
        inputs_flip[:, t * tile : (t + 1) * tile] = inputs[t * tile : (t + 1) * tile, :].T

    def first_layer(t, carry):
        cols = lanes_at(t, tile)
        pre = matmul(inputs[...], first_ref[:, cols]) + bias_one_ref[:, cols]
        value = jnp.maximum(pre, 0.0) + jnp.log1p(jnp.exp(-jnp.abs(pre)))
        hidden[:, cols] = value.astype(jnp.bfloat16)
        return carry

    lax.fori_loop(0, hidden_width // tile, first_layer, 0)
    inverse = 1.0 / count_ref[...].astype(jnp.float32)

    def select(t, carry):
        cols = lanes_at(t, tile)
        rows[:nodes, cols] = matmul(picks_ref[:nodes, :], hidden[:, cols]).astype(jnp.bfloat16)
        total = matmul(picks_ref[nodes:, :], hidden[:, cols])
        rows[nodes:, cols] = (total * inverse).astype(jnp.bfloat16)
        return carry

    lax.fori_loop(0, hidden_width // tile, select, 0)

    def second_layer(t, carry):
        cols = lanes_at(t, tile)
        pre = matmul(rows[:nodes, :], root_ref[:, cols]) + matmul(rows[nodes:, :], near_ref[:, cols])
        pre = pre + bias_two_ref[:, cols]
        gate = jax.nn.sigmoid(pre)
        out_ref[:, cols] = (pre * gate).astype(jnp.bfloat16)
        grad = upstream_ref[:, cols].astype(jnp.float32) * gate * (1.0 + pre * (1.0 - gate))
        grad = grad.astype(jnp.bfloat16)
        slope[:, cols] = grad
        bias_grads[0:1, cols] = jnp.sum(grad.astype(jnp.float32), axis=0, keepdims=True)
        return carry

    lax.fori_loop(0, hidden_width // tile, second_layer, 0)

    for place, to_ref in enumerate((kept_ref, sent_ref)):
        which = core ^ place

        def weight_grads(t, carry, to_ref=to_ref, which=which):
            left = rows[pl.ds(pl.multiple_of(which * nodes, nodes), nodes), lanes_at(t, tile)]
            product = across(left, slope[...]).astype(jnp.bfloat16)
            for c in range(tile // 16):
                for lane in range(hidden_width // LANES):
                    to_ref[t * (tile // 16) + c, lane * 16 : (lane + 1) * 16, :] = product[
                        c * 16 : (c + 1) * 16, lane * LANES : (lane + 1) * LANES
                    ]
            return carry

        lax.fori_loop(0, hidden_width // tile, weight_grads, 0)

    def backward(t, carry):
        cols = lanes_at(t, tile)
        back[:nodes, cols] = along(slope[...], root_ref[cols, :]).astype(jnp.bfloat16)
        near = along(slope[...], near_ref[cols, :])
        back[nodes:, cols] = (near * inverse).astype(jnp.bfloat16)
        return carry

    lax.fori_loop(0, hidden_width // tile, backward, 0)

    def first_grads(t, carry):
        cols = lanes_at(t, tile)
        table_grad = matmul(flip_ref[...], back[:, cols])
        grad = table_grad * (1.0 - jnp.exp(-hidden[:, cols].astype(jnp.float32)))
        grad = grad.astype(jnp.bfloat16)
        bias_grads[1:2, cols] = jnp.sum(grad.astype(jnp.float32), axis=0, keepdims=True)
        for place, to_ref in enumerate((kept_ref, sent_ref)):
            which = core ^ place
            left = inputs_flip[pl.ds(pl.multiple_of(which * LANES, LANES), LANES), :]
            product = matmul(left, grad).astype(jnp.bfloat16)
            for c in range(8):
                for lane in range(tile // LANES):
                    chunk = c * 8 + t * (tile // LANES) + lane
                    to_ref[chunk, LANES : LANES + 16, :] = product[
                        c * 16 : (c + 1) * 16, lane * LANES : (lane + 1) * LANES
                    ]
        return carry

    lax.fori_loop(0, hidden_width // tile, first_grads, 0)
    for place, to_ref in enumerate((kept_ref, sent_ref)):
        which = core ^ place
        to_ref[:, LANES + 16 :, :] = jnp.zeros((to_ref.shape[0], 8, LANES), jnp.bfloat16)
        for lane in range(8):
            cols = slice(lane * LANES, (lane + 1) * LANES)
            row = jnp.where(which == 0, bias_grads[0:1, cols], bias_grads[1:2, cols])
            to_ref[lane, LANES + 16 :, :] = jnp.broadcast_to(row, (8, LANES)).astype(jnp.bfloat16)


def owner_step(
    core, arrived, first, bias_one, picked, flipped, count, root, near, bias_two, upstream
):
    nodes, hidden_width = upstream.shape
    slots = picked.shape[1]
    depth = first.shape[0]
    bf16, f32 = jnp.bfloat16, jnp.float32
    share = jax.ShapeDtypeStruct((64, CHUNK, LANES), bf16)
    return pl.pallas_call(
        owner_kernel,
        out_shape=(jax.ShapeDtypeStruct((nodes, hidden_width), bf16), share, share),
        in_specs=[SMEM] + [VMEM] * 10,
        out_specs=(VMEM, VMEM, VMEM),
        scratch_shapes=[
            pltpu.VMEM((slots, depth), bf16),
            pltpu.VMEM((depth, slots), bf16),
            pltpu.VMEM((slots, hidden_width), bf16),
            pltpu.VMEM((2 * nodes, hidden_width), bf16),
            pltpu.VMEM((nodes, hidden_width), bf16),
            pltpu.VMEM((2 * nodes, hidden_width), bf16),
            pltpu.VMEM((8, hidden_width), f32),
        ],
        name="owner_step",
        cost_estimate=pl.CostEstimate(
            flops=12_000_000_000, bytes_accessed=18_000_000, transcendentals=3_000_000
        ),
    )(core, arrived, first, bias_one, picked, flipped, count, root, near, bias_two, upstream)


def spread_kernel(core_ref, z_ref, kept_ref, other_ref, root_ref, near_ref, first_root_ref, first_near_ref, bias_two_ref, bias_one_ref):
    even = core_ref[0] == 0
    z = z_ref[0]

    def one_chunk(c, carry):
        at = pl.ds(pl.multiple_of(c * 16, 16), 16)
        for lane in range(8):
            kept = kept_ref[c, lane * 16 : (lane + 1) * 16, :].astype(jnp.float32)
            other = other_ref[c, lane * 16 : (lane + 1) * 16, :].astype(jnp.float32)
            cols = slice(lane * LANES, (lane + 1) * LANES)
            root_ref[at, cols] = jnp.where(even, kept, other)
            near_ref[at, cols] = jnp.where(even, other, kept)
        return carry

    lax.fori_loop(0, 64, one_chunk, 0)
    here = lax.shift_right_logical(z, 1) == core_ref[0]
    base = lax.bitwise_and(z, 1) * 4
    for j, to_ref in enumerate((first_root_ref, first_near_ref)):
        for i in range(2):
            for lane in range(8):
                chunk = (base + 2 * j + i) * 8 + lane
                kept = kept_ref[chunk, LANES : LANES + 16, :].astype(jnp.float32)
                other = other_ref[chunk, LANES : LANES + 16, :].astype(jnp.float32)
                to_ref[i * 16 : (i + 1) * 16, lane * LANES : (lane + 1) * LANES] = jnp.where(
                    here, kept, other
                )
    for lane in range(8):
        kept = kept_ref[lane, LANES + 16 :, :].astype(jnp.float32)[0:1, :]
        other = other_ref[lane, LANES + 16 :, :].astype(jnp.float32)[0:1, :]
        cols = slice(lane * LANES, (lane + 1) * LANES)
        bias_two_ref[:, cols] = jnp.where(even, kept, other)
        bias_one_ref[:, cols] = jnp.where(even, other, kept)


def spread(core, z, kept, other, hidden_width):
    f32 = jnp.float32
    square = jax.ShapeDtypeStruct((hidden_width, hidden_width), f32)
    slab = jax.ShapeDtypeStruct((32, hidden_width), f32)
    line = jax.ShapeDtypeStruct((1, hidden_width), f32)
    return pl.pallas_call(
        spread_kernel,
        out_shape=(square, square, slab, slab, line, line),
        in_specs=[SMEM, SMEM, VMEM, VMEM],
        out_specs=(VMEM,) * 6,
        name="spread",
    )(core, z, kept, other)


def weights_of_all(own, z):
    first = lax.ppermute(own, "z", [(0, 1), (1, 0), (2, 3), (3, 2)])
    odd = lax.bitwise_and(z, 1) == 1
    pair = jnp.concatenate([jnp.where(odd, first, own), jnp.where(odd, own, first)], axis=0)
    second = lax.ppermute(pair, "z", [(0, 3), (3, 0), (1, 2), (2, 1)])
    late = z >= 2
    return jnp.concatenate([jnp.where(late, second, pair), jnp.where(late, pair, second)], axis=0)


def exchange(value, axes):
    return lax.all_to_all(value, axes, split_axis=0, concat_axis=0, tiled=True)


def local(
    features,
    first_adjacent,
    first_center,
    first_count,
    owner_map,
    first_root,
    first_near,
    first_bias,
    second_adjacent,
    second_center,
    second_count,
    second_root,
    second_near,
    second_bias,
    upstream,
):
    owners = 128
    hidden_width = first_root.shape[1]
    z = lax.axis_index("z")
    core = lax.axis_index("core")[None]
    first_all = weights_of_all(jnp.concatenate([first_root, first_near], axis=0), z)
    columns = jnp.concatenate([first_adjacent, first_center[:, None]], axis=1).T
    packed = aggregate(features, columns, first_count[None], owner_map[None], owners)
    arrived = exchange(packed, AXES)
    count = second_count[:, None]
    picked, flipped = picks(second_adjacent, second_center[:, None], count, owners * 8)
    layer_output, kept, sent = owner_step(
        core, arrived, first_all, first_bias[None], picked, flipped, count, second_root,
        second_near, second_bias[None], upstream,
    )
    received = lax.ppermute(sent, "core", [(0, 1), (1, 0)])
    both = (kept.astype(jnp.float32) + received.astype(jnp.float32)).astype(jnp.bfloat16)
    terms = exchange(both, CHIPS)
    total = jnp.sum(terms.astype(jnp.float32), axis=0).astype(jnp.bfloat16)
    mine = exchange(jnp.broadcast_to(total[None], terms.shape), CHIPS)
    other = lax.ppermute(mine, "core", [(0, 1), (1, 0)])
    root_two, near_two, root_one, near_one, bias_two, bias_one = spread(
        core, z[None], mine, other, hidden_width
    )
    return (layer_output, root_two, near_two, bias_two[0], root_one, near_one, bias_one[0])


def solution(mesh):
    chips = Mesh(mesh.devices.reshape(4, 4, 4, 2), AXES)
    trainer = ("x", "y", "core")
    return jax.shard_map(
        local,
        mesh=chips,
        in_specs=(
            P("z", trainer),
            P(trainer, None),
            P(trainer),
            P(trainer),
            P(trainer),
            P("z", None),
            P("z", None),
            P(),
            P(AXES, None),
            P(AXES),
            P(AXES),
            P(),
            P(),
            P(),
            P(AXES, None),
        ),
        out_specs=(
            P(AXES, None),
            P(),
            P(),
            P(),
            P("z", None),
            P("z", None),
            P(),
        ),
        check_vma=False,
    )
```

```python
import jax
import jax.numpy as jnp
from jax import lax
from jax.experimental import pallas as pl
from jax.experimental.pallas import tpu as pltpu
from jax.sharding import Mesh, PartitionSpec as P

CAP = 32
LANES = 128
AXES = ("z", "x", "y", "core")
CHIPS = ("z", "x", "y")
CHUNK = 152
VMEM = pl.BlockSpec(memory_space=pltpu.VMEM)
ALONG_LANES = lax.GatherDimensionNumbers(
    offset_dims=(),
    collapsed_slice_dims=(1,),
    start_index_map=(1,),
    operand_batching_dims=(0,),
    start_indices_batching_dims=(0,),
)
SMEM = pl.BlockSpec(memory_space=pltpu.SMEM)


def lanes_at(at, size=LANES):
    return pl.ds(pl.multiple_of(at * size, size), size)


def across(left, right):
    return lax.dot_general(
        left, right, (((0,), (0,)), ((), ())), preferred_element_type=jnp.float32
    )


def along(left, right):
    return lax.dot_general(
        left, right, (((1,), (1,)), ((), ())), preferred_element_type=jnp.float32
    )


def matmul(left, right):
    return jnp.dot(left, right, preferred_element_type=jnp.float32)


def take_lanes(rows, index):
    return lax.gather(
        rows, index[..., None], ALONG_LANES, (1, 1), mode=lax.GatherScatterMode.PROMISE_IN_BOUNDS
    )


def find(load, high, low, chunks, parts):
    bits = [lax.bitwise_and(high, jnp.int16(1 << b)) != jnp.int16(0) for b in range(5)]

    def among(start, size, bit):
        if size == 1:
            return [take_lanes(load(start, v), low) for v in range(parts)]
        first = among(start, size // 2, bit - 1)
        last = among(start + size // 2, size // 2, bit - 1)
        return [jnp.where(bits[bit], q, p) for p, q in zip(first, last)]

    return among(0, chunks, chunks.bit_length() - 2)


def aggregate_kernel(feat_ref, adj_ref, count_ref, owner_ref, out_ref, index, rows, places, stage, wide):
    width, inputs = feat_ref.shape
    nodes = owner_ref.shape[1]
    owners = out_ref.shape[0]
    fan = adj_ref.shape[0] - 1
    chunks = inputs // LANES
    groups = nodes // LANES
    parts = width // 16
    steps = (fan + 1) // 4
    i16, bf16, f32 = jnp.int16, jnp.bfloat16, jnp.float32
    for g in range(groups):
        for s in range(steps):
            index[g * steps + s, 0:4] = adj_ref[s * 4 : s * 4 + 4, g * LANES : (g + 1) * LANES]

    def one_group(g, carry):
        count = count_ref[:, lanes_at(g)]

        def four(s, total):
            total = list(total)
            for j in range(4):
                at = index[g * steps + s, j : j + 1, :]
                high = jnp.broadcast_to(lax.shift_right_logical(at, 7), (16, LANES)).astype(i16)
                low = jnp.broadcast_to(lax.bitwise_and(at, LANES - 1), (16, LANES)).astype(i16)
                valid = jnp.broadcast_to(s * 4 + j < count, (16, LANES))
                found = find(
                    lambda c, v: feat_ref[v * 16 : (v + 1) * 16, c * LANES : (c + 1) * LANES],
                    high, low, chunks, parts,
                )
                if j == 3:
                    for v in range(parts):
                        rows[v * 16 : (v + 1) * 16, lanes_at(g)] = found[v]
                for v in range(parts):
                    total[v] = total[v] + jnp.where(valid, found[v].astype(f32), 0.0)
            return tuple(total)

        zero = jnp.zeros((16, LANES), f32)
        total = lax.fori_loop(0, steps, four, (zero,) * parts)
        divisor = jnp.broadcast_to(count.astype(f32), (16, LANES))
        for v in range(parts):
            near = (total[v] / divisor).astype(bf16)
            rows[width + v * 16 : width + (v + 1) * 16, lanes_at(g)] = near
        return carry

    lax.fori_loop(0, groups, one_group, 0)

    span = 256
    before = (
        lax.broadcasted_iota(jnp.int32, (span, span), 0)
        < lax.broadcasted_iota(jnp.int32, (span, span), 1)
    ).astype(bf16)
    owner_ids = lax.broadcasted_iota(jnp.int32, (owners, span), 0)
    ranks = lax.broadcasted_iota(jnp.int32, (CAP, span), 0)
    seen = jnp.zeros((owners, 1), f32)
    found_at = jnp.zeros((3 * CAP, owners), f32)
    for b in range(nodes // span):
        hit = owner_ids == owner_ref[:, b * span : (b + 1) * span]
        picked = hit.astype(bf16)
        earlier = matmul(picked, before) + seen
        rank = jnp.sum(jnp.where(hit, earlier, 0.0), axis=0, keepdims=True).astype(jnp.int32)
        seen = seen + jnp.sum(jnp.where(hit, 1.0, 0.0), axis=1, keepdims=True)
        node = lax.broadcasted_iota(jnp.int32, (CAP, span), 1) + b * span
        mine = ranks == rank
        weights = jnp.concatenate(
            [
                jnp.where(mine, lax.shift_right_logical(node, 7), 0).astype(f32),
                jnp.where(mine, lax.bitwise_and(node, LANES - 1), 0).astype(f32),
                jnp.where(mine, 1.0, 0.0),
            ],
            axis=0,
        ).astype(bf16)
        found_at = found_at + along(weights, picked)
    found_at = found_at.astype(jnp.int32)
    for q in range(CAP // 4):
        for kind in range(3):
            at = kind * CAP + q * 4
            places[q, kind * 4 : (kind + 1) * 4] = found_at[at : at + 4]

    half = 2 * width

    def four_ranks(q, carry):
        for j in range(4):
            high = jnp.broadcast_to(places[q, j : j + 1, :], (16, owners)).astype(i16)
            low = jnp.broadcast_to(places[q, 4 + j : 5 + j, :], (16, owners)).astype(i16)
            filled = jnp.broadcast_to(places[q, 8 + j : 9 + j, :], (16, owners)) > 0
            found = find(
                lambda c, v: rows[v * 16 : (v + 1) * 16, c * LANES : (c + 1) * LANES],
                high, low, groups, half // 16,
            )
            for v in range(half // 16):
                at = (j % 2) * half + v * 16
                stage[j // 2, at : at + 16, :] = jnp.where(filled, found[v].astype(f32), 0.0)
        for pair in range(2):
            wide[pl.ds(q * 2 + pair, owners, stride=16), :] = stage[pair].T
        return carry

    lax.fori_loop(0, CAP // 4, four_ranks, 0)

    def finish(t, carry):
        at = pl.ds(pl.multiple_of(t * 8, 8), 8)
        out_ref[at] = wide[lanes_at(t), :].astype(bf16).reshape(8, 16, LANES)
        return carry

    lax.fori_loop(0, owners // 8, finish, 0)


def aggregate(features, adjacent, count, owner, owners):
    width, inputs = features.shape
    nodes = owner.shape[1]
    return pl.pallas_call(
        aggregate_kernel,
        out_shape=jax.ShapeDtypeStruct((owners, 16, LANES), jnp.bfloat16),
        in_specs=[VMEM] * 4,
        out_specs=VMEM,
        scratch_shapes=[
            pltpu.VMEM((nodes // LANES * 4, 4, LANES), jnp.int32),
            pltpu.VMEM((2 * width, nodes), jnp.bfloat16),
            pltpu.VMEM((CAP // 4, 12, LANES), jnp.int32),
            pltpu.VMEM((2, 4 * width, owners), jnp.float32),
            pltpu.VMEM((16 * owners, LANES), jnp.float32),
        ],
        name="aggregate",
        cost_estimate=pl.CostEstimate(flops=40_000_000, bytes_accessed=3_000_000, transcendentals=0),
    )(features, adjacent, count, owner)


def picks_kernel(adj_ref, center_ref, count_ref, out_ref, flip_ref):
    nodes, fan = adj_ref.shape
    slots = out_ref.shape[1]

    def table_row(slot):
        odd = lax.shift_left(lax.bitwise_and(slot, 1), 4)
        pair = lax.bitwise_and(lax.shift_right_logical(slot, 1), 15)
        return lax.bitwise_and(slot, -CAP) + odd + pair

    def one_tile(t, carry):
        at = pl.ds(pl.multiple_of(t * 16, 16), 16)
        number = lax.broadcasted_iota(jnp.int32, (16, fan), 1)
        adjacent = jnp.where(number < count_ref[at, :], table_row(adj_ref[at, :]), -1)
        center = jnp.broadcast_to(table_row(center_ref[at, :]), (16, LANES))
        spread = [jnp.broadcast_to(adjacent[:, k : k + 1], (16, LANES)) for k in range(fan)]
        for c in range(slots // LANES):
            ids = lax.broadcasted_iota(jnp.int32, (16, LANES), 1) + c * LANES
            total = jnp.zeros((16, LANES), jnp.float32)
            for k in range(fan):
                total = total + jnp.where(spread[k] == ids, 1.0, 0.0)
            out_ref[at, c * LANES : (c + 1) * LANES] = jnp.where(center == ids, 1.0, 0.0).astype(
                out_ref.dtype
            )
            low = pl.ds(pl.multiple_of(nodes + t * 16, 16), 16)
            out_ref[low, c * LANES : (c + 1) * LANES] = total.astype(out_ref.dtype)
        return carry

    lax.fori_loop(0, nodes // 16, one_tile, 0)

    def one_flip(t, carry):
        flip_ref[:, lanes_at(t)] = out_ref[lanes_at(t), :].T
        return carry

    lax.fori_loop(0, 2 * nodes // LANES, one_flip, 0)


def picks(adjacent, center, count, slots):
    nodes = adjacent.shape[0]
    return pl.pallas_call(
        picks_kernel,
        out_shape=(
            jax.ShapeDtypeStruct((2 * nodes, slots), jnp.bfloat16),
            jax.ShapeDtypeStruct((slots, 2 * nodes), jnp.bfloat16),
        ),
        in_specs=[VMEM] * 3,
        out_specs=(VMEM, VMEM),
        name="picks",
        cost_estimate=pl.CostEstimate(flops=20_000_000, bytes_accessed=5_000_000, transcendentals=0),
    )(adjacent, center, count)


def owner_kernel(
    core_ref, arrived_ref, first_ref, bias_one_ref, picks_ref, flip_ref, count_ref, root_ref,
    near_ref, bias_two_ref, upstream_ref, out_ref, kept_ref, sent_ref, inputs, inputs_flip,
    hidden, rows, slope, back, bias_grads,
):
    core = core_ref[0]
    slots, depth = inputs.shape
    hidden_width = hidden.shape[1]
    nodes = slope.shape[0]
    quarter = depth // 4
    sources = slots // CAP
    tile = 256

    def one_source(t, carry):
        for e in range(2):
            pieces = [
                arrived_ref[f * sources + t, :, e * quarter : (e + 1) * quarter] for f in range(4)
            ]
            at = pl.ds(pl.multiple_of(t * CAP + e * 16, 16), 16)
            inputs[at, :] = jnp.concatenate(pieces, axis=1)
        return carry

    lax.fori_loop(0, sources, one_source, 0)
    for t in range(slots // tile):
        inputs_flip[:, t * tile : (t + 1) * tile] = inputs[t * tile : (t + 1) * tile, :].T

    def first_layer(t, carry):
        cols = lanes_at(t, tile)
        pre = matmul(inputs[...], first_ref[:, cols]) + bias_one_ref[:, cols]
        value = jnp.maximum(pre, 0.0) + jnp.log1p(jnp.exp(-jnp.abs(pre)))
        hidden[:, cols] = value.astype(jnp.bfloat16)
        return carry

    lax.fori_loop(0, hidden_width // tile, first_layer, 0)
    inverse = 1.0 / count_ref[...].astype(jnp.float32)

    def select(t, carry):
        cols = lanes_at(t, tile)
        rows[:nodes, cols] = matmul(picks_ref[:nodes, :], hidden[:, cols]).astype(jnp.bfloat16)
        total = matmul(picks_ref[nodes:, :], hidden[:, cols])
        rows[nodes:, cols] = (total * inverse).astype(jnp.bfloat16)
        return carry

    lax.fori_loop(0, hidden_width // tile, select, 0)

    def second_layer(t, carry):
        cols = lanes_at(t, tile)
        pre = matmul(rows[:nodes, :], root_ref[:, cols]) + matmul(rows[nodes:, :], near_ref[:, cols])
        pre = pre + bias_two_ref[:, cols]
        gate = jax.nn.sigmoid(pre)
        out_ref[:, cols] = (pre * gate).astype(jnp.bfloat16)
        grad = upstream_ref[:, cols].astype(jnp.float32) * gate * (1.0 + pre * (1.0 - gate))
        grad = grad.astype(jnp.bfloat16)
        slope[:, cols] = grad
        bias_grads[0:1, cols] = jnp.sum(grad.astype(jnp.float32), axis=0, keepdims=True)
        return carry

    lax.fori_loop(0, hidden_width // tile, second_layer, 0)

    for place, to_ref in enumerate((kept_ref, sent_ref)):
        which = core ^ place

        def weight_grads(t, carry, to_ref=to_ref, which=which):
            left = rows[pl.ds(pl.multiple_of(which * nodes, nodes), nodes), lanes_at(t, tile)]
            product = across(left, slope[...]).astype(jnp.bfloat16)
            for c in range(tile // 16):
                for lane in range(hidden_width // LANES):
                    to_ref[t * (tile // 16) + c, lane * 16 : (lane + 1) * 16, :] = product[
                        c * 16 : (c + 1) * 16, lane * LANES : (lane + 1) * LANES
                    ]
            return carry

        lax.fori_loop(0, hidden_width // tile, weight_grads, 0)

    def backward(t, carry):
        cols = lanes_at(t, tile)
        back[:nodes, cols] = along(slope[...], root_ref[cols, :]).astype(jnp.bfloat16)
        near = along(slope[...], near_ref[cols, :])
        back[nodes:, cols] = (near * inverse).astype(jnp.bfloat16)
        return carry

    lax.fori_loop(0, hidden_width // tile, backward, 0)

    def first_grads(t, carry):
        cols = lanes_at(t, tile)
        table_grad = matmul(flip_ref[...], back[:, cols])
        grad = table_grad * (1.0 - jnp.exp(-hidden[:, cols].astype(jnp.float32)))
        grad = grad.astype(jnp.bfloat16)
        bias_grads[1:2, cols] = jnp.sum(grad.astype(jnp.float32), axis=0, keepdims=True)
        for place, to_ref in enumerate((kept_ref, sent_ref)):
            which = core ^ place
            left = inputs_flip[pl.ds(pl.multiple_of(which * LANES, LANES), LANES), :]
            product = matmul(left, grad).astype(jnp.bfloat16)
            for c in range(8):
                for lane in range(tile // LANES):
                    chunk = c * 8 + t * (tile // LANES) + lane
                    to_ref[chunk, LANES : LANES + 16, :] = product[
                        c * 16 : (c + 1) * 16, lane * LANES : (lane + 1) * LANES
                    ]
        return carry

    lax.fori_loop(0, hidden_width // tile, first_grads, 0)
    for place, to_ref in enumerate((kept_ref, sent_ref)):
        which = core ^ place
        to_ref[:, LANES + 16 :, :] = jnp.zeros((to_ref.shape[0], 8, LANES), jnp.bfloat16)
        for lane in range(8):
            cols = slice(lane * LANES, (lane + 1) * LANES)
            row = jnp.where(which == 0, bias_grads[0:1, cols], bias_grads[1:2, cols])
            to_ref[lane, LANES + 16 :, :] = jnp.broadcast_to(row, (8, LANES)).astype(jnp.bfloat16)


def owner_step(
    core, arrived, first, bias_one, picked, flipped, count, root, near, bias_two, upstream
):
    nodes, hidden_width = upstream.shape
    slots = picked.shape[1]
    depth = first.shape[0]
    bf16, f32 = jnp.bfloat16, jnp.float32
    share = jax.ShapeDtypeStruct((64, CHUNK, LANES), bf16)
    return pl.pallas_call(
        owner_kernel,
        out_shape=(jax.ShapeDtypeStruct((nodes, hidden_width), bf16), share, share),
        in_specs=[SMEM] + [VMEM] * 10,
        out_specs=(VMEM, VMEM, VMEM),
        scratch_shapes=[
            pltpu.VMEM((slots, depth), bf16),
            pltpu.VMEM((depth, slots), bf16),
            pltpu.VMEM((slots, hidden_width), bf16),
            pltpu.VMEM((2 * nodes, hidden_width), bf16),
            pltpu.VMEM((nodes, hidden_width), bf16),
            pltpu.VMEM((2 * nodes, hidden_width), bf16),
            pltpu.VMEM((8, hidden_width), f32),
        ],
        name="owner_step",
        cost_estimate=pl.CostEstimate(
            flops=12_000_000_000, bytes_accessed=18_000_000, transcendentals=3_000_000
        ),
    )(core, arrived, first, bias_one, picked, flipped, count, root, near, bias_two, upstream)


def spread_kernel(core_ref, z_ref, kept_ref, other_ref, root_ref, near_ref, first_root_ref, first_near_ref, bias_two_ref, bias_one_ref):
    even = core_ref[0] == 0
    z = z_ref[0]

    def one_chunk(c, carry):
        at = pl.ds(pl.multiple_of(c * 16, 16), 16)
        for lane in range(8):
            kept = kept_ref[c, lane * 16 : (lane + 1) * 16, :].astype(jnp.float32)
            other = other_ref[c, lane * 16 : (lane + 1) * 16, :].astype(jnp.float32)
            cols = slice(lane * LANES, (lane + 1) * LANES)
            root_ref[at, cols] = jnp.where(even, kept, other)
            near_ref[at, cols] = jnp.where(even, other, kept)
        return carry

    lax.fori_loop(0, 64, one_chunk, 0)
    here = lax.shift_right_logical(z, 1) == core_ref[0]
    base = lax.bitwise_and(z, 1) * 4
    for j, to_ref in enumerate((first_root_ref, first_near_ref)):
        for i in range(2):
            for lane in range(8):
                chunk = (base + 2 * j + i) * 8 + lane
                kept = kept_ref[chunk, LANES : LANES + 16, :].astype(jnp.float32)
                other = other_ref[chunk, LANES : LANES + 16, :].astype(jnp.float32)
                to_ref[i * 16 : (i + 1) * 16, lane * LANES : (lane + 1) * LANES] = jnp.where(
                    here, kept, other
                )
    for lane in range(8):
        kept = kept_ref[lane, LANES + 16 :, :].astype(jnp.float32)[0:1, :]
        other = other_ref[lane, LANES + 16 :, :].astype(jnp.float32)[0:1, :]
        cols = slice(lane * LANES, (lane + 1) * LANES)
        bias_two_ref[:, cols] = jnp.where(even, kept, other)
        bias_one_ref[:, cols] = jnp.where(even, other, kept)


def spread(core, z, kept, other, hidden_width):
    f32 = jnp.float32
    square = jax.ShapeDtypeStruct((hidden_width, hidden_width), f32)
    slab = jax.ShapeDtypeStruct((32, hidden_width), f32)
    line = jax.ShapeDtypeStruct((1, hidden_width), f32)
    return pl.pallas_call(
        spread_kernel,
        out_shape=(square, square, slab, slab, line, line),
        in_specs=[SMEM, SMEM, VMEM, VMEM],
        out_specs=(VMEM,) * 6,
        name="spread",
    )(core, z, kept, other)


def weights_of_pair(own, z):
    first = lax.ppermute(own, "z", [(0, 1), (1, 0), (2, 3), (3, 2)])
    odd = lax.bitwise_and(z, 1) == 1
    return jnp.concatenate([jnp.where(odd, first, own), jnp.where(odd, own, first)], axis=0)


def weights_of_all(pair, z):
    second = lax.ppermute(pair, "z", [(0, 3), (3, 0), (1, 2), (2, 1)])
    late = z >= 2
    return jnp.concatenate([jnp.where(late, second, pair), jnp.where(late, pair, second)], axis=0)


def exchange(value, axes):
    return lax.all_to_all(value, axes, split_axis=0, concat_axis=0, tiled=True)


def local(
    features,
    first_adjacent,
    first_center,
    first_count,
    owner_map,
    first_root,
    first_near,
    first_bias,
    second_adjacent,
    second_center,
    second_count,
    second_root,
    second_near,
    second_bias,
    upstream,
):
    owners = 128
    hidden_width = first_root.shape[1]
    z = lax.axis_index("z")
    core = lax.axis_index("core")[None]
    pair = weights_of_pair(jnp.concatenate([first_root, first_near], axis=0), z)
    columns = jnp.concatenate([first_adjacent, first_center[:, None]], axis=1).T
    packed = aggregate(features, columns, first_count[None], owner_map[None], owners)
    packed, pair = lax.optimization_barrier((packed, pair))
    first_all = weights_of_all(pair, z)
    arrived = exchange(packed, AXES)
    count = second_count[:, None]
    picked, flipped = picks(second_adjacent, second_center[:, None], count, owners * 8)
    layer_output, kept, sent = owner_step(
        core, arrived, first_all, first_bias[None], picked, flipped, count, second_root,
        second_near, second_bias[None], upstream,
    )
    received = lax.ppermute(sent, "core", [(0, 1), (1, 0)])
    both = (kept.astype(jnp.float32) + received.astype(jnp.float32)).astype(jnp.bfloat16)
    terms = exchange(both, CHIPS)
    total = jnp.sum(terms.astype(jnp.float32), axis=0).astype(jnp.bfloat16)
    mine = exchange(jnp.broadcast_to(total[None], terms.shape), CHIPS)
    other = lax.ppermute(mine, "core", [(0, 1), (1, 0)])
    root_two, near_two, root_one, near_one, bias_two, bias_one = spread(
        core, z[None], mine, other, hidden_width
    )
    return (layer_output, root_two, near_two, bias_two[0], root_one, near_one, bias_one[0])


def solution(mesh):
    chips = Mesh(mesh.devices.reshape(4, 4, 4, 2), AXES)
    trainer = ("x", "y", "core")
    return jax.shard_map(
        local,
        mesh=chips,
        in_specs=(
            P("z", trainer),
            P(trainer, None),
            P(trainer),
            P(trainer),
            P(trainer),
            P("z", None),
            P("z", None),
            P(),
            P(AXES, None),
            P(AXES),
            P(AXES),
            P(),
            P(),
            P(),
            P(AXES, None),
        ),
        out_specs=(
            P(AXES, None),
            P(),
            P(),
            P(),
            P("z", None),
            P("z", None),
            P(),
        ),
        check_vma=False,
    )
```

```python
import jax
import jax.numpy as jnp
from jax import lax
from jax.experimental import pallas as pl
from jax.experimental.pallas import tpu as pltpu
from jax.sharding import Mesh, PartitionSpec as P


CAP = 32
LANES = 128
AXES = ("z", "x", "y", "core")
CHIPS = ("z", "x", "y")
CHUNK = 152
VMEM = pl.BlockSpec(memory_space=pltpu.VMEM)
ALONG_LANES = lax.GatherDimensionNumbers(
    offset_dims=(),
    collapsed_slice_dims=(1,),
    start_index_map=(1,),
    operand_batching_dims=(0,),
    start_indices_batching_dims=(0,),
)
SMEM = pl.BlockSpec(memory_space=pltpu.SMEM)


def lanes_at(at, size=LANES):
    return pl.ds(pl.multiple_of(at * size, size), size)


def across(left, right):
    return lax.dot_general(
        left, right, (((0,), (0,)), ((), ())), preferred_element_type=jnp.float32
    )


def along(left, right):
    return lax.dot_general(
        left, right, (((1,), (1,)), ((), ())), preferred_element_type=jnp.float32
    )


def matmul(left, right):
    return jnp.dot(left, right, preferred_element_type=jnp.float32)


def take_lanes(rows, index):
    return lax.gather(
        rows, index[..., None], ALONG_LANES, (1, 1), mode=lax.GatherScatterMode.PROMISE_IN_BOUNDS
    )


def find(load, high, low, chunks, parts):
    bits = [lax.bitwise_and(high, jnp.int16(1 << b)) != jnp.int16(0) for b in range(5)]

    def among(start, size, bit):
        if size == 1:
            return [take_lanes(load(start, v), low) for v in range(parts)]
        first = among(start, size // 2, bit - 1)
        last = among(start + size // 2, size // 2, bit - 1)
        return [jnp.where(bits[bit], q, p) for p, q in zip(first, last)]

    return among(0, chunks, chunks.bit_length() - 2)


def aggregate_kernel(feat_ref, adj_ref, count_ref, owner_ref, out_ref, index, rows, places, stage, wide):
    width, inputs = feat_ref.shape
    nodes = owner_ref.shape[1]
    owners = out_ref.shape[0]
    fan = adj_ref.shape[0] - 1
    chunks = inputs // LANES
    groups = nodes // LANES
    parts = width // 16
    steps = (fan + 1) // 4
    i16, bf16, f32 = jnp.int16, jnp.bfloat16, jnp.float32
    for g in range(groups):
        for s in range(steps):
            index[g * steps + s, 0:4] = adj_ref[s * 4 : s * 4 + 4, g * LANES : (g + 1) * LANES]

    def one_group(g, carry):
        count = count_ref[:, lanes_at(g)]

        def four(s, total):
            total = list(total)
            for j in range(4):
                at = index[g * steps + s, j : j + 1, :]
                high = jnp.broadcast_to(lax.shift_right_logical(at, 7), (16, LANES)).astype(i16)
                low = jnp.broadcast_to(lax.bitwise_and(at, LANES - 1), (16, LANES)).astype(i16)
                valid = jnp.broadcast_to(s * 4 + j < count, (16, LANES))
                found = find(
                    lambda c, v: feat_ref[v * 16 : (v + 1) * 16, c * LANES : (c + 1) * LANES],
                    high, low, chunks, parts,
                )
                if j == 3:
                    for v in range(parts):
                        rows[v * 16 : (v + 1) * 16, lanes_at(g)] = found[v]
                for v in range(parts):
                    total[v] = total[v] + jnp.where(valid, found[v].astype(f32), 0.0)
            return tuple(total)

        zero = jnp.zeros((16, LANES), f32)
        total = lax.fori_loop(0, steps, four, (zero,) * parts)
        divisor = jnp.broadcast_to(count.astype(f32), (16, LANES))
        for v in range(parts):
            near = (total[v] / divisor).astype(bf16)
            rows[width + v * 16 : width + (v + 1) * 16, lanes_at(g)] = near
        return carry

    lax.fori_loop(0, groups, one_group, 0)

    span = 256
    before = (
        lax.broadcasted_iota(jnp.int32, (span, span), 0)
        < lax.broadcasted_iota(jnp.int32, (span, span), 1)
    ).astype(bf16)
    owner_ids = lax.broadcasted_iota(jnp.int32, (owners, span), 0)
    ranks = lax.broadcasted_iota(jnp.int32, (CAP, span), 0)
    seen = jnp.zeros((owners, 1), f32)
    found_at = jnp.zeros((3 * CAP, owners), f32)
    for b in range(nodes // span):
        hit = owner_ids == owner_ref[:, b * span : (b + 1) * span]
        picked = hit.astype(bf16)
        earlier = matmul(picked, before) + seen
        rank = jnp.sum(jnp.where(hit, earlier, 0.0), axis=0, keepdims=True).astype(jnp.int32)
        seen = seen + jnp.sum(jnp.where(hit, 1.0, 0.0), axis=1, keepdims=True)
        node = lax.broadcasted_iota(jnp.int32, (CAP, span), 1) + b * span
        mine = ranks == rank
        weights = jnp.concatenate(
            [
                jnp.where(mine, lax.shift_right_logical(node, 7), 0).astype(f32),
                jnp.where(mine, lax.bitwise_and(node, LANES - 1), 0).astype(f32),
                jnp.where(mine, 1.0, 0.0),
            ],
            axis=0,
        ).astype(bf16)
        found_at = found_at + along(weights, picked)
    found_at = found_at.astype(jnp.int32)
    for q in range(CAP // 4):
        for kind in range(3):
            at = kind * CAP + q * 4
            places[q, kind * 4 : (kind + 1) * 4] = found_at[at : at + 4]

    half = 2 * width

    def four_ranks(q, carry):
        for j in range(4):
            high = jnp.broadcast_to(places[q, j : j + 1, :], (16, owners)).astype(i16)
            low = jnp.broadcast_to(places[q, 4 + j : 5 + j, :], (16, owners)).astype(i16)
            filled = jnp.broadcast_to(places[q, 8 + j : 9 + j, :], (16, owners)) > 0
            found = find(
                lambda c, v: rows[v * 16 : (v + 1) * 16, c * LANES : (c + 1) * LANES],
                high, low, groups, half // 16,
            )
            for v in range(half // 16):
                at = (j % 2) * half + v * 16
                stage[j // 2, at : at + 16, :] = jnp.where(filled, found[v].astype(f32), 0.0)
        for pair in range(2):
            wide[pl.ds(q * 2 + pair, owners, stride=16), :] = stage[pair].T
        return carry

    lax.fori_loop(0, CAP // 4, four_ranks, 0)

    def finish(t, carry):
        at = pl.ds(pl.multiple_of(t * 8, 8), 8)
        out_ref[at] = wide[lanes_at(t), :].astype(bf16).reshape(8, 16, LANES)
        return carry

    lax.fori_loop(0, owners // 8, finish, 0)


def aggregate(features, adjacent, count, owner, owners):
    width, _ = features.shape
    nodes = owner.shape[1]
    return pl.pallas_call(
        aggregate_kernel,
        out_shape=jax.ShapeDtypeStruct((owners, 16, LANES), jnp.bfloat16),
        in_specs=[VMEM] * 4,
        out_specs=VMEM,
        scratch_shapes=[
            pltpu.VMEM((nodes // LANES * 4, 4, LANES), jnp.int32),
            pltpu.VMEM((2 * width, nodes), jnp.bfloat16),
            pltpu.VMEM((CAP // 4, 12, LANES), jnp.int32),
            pltpu.VMEM((2, 4 * width, owners), jnp.float32),
            pltpu.VMEM((16 * owners, LANES), jnp.float32),
        ],
        name="aggregate",
        compiler_params=pltpu.CompilerParams(vmem_limit_bytes=12 << 20),
        cost_estimate=pl.CostEstimate(flops=40_000_000, bytes_accessed=3_000_000, transcendentals=0),
    )(features, adjacent, count, owner)


def picks_kernel(adj_ref, center_ref, count_ref, out_ref, flip_ref):
    nodes, fan = adj_ref.shape
    slots = out_ref.shape[1]

    def table_row(slot):
        odd = lax.shift_left(lax.bitwise_and(slot, 1), 4)
        pair = lax.bitwise_and(lax.shift_right_logical(slot, 1), 15)
        return lax.bitwise_and(slot, -CAP) + odd + pair

    def one_tile(t, carry):
        at = pl.ds(pl.multiple_of(t * 16, 16), 16)
        number = lax.broadcasted_iota(jnp.int32, (16, fan), 1)
        adjacent = jnp.where(number < count_ref[at, :], table_row(adj_ref[at, :]), -1)
        center = jnp.broadcast_to(table_row(center_ref[at, :]), (16, LANES))
        spread = [jnp.broadcast_to(adjacent[:, k : k + 1], (16, LANES)) for k in range(fan)]
        for c in range(slots // LANES):
            ids = lax.broadcasted_iota(jnp.int32, (16, LANES), 1) + c * LANES
            total = jnp.zeros((16, LANES), jnp.float32)
            for k in range(fan):
                total = total + jnp.where(spread[k] == ids, 1.0, 0.0)
            out_ref[at, c * LANES : (c + 1) * LANES] = jnp.where(center == ids, 1.0, 0.0).astype(
                out_ref.dtype
            )
            low = pl.ds(pl.multiple_of(nodes + t * 16, 16), 16)
            out_ref[low, c * LANES : (c + 1) * LANES] = total.astype(out_ref.dtype)
        return carry

    lax.fori_loop(0, nodes // 16, one_tile, 0)

    def one_flip(t, carry):
        flip_ref[:, lanes_at(t)] = out_ref[lanes_at(t), :].T
        return carry

    lax.fori_loop(0, 2 * nodes // LANES, one_flip, 0)


def picks(adjacent, center, count, slots):
    nodes = adjacent.shape[0]
    return pl.pallas_call(
        picks_kernel,
        out_shape=(
            jax.ShapeDtypeStruct((2 * nodes, slots), jnp.bfloat16),
            jax.ShapeDtypeStruct((slots, 2 * nodes), jnp.bfloat16),
        ),
        in_specs=[VMEM] * 3,
        out_specs=(VMEM, VMEM),
        name="picks",
        compiler_params=pltpu.CompilerParams(vmem_limit_bytes=12 << 20),
        cost_estimate=pl.CostEstimate(flops=20_000_000, bytes_accessed=5_000_000, transcendentals=0),
    )(adjacent, center, count)


def call(kernel, outs, ins, smem=0, scratch=(), limit=16, flops=0, moved=0, exps=0):
    return pl.pallas_call(
        kernel,
        out_shape=outs,
        in_specs=[SMEM] * smem + [VMEM] * (ins - smem),
        out_specs=(VMEM,) * len(outs),
        scratch_shapes=scratch,
        compiler_params=pltpu.CompilerParams(vmem_limit_bytes=limit << 20),
        cost_estimate=pl.CostEstimate(flops=flops, bytes_accessed=moved, transcendentals=exps),
    )


def put_chunks(to_ref, t, product):
    for c in range(product.shape[0] // 16):
        for lane in range(product.shape[1] // LANES):
            to_ref[t * (product.shape[0] // 16) + c, lane * 16 : (lane + 1) * 16, :] = product[
                c * 16 : (c + 1) * 16, lane * LANES : (lane + 1) * LANES
            ]


def forward_kernel(
    core_ref, arrived_ref, first_ref, bias_one_ref, picks_ref, count_ref, root_ref, near_ref,
    bias_two_ref, upstream_ref, out_ref, sent_ref, hidden, rows, slope, inputs_flip, bias_grad,
    inputs,
):
    slots, depth = inputs.shape
    hidden_width = hidden.shape[1]
    nodes = slope.shape[0]
    quarter = depth // 4
    sources = slots // CAP
    tile = 256

    def one_source(t, carry):
        for e in range(2):
            pieces = [
                arrived_ref[f * sources + t, :, e * quarter : (e + 1) * quarter] for f in range(4)
            ]
            at = pl.ds(pl.multiple_of(t * CAP + e * 16, 16), 16)
            inputs[at, :] = jnp.concatenate(pieces, axis=1)
        return carry

    lax.fori_loop(0, sources, one_source, 0)
    for t in range(slots // tile):
        inputs_flip[:, t * tile : (t + 1) * tile] = inputs[t * tile : (t + 1) * tile, :].T

    def first_layer(t, carry):
        cols = lanes_at(t, tile)
        pre = matmul(inputs[...], first_ref[:, cols]) + bias_one_ref[:, cols]
        value = jnp.maximum(pre, 0.0) + jnp.log1p(jnp.exp(-jnp.abs(pre)))
        hidden[:, cols] = value.astype(jnp.bfloat16)
        return carry

    lax.fori_loop(0, hidden_width // tile, first_layer, 0)
    inverse = 1.0 / count_ref[...].astype(jnp.float32)

    def select(t, carry):
        cols = lanes_at(t, tile)
        rows[:nodes, cols] = matmul(picks_ref[:nodes, :], hidden[:, cols]).astype(jnp.bfloat16)
        total = matmul(picks_ref[nodes:, :], hidden[:, cols])
        rows[nodes:, cols] = (total * inverse).astype(jnp.bfloat16)
        return carry

    lax.fori_loop(0, hidden_width // tile, select, 0)

    def second_layer(t, carry):
        cols = lanes_at(t, tile)
        pre = matmul(rows[:nodes, :], root_ref[:, cols]) + matmul(rows[nodes:, :], near_ref[:, cols])
        pre = pre + bias_two_ref[:, cols]
        gate = jax.nn.sigmoid(pre)
        out_ref[:, cols] = (pre * gate).astype(jnp.bfloat16)
        grad = upstream_ref[:, cols].astype(jnp.float32) * gate * (1.0 + pre * (1.0 - gate))
        grad = grad.astype(jnp.bfloat16)
        slope[:, cols] = grad
        bias_grad[0:1, cols] = jnp.sum(grad.astype(jnp.float32), axis=0, keepdims=True)
        return carry

    lax.fori_loop(0, hidden_width // tile, second_layer, 0)
    start = (core_ref[0] ^ 1) * nodes

    def weight_grads(t, carry):
        left = rows[pl.ds(pl.multiple_of(start, nodes), nodes), lanes_at(t, tile)]
        put_chunks(sent_ref, t, across(left, slope[...]).astype(jnp.bfloat16))
        return carry

    lax.fori_loop(0, hidden_width // tile, weight_grads, 0)


def kept_kernel(
    core_ref, rows_ref, slope_ref, received_ref, kept_one_ref, received_one_ref, both_ref
):
    nodes, hidden_width = slope_ref.shape
    tile = 256
    start = core_ref[0] * nodes

    def weight_grads(t, carry):
        left = rows_ref[pl.ds(pl.multiple_of(start, nodes), nodes), lanes_at(t, tile)]
        product = across(left, slope_ref[...])
        for c in range(tile // 16):
            chunk = t * (tile // 16) + c
            for lane in range(hidden_width // LANES):
                at = slice(lane * 16, (lane + 1) * 16)
                mine = product[c * 16 : (c + 1) * 16, lane * LANES : (lane + 1) * LANES]
                other = received_ref[chunk, at, :].astype(jnp.float32)
                both_ref[chunk, at, :] = (mine + other).astype(jnp.bfloat16)
            mine = kept_one_ref[chunk].astype(jnp.float32)
            other = received_one_ref[chunk].astype(jnp.float32)
            both_ref[chunk, LANES:, :] = (mine + other).astype(jnp.bfloat16)
        return carry

    lax.fori_loop(0, hidden_width // tile, weight_grads, 0)


def backward_kernel(
    core_ref, slope_ref, root_ref, near_ref, count_ref, flip_ref, hidden_ref, inputs_flip_ref,
    bias_two_ref, kept_ref, sent_ref, back, bias_grads,
):
    core = core_ref[0]
    nodes, hidden_width = slope_ref.shape
    tile = 256
    bias_grads[0:1, :] = bias_two_ref[0:1, :]
    inverse = 1.0 / count_ref[...].astype(jnp.float32)

    def backward(t, carry):
        cols = lanes_at(t, tile)
        back[:nodes, cols] = along(slope_ref[...], root_ref[cols, :]).astype(jnp.bfloat16)
        near = along(slope_ref[...], near_ref[cols, :])
        back[nodes:, cols] = (near * inverse).astype(jnp.bfloat16)
        return carry

    lax.fori_loop(0, hidden_width // tile, backward, 0)

    def first_grads(t, carry):
        cols = lanes_at(t, tile)
        table_grad = matmul(flip_ref[...], back[:, cols])
        grad = table_grad * (1.0 - jnp.exp(-hidden_ref[:, cols].astype(jnp.float32)))
        grad = grad.astype(jnp.bfloat16)
        bias_grads[1:2, cols] = jnp.sum(grad.astype(jnp.float32), axis=0, keepdims=True)
        for place, to_ref in enumerate((kept_ref, sent_ref)):
            which = core ^ place
            left = inputs_flip_ref[pl.ds(pl.multiple_of(which * LANES, LANES), LANES), :]
            product = matmul(left, grad).astype(jnp.bfloat16)
            for c in range(8):
                for lane in range(tile // LANES):
                    chunk = c * 8 + t * (tile // LANES) + lane
                    to_ref[chunk, 0:16, :] = product[
                        c * 16 : (c + 1) * 16, lane * LANES : (lane + 1) * LANES
                    ]
        return carry

    lax.fori_loop(0, hidden_width // tile, first_grads, 0)
    for place, to_ref in enumerate((kept_ref, sent_ref)):
        which = core ^ place
        to_ref[:, 16:, :] = jnp.zeros((to_ref.shape[0], 8, LANES), jnp.bfloat16)
        for lane in range(8):
            cols = slice(lane * LANES, (lane + 1) * LANES)
            row = jnp.where(which == 0, bias_grads[0:1, cols], bias_grads[1:2, cols])
            to_ref[lane, 16:, :] = jnp.broadcast_to(row, (8, LANES)).astype(jnp.bfloat16)


def shaped(*shape, dtype=jnp.bfloat16):
    return jax.ShapeDtypeStruct(shape, dtype)


def spread_kernel(core_ref, z_ref, kept_ref, other_ref, root_ref, near_ref, first_root_ref, first_near_ref, bias_two_ref, bias_one_ref):
    core, z = core_ref[0], z_ref[0]
    step = pl.program_id(0)
    even = core == 0
    for c in range(8):
        for lane in range(8):
            kept = kept_ref[c, lane * 16 : (lane + 1) * 16, :].astype(jnp.float32)
            other = other_ref[c, lane * 16 : (lane + 1) * 16, :].astype(jnp.float32)
            at, cols = slice(c * 16, (c + 1) * 16), slice(lane * LANES, (lane + 1) * LANES)
            root_ref[at, cols] = jnp.where(even, kept, other)
            near_ref[at, cols] = jnp.where(even, other, kept)

    here = lax.shift_right_logical(z, 1) == core
    base = lax.bitwise_and(z, 1) * 4
    for j, to_ref in enumerate((first_root_ref, first_near_ref)):
        for i in range(2):

            @pl.when(step == base + 2 * j + i)
            def _(to_ref=to_ref, i=i):
                for lane in range(8):
                    kept = kept_ref[lane, LANES : LANES + 16, :].astype(jnp.float32)
                    other = other_ref[lane, LANES : LANES + 16, :].astype(jnp.float32)
                    at, cols = slice(i * 16, (i + 1) * 16), slice(lane * LANES, (lane + 1) * LANES)
                    to_ref[at, cols] = jnp.where(here, kept, other)

    @pl.when(step == 0)
    def _():
        for lane in range(8):
            kept = kept_ref[lane, LANES + 16 :, :].astype(jnp.float32)[0:1, :]
            other = other_ref[lane, LANES + 16 :, :].astype(jnp.float32)[0:1, :]
            cols = slice(lane * LANES, (lane + 1) * LANES)
            bias_two_ref[:, cols] = jnp.where(even, kept, other)
            bias_one_ref[:, cols] = jnp.where(even, other, kept)


def spread(core, z, kept, other, hidden_width):
    f32 = jnp.float32
    wide = pl.BlockSpec((LANES, hidden_width), lambda s: (s, 0))
    slab = pl.BlockSpec((32, hidden_width), lambda s: (0, 0))
    line = pl.BlockSpec((1, hidden_width), lambda s: (0, 0))
    block = pl.BlockSpec((8, CHUNK, LANES), lambda s: (s, 0, 0))
    return pl.pallas_call(
        spread_kernel,
        grid=(8,),
        out_shape=(
            shaped(hidden_width, hidden_width, dtype=f32),
            shaped(hidden_width, hidden_width, dtype=f32),
            shaped(32, hidden_width, dtype=f32),
            shaped(32, hidden_width, dtype=f32),
            shaped(1, hidden_width, dtype=f32),
            shaped(1, hidden_width, dtype=f32),
        ),
        in_specs=[SMEM, SMEM, block, block],
        out_specs=(wide, wide, slab, slab, line, line),
        name="spread",
        compiler_params=pltpu.CompilerParams(vmem_limit_bytes=16 << 20),
    )(core, z, kept, other)


def weights_of_pair(own, z):
    first = lax.ppermute(own, "z", [(0, 1), (1, 0), (2, 3), (3, 2)])
    odd = lax.bitwise_and(z, 1) == 1
    return jnp.concatenate([jnp.where(odd, first, own), jnp.where(odd, own, first)], axis=0)


def weights_of_all(pair, z):
    second = lax.ppermute(pair, "z", [(0, 3), (3, 0), (1, 2), (2, 1)])
    late = z >= 2
    return jnp.concatenate([jnp.where(late, second, pair), jnp.where(late, pair, second)], axis=0)


def exchange(value, axes):
    return lax.all_to_all(value, axes, split_axis=0, concat_axis=0, tiled=True)


def step(
    features,
    first_adjacent,
    first_center,
    first_count,
    owner_map,
    first_root,
    first_near,
    first_bias,
    second_adjacent,
    second_center,
    second_count,
    second_root,
    second_near,
    second_bias,
    upstream,
):
    owners = 128
    hidden_width = first_root.shape[1]
    z = lax.axis_index("z")
    core = lax.axis_index("core")[None]
    pair = weights_of_pair(jnp.concatenate([first_root, first_near], axis=0), z)
    columns = jnp.concatenate([first_adjacent, first_center[:, None]], axis=1).T
    packed = aggregate(features, columns, first_count[None], owner_map[None], owners)
    packed, pair = lax.optimization_barrier((packed, pair))
    first_all = weights_of_all(pair, z)
    arrived = exchange(packed, AXES)
    count = second_count[:, None]
    picked, flipped = picks(second_adjacent, second_center[:, None], count, owners * 8)
    slots, depth = picked.shape[1], first_all.shape[0]
    nodes = upstream.shape[0]
    layer_output, sent_two, hidden, rows, slope, inputs_flip, bias_grad = call(
        forward_kernel,
        (
            shaped(nodes, hidden_width),
            shaped(64, LANES, LANES),
            shaped(slots, hidden_width),
            shaped(2 * nodes, hidden_width),
            shaped(nodes, hidden_width),
            shaped(depth, slots),
            shaped(8, hidden_width, dtype=jnp.float32),
        ),
        10,
        smem=1,
        scratch=[pltpu.VMEM((slots, depth), jnp.bfloat16)],
        limit=28,
        flops=6_000_000_000,
        moved=18_000_000,
        exps=3_000_000,
    )(
        core, arrived, first_all, first_bias[None], picked, count, second_root, second_near,
        second_bias[None], upstream,
    )
    received = lax.ppermute(sent_two, "core", [(0, 1), (1, 0)])
    kept_one, sent_one = call(
        backward_kernel, (shaped(64, 24, LANES), shaped(64, 24, LANES)), 9, smem=1,
        scratch=[
            pltpu.VMEM((2 * nodes, hidden_width), jnp.bfloat16),
            pltpu.VMEM((8, hidden_width), jnp.float32),
        ],
        limit=24, flops=4_700_000_000, moved=12_000_000, exps=1_000_000,
    )(core, slope, second_root, second_near, count, flipped, hidden, inputs_flip, bias_grad)
    received_one = lax.ppermute(sent_one, "core", [(0, 1), (1, 0)])
    (both,) = call(
        kept_kernel, (shaped(64, CHUNK, LANES),), 6, smem=1, limit=20,
        flops=1_000_000_000, moved=7_000_000,
    )(core, rows, slope, received, kept_one, received_one)
    terms = exchange(both, CHIPS)
    total = jnp.sum(terms.astype(jnp.float32), axis=0).astype(jnp.bfloat16)
    mine = exchange(jnp.broadcast_to(total[None], terms.shape), CHIPS)
    other = lax.ppermute(mine, "core", [(0, 1), (1, 0)])
    root_two, near_two, root_one, near_one, bias_two, bias_one = spread(
        core, z[None], mine, other, hidden_width
    )
    return (layer_output, root_two, near_two, bias_two[0], root_one, near_one, bias_one[0])


def solution(mesh):
    chips = Mesh(mesh.devices.reshape(4, 4, 4, 2), AXES)
    trainer = ("x", "y", "core")
    return jax.shard_map(
        step,
        mesh=chips,
        in_specs=(
            P("z", trainer),
            P(trainer, None),
            P(trainer),
            P(trainer),
            P(trainer),
            P("z", None),
            P("z", None),
            P(),
            P(AXES, None),
            P(AXES),
            P(AXES),
            P(),
            P(),
            P(),
            P(AXES, None),
        ),
        out_specs=(
            P(AXES, None),
            P(),
            P(),
            P(),
            P("z", None),
            P("z", None),
            P(),
        ),
        check_vma=False,
    )
```

```python
import jax
import jax.numpy as jnp
from jax import lax
from jax.experimental import pallas as pl
from jax.experimental.pallas import tpu as pltpu
from jax.sharding import Mesh, PartitionSpec as P


CAP = 32
LANES = 128
AXES = ("z", "x", "y", "core")
CHIPS = ("z", "x", "y")
VMEM = pl.BlockSpec(memory_space=pltpu.VMEM)
ALONG_LANES = lax.GatherDimensionNumbers(
    offset_dims=(),
    collapsed_slice_dims=(1,),
    start_index_map=(1,),
    operand_batching_dims=(0,),
    start_indices_batching_dims=(0,),
)
SMEM = pl.BlockSpec(memory_space=pltpu.SMEM)


def lanes_at(at, size=LANES):
    return pl.ds(pl.multiple_of(at * size, size), size)


def across(left, right):
    return lax.dot_general(
        left, right, (((0,), (0,)), ((), ())), preferred_element_type=jnp.float32
    )


def along(left, right):
    return lax.dot_general(
        left, right, (((1,), (1,)), ((), ())), preferred_element_type=jnp.float32
    )


def matmul(left, right):
    return jnp.dot(left, right, preferred_element_type=jnp.float32)


def take_lanes(rows, index):
    return lax.gather(
        rows, index[..., None], ALONG_LANES, (1, 1), mode=lax.GatherScatterMode.PROMISE_IN_BOUNDS
    )


def find(load, high, low, chunks, parts):
    bits = [lax.bitwise_and(high, jnp.int16(1 << b)) != jnp.int16(0) for b in range(5)]

    def among(start, size, bit):
        if size == 1:
            return [take_lanes(load(start, v), low) for v in range(parts)]
        first = among(start, size // 2, bit - 1)
        last = among(start + size // 2, size // 2, bit - 1)
        return [jnp.where(bits[bit], q, p) for p, q in zip(first, last)]

    return among(0, chunks, chunks.bit_length() - 2)


def aggregate_kernel(feat_ref, adj_ref, count_ref, owner_ref, out_ref, index, rows, places, stage, wide):
    width, inputs = feat_ref.shape
    nodes = owner_ref.shape[1]
    owners = out_ref.shape[0]
    fan = adj_ref.shape[0] - 1
    chunks = inputs // LANES
    groups = nodes // LANES
    parts = width // 16
    steps = (fan + 1) // 4
    i16, bf16, f32 = jnp.int16, jnp.bfloat16, jnp.float32
    for g in range(groups):
        for s in range(steps):
            index[g * steps + s, 0:4] = adj_ref[s * 4 : s * 4 + 4, g * LANES : (g + 1) * LANES]

    def one_group(g, carry):
        count = count_ref[:, lanes_at(g)]

        def four(s, total):
            total = list(total)
            for j in range(4):
                at = index[g * steps + s, j : j + 1, :]
                high = jnp.broadcast_to(lax.shift_right_logical(at, 7), (16, LANES)).astype(i16)
                low = jnp.broadcast_to(lax.bitwise_and(at, LANES - 1), (16, LANES)).astype(i16)
                valid = jnp.broadcast_to(s * 4 + j < count, (16, LANES))
                found = find(
                    lambda c, v: feat_ref[v * 16 : (v + 1) * 16, c * LANES : (c + 1) * LANES],
                    high, low, chunks, parts,
                )
                if j == 3:
                    for v in range(parts):
                        rows[v * 16 : (v + 1) * 16, lanes_at(g)] = found[v]
                for v in range(parts):
                    total[v] = total[v] + jnp.where(valid, found[v].astype(f32), 0.0)
            return tuple(total)

        zero = jnp.zeros((16, LANES), f32)
        total = lax.fori_loop(0, steps, four, (zero,) * parts)
        divisor = jnp.broadcast_to(count.astype(f32), (16, LANES))
        for v in range(parts):
            near = (total[v] / divisor).astype(bf16)
            rows[width + v * 16 : width + (v + 1) * 16, lanes_at(g)] = near
        return carry

    lax.fori_loop(0, groups, one_group, 0)

    span = 256
    before = (
        lax.broadcasted_iota(jnp.int32, (span, span), 0)
        < lax.broadcasted_iota(jnp.int32, (span, span), 1)
    ).astype(bf16)
    owner_ids = lax.broadcasted_iota(jnp.int32, (owners, span), 0)
    ranks = lax.broadcasted_iota(jnp.int32, (CAP, span), 0)
    seen = jnp.zeros((owners, 1), f32)
    found_at = jnp.zeros((3 * CAP, owners), f32)
    for b in range(nodes // span):
        hit = owner_ids == owner_ref[:, b * span : (b + 1) * span]
        picked = hit.astype(bf16)
        earlier = matmul(picked, before) + seen
        rank = jnp.sum(jnp.where(hit, earlier, 0.0), axis=0, keepdims=True).astype(jnp.int32)
        seen = seen + jnp.sum(jnp.where(hit, 1.0, 0.0), axis=1, keepdims=True)
        node = lax.broadcasted_iota(jnp.int32, (CAP, span), 1) + b * span
        mine = ranks == rank
        weights = jnp.concatenate(
            [
                jnp.where(mine, lax.shift_right_logical(node, 7), 0).astype(f32),
                jnp.where(mine, lax.bitwise_and(node, LANES - 1), 0).astype(f32),
                jnp.where(mine, 1.0, 0.0),
            ],
            axis=0,
        ).astype(bf16)
        found_at = found_at + along(weights, picked)
    found_at = found_at.astype(jnp.int32)
    for q in range(CAP // 4):
        for kind in range(3):
            at = kind * CAP + q * 4
            places[q, kind * 4 : (kind + 1) * 4] = found_at[at : at + 4]

    half = 2 * width

    def four_ranks(q, carry):
        for j in range(4):
            high = jnp.broadcast_to(places[q, j : j + 1, :], (16, owners)).astype(i16)
            low = jnp.broadcast_to(places[q, 4 + j : 5 + j, :], (16, owners)).astype(i16)
            filled = jnp.broadcast_to(places[q, 8 + j : 9 + j, :], (16, owners)) > 0
            found = find(
                lambda c, v: rows[v * 16 : (v + 1) * 16, c * LANES : (c + 1) * LANES],
                high, low, groups, half // 16,
            )
            for v in range(half // 16):
                at = (j % 2) * half + v * 16
                stage[j // 2, at : at + 16, :] = jnp.where(filled, found[v].astype(f32), 0.0)
        for pair in range(2):
            wide[pl.ds(q * 2 + pair, owners, stride=16), :] = stage[pair].T
        return carry

    lax.fori_loop(0, CAP // 4, four_ranks, 0)

    def finish(t, carry):
        at = pl.ds(pl.multiple_of(t * 8, 8), 8)
        out_ref[at] = wide[lanes_at(t), :].astype(bf16).reshape(8, 16, LANES)
        return carry

    lax.fori_loop(0, owners // 8, finish, 0)


def aggregate(features, adjacent, count, owner, owners):
    width, _ = features.shape
    nodes = owner.shape[1]
    return pl.pallas_call(
        aggregate_kernel,
        out_shape=jax.ShapeDtypeStruct((owners, 16, LANES), jnp.bfloat16),
        in_specs=[VMEM] * 4,
        out_specs=VMEM,
        scratch_shapes=[
            pltpu.VMEM((nodes // LANES * 4, 4, LANES), jnp.int32),
            pltpu.VMEM((2 * width, nodes), jnp.bfloat16),
            pltpu.VMEM((CAP // 4, 12, LANES), jnp.int32),
            pltpu.VMEM((2, 4 * width, owners), jnp.float32),
            pltpu.VMEM((16 * owners, LANES), jnp.float32),
        ],
        name="aggregate",
        compiler_params=pltpu.CompilerParams(vmem_limit_bytes=12 << 20),
        cost_estimate=pl.CostEstimate(flops=40_000_000, bytes_accessed=3_000_000, transcendentals=0),
    )(features, adjacent, count, owner)


def picks_kernel(adj_ref, center_ref, count_ref, out_ref, flip_ref):
    nodes, fan = adj_ref.shape
    slots = out_ref.shape[1]

    def table_row(slot):
        odd = lax.shift_left(lax.bitwise_and(slot, 1), 4)
        pair = lax.bitwise_and(lax.shift_right_logical(slot, 1), 15)
        return lax.bitwise_and(slot, -CAP) + odd + pair

    def one_tile(t, carry):
        at = pl.ds(pl.multiple_of(t * 16, 16), 16)
        number = lax.broadcasted_iota(jnp.int32, (16, fan), 1)
        adjacent = jnp.where(number < count_ref[at, :], table_row(adj_ref[at, :]), -1)
        center = jnp.broadcast_to(table_row(center_ref[at, :]), (16, LANES))
        spread = [jnp.broadcast_to(adjacent[:, k : k + 1], (16, LANES)) for k in range(fan)]
        for c in range(slots // LANES):
            ids = lax.broadcasted_iota(jnp.int32, (16, LANES), 1) + c * LANES
            total = jnp.zeros((16, LANES), jnp.float32)
            for k in range(fan):
                total = total + jnp.where(spread[k] == ids, 1.0, 0.0)
            out_ref[at, c * LANES : (c + 1) * LANES] = jnp.where(center == ids, 1.0, 0.0).astype(
                out_ref.dtype
            )
            low = pl.ds(pl.multiple_of(nodes + t * 16, 16), 16)
            out_ref[low, c * LANES : (c + 1) * LANES] = total.astype(out_ref.dtype)
        return carry

    lax.fori_loop(0, nodes // 16, one_tile, 0)

    def one_flip(t, carry):
        flip_ref[:, lanes_at(t)] = out_ref[lanes_at(t), :].T
        return carry

    lax.fori_loop(0, 2 * nodes // LANES, one_flip, 0)


def picks(adjacent, center, count, slots):
    nodes = adjacent.shape[0]
    return pl.pallas_call(
        picks_kernel,
        out_shape=(
            jax.ShapeDtypeStruct((2 * nodes, slots), jnp.bfloat16),
            jax.ShapeDtypeStruct((slots, 2 * nodes), jnp.bfloat16),
        ),
        in_specs=[VMEM] * 3,
        out_specs=(VMEM, VMEM),
        name="picks",
        compiler_params=pltpu.CompilerParams(vmem_limit_bytes=12 << 20),
        cost_estimate=pl.CostEstimate(flops=20_000_000, bytes_accessed=5_000_000, transcendentals=0),
    )(adjacent, center, count)


def call(kernel, outs, ins, smem=0, scratch=(), limit=16, flops=0, moved=0, exps=0):
    return pl.pallas_call(
        kernel,
        out_shape=outs,
        in_specs=[SMEM] * smem + [VMEM] * (ins - smem),
        out_specs=(VMEM,) * len(outs),
        scratch_shapes=scratch,
        compiler_params=pltpu.CompilerParams(vmem_limit_bytes=limit << 20),
        cost_estimate=pl.CostEstimate(flops=flops, bytes_accessed=moved, transcendentals=exps),
    )


def put_chunks(to_ref, t, product):
    for c in range(product.shape[0] // 16):
        for lane in range(product.shape[1] // LANES):
            to_ref[t * (product.shape[0] // 16) + c, lane * 16 : (lane + 1) * 16, :] = product[
                c * 16 : (c + 1) * 16, lane * LANES : (lane + 1) * LANES
            ]


def forward_kernel(
    core_ref, z_ref, arrived_ref, pair_ref, other_pair_ref, bias_one_ref, picks_ref, count_ref, root_ref, near_ref,
    bias_two_ref, upstream_ref, out_ref, sent_ref, hidden, rows, slope, inputs_flip, bias_grad,
    inputs,
):
    slots, depth = inputs.shape
    hidden_width = hidden.shape[1]
    nodes = slope.shape[0]
    quarter = depth // 4
    sources = slots // CAP
    tile = 256

    def one_source(t, carry):
        for e in range(2):
            pieces = [
                arrived_ref[f * sources + t, :, e * quarter : (e + 1) * quarter] for f in range(4)
            ]
            at = pl.ds(pl.multiple_of(t * CAP + e * 16, 16), 16)
            inputs[at, :] = jnp.concatenate(pieces, axis=1)
        return carry

    lax.fori_loop(0, sources, one_source, 0)
    for t in range(slots // tile):
        inputs_flip[:, t * tile : (t + 1) * tile] = inputs[t * tile : (t + 1) * tile, :].T

    late = z_ref[0] >= 2

    def first_layer(t, carry):
        cols = lanes_at(t, tile)
        pair, other = pair_ref[:, cols], other_pair_ref[:, cols]
        pre = matmul(inputs[:, : depth // 2], jnp.where(late, other, pair))
        pre = pre + matmul(inputs[:, depth // 2 :], jnp.where(late, pair, other))
        pre = pre + bias_one_ref[:, cols]
        value = jnp.maximum(pre, 0.0) + jnp.log1p(jnp.exp(-jnp.abs(pre)))
        hidden[:, cols] = value.astype(jnp.bfloat16)
        return carry

    lax.fori_loop(0, hidden_width // tile, first_layer, 0)
    inverse = 1.0 / count_ref[...].astype(jnp.float32)

    def select(t, carry):
        cols = lanes_at(t, tile)
        rows[:nodes, cols] = matmul(picks_ref[:nodes, :], hidden[:, cols]).astype(jnp.bfloat16)
        total = matmul(picks_ref[nodes:, :], hidden[:, cols])
        rows[nodes:, cols] = (total * inverse).astype(jnp.bfloat16)
        return carry

    lax.fori_loop(0, hidden_width // tile, select, 0)

    def second_layer(t, carry):
        cols = lanes_at(t, tile)
        pre = matmul(rows[:nodes, :], root_ref[:, cols]) + matmul(rows[nodes:, :], near_ref[:, cols])
        pre = pre + bias_two_ref[:, cols]
        gate = jax.nn.sigmoid(pre)
        out_ref[:, cols] = (pre * gate).astype(jnp.bfloat16)
        grad = upstream_ref[:, cols].astype(jnp.float32) * gate * (1.0 + pre * (1.0 - gate))
        grad = grad.astype(jnp.bfloat16)
        slope[:, cols] = grad
        bias_grad[0:1, cols] = jnp.sum(grad.astype(jnp.float32), axis=0, keepdims=True)
        return carry

    lax.fori_loop(0, hidden_width // tile, second_layer, 0)
    start = (core_ref[0] ^ 1) * nodes

    def weight_grads(t, carry):
        left = rows[pl.ds(pl.multiple_of(start, nodes), nodes), lanes_at(t, tile)]
        put_chunks(sent_ref, t, across(left, slope[...]).astype(jnp.bfloat16))
        return carry

    lax.fori_loop(0, hidden_width // tile, weight_grads, 0)


def kept_kernel(core_ref, rows_ref, slope_ref, received_ref, both_ref):
    nodes, hidden_width = slope_ref.shape
    tile = 256
    start = core_ref[0] * nodes

    def weight_grads(t, carry):
        left = rows_ref[pl.ds(pl.multiple_of(start, nodes), nodes), lanes_at(t, tile)]
        product = across(left, slope_ref[...])
        for c in range(tile // 16):
            chunk = t * (tile // 16) + c
            for lane in range(hidden_width // LANES):
                at = slice(lane * 16, (lane + 1) * 16)
                mine = product[c * 16 : (c + 1) * 16, lane * LANES : (lane + 1) * LANES]
                other = received_ref[chunk, at, :].astype(jnp.float32)
                both_ref[chunk, at, :] = (mine + other).astype(jnp.bfloat16)
        return carry

    lax.fori_loop(0, hidden_width // tile, weight_grads, 0)


def backward_kernel(slope_ref, root_ref, near_ref, count_ref, back_ref):
    nodes, hidden_width = slope_ref.shape
    tile = 256
    inverse = 1.0 / count_ref[...].astype(jnp.float32)

    def backward(t, carry):
        cols = lanes_at(t, tile)
        back_ref[:nodes, cols] = along(slope_ref[...], root_ref[cols, :]).astype(jnp.bfloat16)
        near = along(slope_ref[...], near_ref[cols, :])
        back_ref[nodes:, cols] = (near * inverse).astype(jnp.bfloat16)
        return carry

    lax.fori_loop(0, hidden_width // tile, backward, 0)


def first_grads_kernel(
    core_ref, z_ref, flip_ref, back_ref, hidden_ref, inputs_flip_ref, bias_two_ref, kept_ref,
    sent_ref, grads, bias_grads,
):
    core, z = core_ref[0], z_ref[0]
    hidden_width = hidden_ref.shape[1]
    depth = inputs_flip_ref.shape[0]
    tile = 256
    bias_grads[0:1, :] = bias_two_ref[0:1, :]

    def first_grads(t, carry):
        cols = lanes_at(t, tile)
        table_grad = matmul(flip_ref[...], back_ref[:, cols])
        grad = table_grad * (1.0 - jnp.exp(-hidden_ref[:, cols].astype(jnp.float32)))
        grad = grad.astype(jnp.bfloat16)
        bias_grads[1:2, cols] = jnp.sum(grad.astype(jnp.float32), axis=0, keepdims=True)
        product = matmul(inputs_flip_ref[...], grad).astype(jnp.bfloat16)
        for part in range(depth // 32):
            grads[part, :, cols] = product[part * 32 : (part + 1) * 32, :]
        return carry

    lax.fori_loop(0, hidden_width // tile, first_grads, 0)
    for place, to_ref in enumerate((kept_ref, sent_ref)):
        which = core ^ place
        row = jnp.where(which == 0, bias_grads[0:1, :], bias_grads[1:2, :])
        row = jnp.broadcast_to(row, (16, hidden_width)).astype(jnp.bfloat16)
        for position, flip in enumerate((0, 3, 1, 2)):
            to_ref[position, 0:32, :] = grads[(z ^ flip) * 2 + which]
            to_ref[position, 32:48, :] = row


def shaped(*shape, dtype=jnp.bfloat16):
    return jax.ShapeDtypeStruct(shape, dtype)


def spread_kernel(core_ref, kept_ref, other_ref, root_ref, near_ref):
    even = core_ref[0] == 0
    for c in range(8):
        for lane in range(8):
            kept = kept_ref[c, lane * 16 : (lane + 1) * 16, :].astype(jnp.float32)
            other = other_ref[c, lane * 16 : (lane + 1) * 16, :].astype(jnp.float32)
            at, cols = slice(c * 16, (c + 1) * 16), slice(lane * LANES, (lane + 1) * LANES)
            root_ref[at, cols] = jnp.where(even, kept, other)
            near_ref[at, cols] = jnp.where(even, other, kept)


def spread(core, kept, other, hidden_width):
    square = shaped(hidden_width, hidden_width, dtype=jnp.float32)
    wide = pl.BlockSpec((LANES, hidden_width), lambda s: (s, 0))
    block = pl.BlockSpec((8, LANES, LANES), lambda s: (s, 0, 0))
    return pl.pallas_call(
        spread_kernel,
        grid=(8,),
        out_shape=(square, square),
        in_specs=[SMEM, block, block],
        out_specs=(wide, wide),
        name="spread",
        compiler_params=pltpu.CompilerParams(vmem_limit_bytes=8 << 20),
    )(core, kept, other)


PAIRS = {1: [(0, 1), (1, 0), (2, 3), (3, 2)], 3: [(0, 3), (3, 0), (1, 2), (2, 1)]}


def plus(mine, other):
    return (mine.astype(jnp.float32) + other.astype(jnp.float32)).astype(jnp.bfloat16)


def weights_of_pair(own, z):
    first = lax.ppermute(own, "z", [(0, 1), (1, 0), (2, 3), (3, 2)])
    odd = lax.bitwise_and(z, 1) == 1
    return jnp.concatenate([jnp.where(odd, first, own), jnp.where(odd, own, first)], axis=0)


def weights_of_others(pair):
    return lax.ppermute(pair, "z", [(0, 3), (3, 0), (1, 2), (2, 1)])


def exchange(value, axes):
    return lax.all_to_all(value, axes, split_axis=0, concat_axis=0, tiled=True)


def step(
    features,
    first_adjacent,
    first_center,
    first_count,
    owner_map,
    first_root,
    first_near,
    first_bias,
    second_adjacent,
    second_center,
    second_count,
    second_root,
    second_near,
    second_bias,
    upstream,
):
    owners = 128
    hidden_width = first_root.shape[1]
    z = lax.axis_index("z")
    core = lax.axis_index("core")[None]
    pair = weights_of_pair(jnp.concatenate([first_root, first_near], axis=0), z)
    columns = jnp.concatenate([first_adjacent, first_center[:, None]], axis=1).T
    packed = aggregate(features, columns, first_count[None], owner_map[None], owners)
    packed, pair = lax.optimization_barrier((packed, pair))
    other_pair = weights_of_others(pair)
    arrived = exchange(packed, AXES)
    count = second_count[:, None]
    picked, flipped = picks(second_adjacent, second_center[:, None], count, owners * 8)
    slots, depth = picked.shape[1], 2 * pair.shape[0]
    nodes = upstream.shape[0]
    layer_output, sent_two, hidden, rows, slope, inputs_flip, bias_grad = call(
        forward_kernel,
        (
            shaped(nodes, hidden_width),
            shaped(64, LANES, LANES),
            shaped(slots, hidden_width),
            shaped(2 * nodes, hidden_width),
            shaped(nodes, hidden_width),
            shaped(depth, slots),
            shaped(8, hidden_width, dtype=jnp.float32),
        ),
        12,
        smem=2,
        scratch=[pltpu.VMEM((slots, depth), jnp.bfloat16)],
        limit=14,
        flops=6_000_000_000,
        moved=18_000_000,
        exps=3_000_000,
    )(
        core, z[None], arrived, pair, other_pair, first_bias[None], picked, count, second_root, second_near,
        second_bias[None], upstream,
    )
    received = lax.ppermute(sent_two, "core", [(0, 1), (1, 0)])
    (back,) = call(
        backward_kernel, (shaped(2 * nodes, hidden_width),), 4, limit=10,
        flops=2_100_000_000, moved=7_000_000,
    )(slope, second_root, second_near, count)
    (both,) = call(
        kept_kernel, (shaped(64, LANES, LANES),), 4, smem=1, limit=10,
        flops=1_000_000_000, moved=7_000_000,
    )(core, rows, slope, received)
    terms = exchange(both, CHIPS)
    kept_one, sent_one = call(
        first_grads_kernel,
        (shaped(4, 48, hidden_width), shaped(4, 48, hidden_width)), 7, smem=2,
        scratch=[
            pltpu.VMEM((depth // 32, 32, hidden_width), jnp.bfloat16),
            pltpu.VMEM((8, hidden_width), jnp.float32),
        ],
        limit=10, flops=2_600_000_000, moved=7_500_000, exps=1_000_000,
    )(core, z[None], flipped, back, hidden, inputs_flip, bias_grad)
    total = jnp.sum(terms.astype(jnp.float32), axis=0).astype(jnp.bfloat16)
    mine = exchange(jnp.broadcast_to(total[None], terms.shape), CHIPS)
    part = plus(kept_one, lax.ppermute(sent_one, "core", [(0, 1), (1, 0)]))
    part = plus(part[:2], lax.ppermute(part[2:], "z", PAIRS[1]))
    part = plus(part[0], lax.ppermute(part[1], "z", PAIRS[3]))
    for axis in ("x", "y"):
        for step_size in (1, 3):
            part = plus(part, lax.ppermute(part, axis, PAIRS[step_size]))
    partner = lax.ppermute(part, "core", [(0, 1), (1, 0)])
    even = core[0] == 0
    first = jnp.where(even, part, partner).astype(jnp.float32)
    second = jnp.where(even, partner, part).astype(jnp.float32)
    other = lax.ppermute(mine, "core", [(0, 1), (1, 0)])
    root_two, near_two = spread(core, mine, other, hidden_width)
    return (layer_output, root_two, near_two, first[32], first[:32], second[:32], second[32])


def solution(mesh):
    chips = Mesh(mesh.devices.reshape(4, 4, 4, 2), AXES)
    trainer = ("x", "y", "core")
    return jax.shard_map(
        step,
        mesh=chips,
        in_specs=(
            P("z", trainer),
            P(trainer, None),
            P(trainer),
            P(trainer),
            P(trainer),
            P("z", None),
            P("z", None),
            P(),
            P(AXES, None),
            P(AXES),
            P(AXES),
            P(),
            P(),
            P(),
            P(AXES, None),
        ),
        out_specs=(
            P(AXES, None),
            P(),
            P(),
            P(),
            P("z", None),
            P("z", None),
            P(),
        ),
        check_vma=False,
    )
```

```python
import jax
import jax.numpy as jnp
from jax import lax
from jax.experimental import pallas as pl
from jax.experimental.pallas import tpu as pltpu
from jax.sharding import Mesh, PartitionSpec as P


CAP = 32
LANES = 128
AXES = ("z", "x", "y", "core")
CHIPS = ("z", "x", "y")
CHUNK = 152
VMEM = pl.BlockSpec(memory_space=pltpu.VMEM)
ALONG_LANES = lax.GatherDimensionNumbers(
    offset_dims=(),
    collapsed_slice_dims=(1,),
    start_index_map=(1,),
    operand_batching_dims=(0,),
    start_indices_batching_dims=(0,),
)
SMEM = pl.BlockSpec(memory_space=pltpu.SMEM)
HBM = pl.BlockSpec(memory_space=pltpu.HBM)


def lanes_at(at, size=LANES):
    return pl.ds(pl.multiple_of(at * size, size), size)


def across(left, right):
    return lax.dot_general(
        left, right, (((0,), (0,)), ((), ())), preferred_element_type=jnp.float32
    )


def along(left, right):
    return lax.dot_general(
        left, right, (((1,), (1,)), ((), ())), preferred_element_type=jnp.float32
    )


def matmul(left, right):
    return jnp.dot(left, right, preferred_element_type=jnp.float32)


def take_lanes(rows, index):
    return lax.gather(
        rows, index[..., None], ALONG_LANES, (1, 1), mode=lax.GatherScatterMode.PROMISE_IN_BOUNDS
    )


def find(load, high, low, chunks, parts):
    bits = [lax.bitwise_and(high, jnp.int16(1 << b)) != jnp.int16(0) for b in range(5)]

    def among(start, size, bit):
        if size == 1:
            return [take_lanes(load(start, v), low) for v in range(parts)]
        first = among(start, size // 2, bit - 1)
        last = among(start + size // 2, size // 2, bit - 1)
        return [jnp.where(bits[bit], q, p) for p, q in zip(first, last)]

    return among(0, chunks, chunks.bit_length() - 2)


def aggregate_kernel(feat_ref, adj_ref, count_ref, owner_ref, out_ref, index, rows, places, stage, wide):
    width, inputs = feat_ref.shape
    nodes = owner_ref.shape[1]
    owners = out_ref.shape[0]
    fan = adj_ref.shape[0] - 1
    chunks = inputs // LANES
    groups = nodes // LANES
    parts = width // 16
    steps = (fan + 1) // 4
    i16, bf16, f32 = jnp.int16, jnp.bfloat16, jnp.float32
    for g in range(groups):
        for s in range(steps):
            index[g * steps + s, 0:4] = adj_ref[s * 4 : s * 4 + 4, g * LANES : (g + 1) * LANES]

    def one_group(g, carry):
        count = count_ref[:, lanes_at(g)]

        def four(s, total):
            total = list(total)
            for j in range(4):
                at = index[g * steps + s, j : j + 1, :]
                high = jnp.broadcast_to(lax.shift_right_logical(at, 7), (16, LANES)).astype(i16)
                low = jnp.broadcast_to(lax.bitwise_and(at, LANES - 1), (16, LANES)).astype(i16)
                valid = jnp.broadcast_to(s * 4 + j < count, (16, LANES))
                found = find(
                    lambda c, v: feat_ref[v * 16 : (v + 1) * 16, c * LANES : (c + 1) * LANES],
                    high, low, chunks, parts,
                )
                if j == 3:
                    for v in range(parts):
                        rows[v * 16 : (v + 1) * 16, lanes_at(g)] = found[v]
                for v in range(parts):
                    total[v] = total[v] + jnp.where(valid, found[v].astype(f32), 0.0)
            return tuple(total)

        zero = jnp.zeros((16, LANES), f32)
        total = lax.fori_loop(0, steps, four, (zero,) * parts)
        divisor = jnp.broadcast_to(count.astype(f32), (16, LANES))
        for v in range(parts):
            near = (total[v] / divisor).astype(bf16)
            rows[width + v * 16 : width + (v + 1) * 16, lanes_at(g)] = near
        return carry

    lax.fori_loop(0, groups, one_group, 0)

    span = 256
    before = (
        lax.broadcasted_iota(jnp.int32, (span, span), 0)
        < lax.broadcasted_iota(jnp.int32, (span, span), 1)
    ).astype(bf16)
    owner_ids = lax.broadcasted_iota(jnp.int32, (owners, span), 0)
    ranks = lax.broadcasted_iota(jnp.int32, (CAP, span), 0)
    seen = jnp.zeros((owners, 1), f32)
    found_at = jnp.zeros((3 * CAP, owners), f32)
    for b in range(nodes // span):
        hit = owner_ids == owner_ref[:, b * span : (b + 1) * span]
        picked = hit.astype(bf16)
        earlier = matmul(picked, before) + seen
        rank = jnp.sum(jnp.where(hit, earlier, 0.0), axis=0, keepdims=True).astype(jnp.int32)
        seen = seen + jnp.sum(jnp.where(hit, 1.0, 0.0), axis=1, keepdims=True)
        node = lax.broadcasted_iota(jnp.int32, (CAP, span), 1) + b * span
        mine = ranks == rank
        weights = jnp.concatenate(
            [
                jnp.where(mine, lax.shift_right_logical(node, 7), 0).astype(f32),
                jnp.where(mine, lax.bitwise_and(node, LANES - 1), 0).astype(f32),
                jnp.where(mine, 1.0, 0.0),
            ],
            axis=0,
        ).astype(bf16)
        found_at = found_at + along(weights, picked)
    found_at = found_at.astype(jnp.int32)
    for q in range(CAP // 4):
        for kind in range(3):
            at = kind * CAP + q * 4
            places[q, kind * 4 : (kind + 1) * 4] = found_at[at : at + 4]

    half = 2 * width

    def four_ranks(q, carry):
        for j in range(4):
            high = jnp.broadcast_to(places[q, j : j + 1, :], (16, owners)).astype(i16)
            low = jnp.broadcast_to(places[q, 4 + j : 5 + j, :], (16, owners)).astype(i16)
            filled = jnp.broadcast_to(places[q, 8 + j : 9 + j, :], (16, owners)) > 0
            found = find(
                lambda c, v: rows[v * 16 : (v + 1) * 16, c * LANES : (c + 1) * LANES],
                high, low, groups, half // 16,
            )
            for v in range(half // 16):
                at = (j % 2) * half + v * 16
                stage[j // 2, at : at + 16, :] = jnp.where(filled, found[v].astype(f32), 0.0)
        for pair in range(2):
            wide[pl.ds(q * 2 + pair, owners, stride=16), :] = stage[pair].T
        return carry

    lax.fori_loop(0, CAP // 4, four_ranks, 0)

    def finish(t, carry):
        at = pl.ds(pl.multiple_of(t * 8, 8), 8)
        out_ref[at] = wide[lanes_at(t), :].astype(bf16).reshape(8, 16, LANES)
        return carry

    lax.fori_loop(0, owners // 8, finish, 0)


def aggregate(features, adjacent, count, owner, owners):
    width, _ = features.shape
    nodes = owner.shape[1]
    return pl.pallas_call(
        aggregate_kernel,
        out_shape=jax.ShapeDtypeStruct((owners, 16, LANES), jnp.bfloat16),
        in_specs=[VMEM] * 4,
        out_specs=VMEM,
        scratch_shapes=[
            pltpu.VMEM((nodes // LANES * 4, 4, LANES), jnp.int32),
            pltpu.VMEM((2 * width, nodes), jnp.bfloat16),
            pltpu.VMEM((CAP // 4, 12, LANES), jnp.int32),
            pltpu.VMEM((2, 4 * width, owners), jnp.float32),
            pltpu.VMEM((16 * owners, LANES), jnp.float32),
        ],
        name="aggregate",
        compiler_params=pltpu.CompilerParams(vmem_limit_bytes=12 << 20),
        cost_estimate=pl.CostEstimate(flops=40_000_000, bytes_accessed=3_000_000, transcendentals=0),
    )(features, adjacent, count, owner)


def picks_kernel(adj_ref, center_ref, count_ref, out_hbm, flip_hbm, out_ref, flip_ref, sent):
    nodes, fan = adj_ref.shape
    slots = out_ref.shape[1]

    def table_row(slot):
        odd = lax.shift_left(lax.bitwise_and(slot, 1), 4)
        pair = lax.bitwise_and(lax.shift_right_logical(slot, 1), 15)
        return lax.bitwise_and(slot, -CAP) + odd + pair

    def one_tile(t, carry):
        at = pl.ds(pl.multiple_of(t * 16, 16), 16)
        number = lax.broadcasted_iota(jnp.int32, (16, fan), 1)
        adjacent = jnp.where(number < count_ref[at, :], table_row(adj_ref[at, :]), -1)
        center = jnp.broadcast_to(table_row(center_ref[at, :]), (16, LANES))
        spread = [jnp.broadcast_to(adjacent[:, k : k + 1], (16, LANES)) for k in range(fan)]
        for c in range(slots // LANES):
            ids = lax.broadcasted_iota(jnp.int32, (16, LANES), 1) + c * LANES
            total = jnp.zeros((16, LANES), jnp.float32)
            for k in range(fan):
                total = total + jnp.where(spread[k] == ids, 1.0, 0.0)
            out_ref[at, c * LANES : (c + 1) * LANES] = jnp.where(center == ids, 1.0, 0.0).astype(
                out_ref.dtype
            )
            low = pl.ds(pl.multiple_of(nodes + t * 16, 16), 16)
            out_ref[low, c * LANES : (c + 1) * LANES] = total.astype(out_ref.dtype)
        return carry

    lax.fori_loop(0, nodes // 16, one_tile, 0)
    straight = pltpu.make_async_copy(out_ref, out_hbm, sent.at[0])
    straight.start()

    def one_flip(t, carry):
        flip_ref[:, lanes_at(t)] = out_ref[lanes_at(t), :].T
        return carry

    lax.fori_loop(0, 2 * nodes // LANES, one_flip, 0)
    flipped = pltpu.make_async_copy(flip_ref, flip_hbm, sent.at[1])
    flipped.start()
    straight.wait()
    flipped.wait()


def picks(adjacent, center, count, slots):
    nodes = adjacent.shape[0]
    return pl.pallas_call(
        picks_kernel,
        out_shape=(shaped(2 * nodes, slots), shaped(slots, 2 * nodes)),
        in_specs=[VMEM] * 3,
        out_specs=(HBM, HBM),
        scratch_shapes=[
            pltpu.VMEM((2 * nodes, slots), jnp.bfloat16),
            pltpu.VMEM((slots, 2 * nodes), jnp.bfloat16),
            pltpu.SemaphoreType.DMA((2,)),
        ],
        name="picks",
        compiler_params=pltpu.CompilerParams(vmem_limit_bytes=60 << 20),
        cost_estimate=pl.CostEstimate(flops=20_000_000, bytes_accessed=5_000_000, transcendentals=0),
    )(adjacent, center, count)


def call(kernel, outs, ins, smem=0, hbm=0, hbm_outs=0, scratch=(), limit=60, flops=0, moved=0, exps=0):
    return pl.pallas_call(
        kernel,
        out_shape=outs,
        in_specs=[SMEM] * smem + [VMEM] * (ins - smem - hbm) + [HBM] * hbm,
        out_specs=(VMEM,) * (len(outs) - hbm_outs) + (HBM,) * hbm_outs,
        scratch_shapes=scratch,
        compiler_params=pltpu.CompilerParams(vmem_limit_bytes=limit << 20),
        cost_estimate=pl.CostEstimate(flops=flops, bytes_accessed=moved, transcendentals=exps),
    )


def put_chunks(to_ref, t, product):
    for c in range(product.shape[0] // 16):
        for lane in range(product.shape[1] // LANES):
            to_ref[t * (product.shape[0] // 16) + c, lane * 16 : (lane + 1) * 16, :] = product[
                c * 16 : (c + 1) * 16, lane * LANES : (lane + 1) * LANES
            ]


def forward_kernel(
    core_ref, z_ref, arrived_ref, pair_ref, other_pair_ref, bias_one_ref, count_ref, bias_two_ref,
    picks_hbm, root_hbm, near_hbm, upstream_hbm, bias_grad, out_hbm, sent_hbm, hidden_hbm,
    rows_hbm, slope_hbm, inputs_flip_hbm, inputs, picks_ref, root_ref, near_ref, upstream_ref,
    out_ref, sent_ref, hidden, rows, slope, inputs_flip, arrivals, departures, sendings,
):
    leaving = {
        name: pltpu.make_async_copy(source, target, departures.at[number])
        for number, (name, source, target) in enumerate(
            (
                ("out", out_ref, out_hbm),
                ("hidden", hidden, hidden_hbm),
                ("rows", rows, rows_hbm),
                ("slope", slope, slope_hbm),
                ("inputs_flip", inputs_flip, inputs_flip_hbm),
            )
        )
    }
    copies = [
        pltpu.make_async_copy(source, target, arrivals.at[number])
        for number, (source, target) in enumerate(
            (
                (picks_hbm, picks_ref),
                (root_hbm, root_ref),
                (near_hbm, near_ref),
                (upstream_hbm, upstream_ref),
            )
        )
    ]
    for copy in copies:
        copy.start()
    slots, depth = inputs.shape
    hidden_width = hidden.shape[1]
    nodes = slope.shape[0]
    quarter = depth // 4
    sources = slots // CAP
    tile = 256

    def one_source(t, carry):
        for e in range(2):
            pieces = [
                arrived_ref[f * sources + t, :, e * quarter : (e + 1) * quarter] for f in range(4)
            ]
            at = pl.ds(pl.multiple_of(t * CAP + e * 16, 16), 16)
            inputs[at, :] = jnp.concatenate(pieces, axis=1)
        return carry

    lax.fori_loop(0, sources, one_source, 0)
    for t in range(slots // tile):
        inputs_flip[:, t * tile : (t + 1) * tile] = inputs[t * tile : (t + 1) * tile, :].T
    leaving["inputs_flip"].start()

    late = z_ref[0] >= 2

    def first_layer(t, carry):
        cols = lanes_at(t, tile)
        pair, other = pair_ref[:, cols], other_pair_ref[:, cols]
        pre = matmul(inputs[:, : depth // 2], jnp.where(late, other, pair))
        pre = pre + matmul(inputs[:, depth // 2 :], jnp.where(late, pair, other))
        pre = pre + bias_one_ref[:, cols]
        value = jnp.maximum(pre, 0.0) + jnp.log1p(jnp.exp(-jnp.abs(pre)))
        hidden[:, cols] = value.astype(jnp.bfloat16)
        return carry

    lax.fori_loop(0, hidden_width // tile, first_layer, 0)
    leaving["hidden"].start()
    inverse = 1.0 / count_ref[...].astype(jnp.float32)
    copies[0].wait()

    def select(t, carry):
        cols = lanes_at(t, tile)
        rows[:nodes, cols] = matmul(picks_ref[:nodes, :], hidden[:, cols]).astype(jnp.bfloat16)
        total = matmul(picks_ref[nodes:, :], hidden[:, cols])
        rows[nodes:, cols] = (total * inverse).astype(jnp.bfloat16)
        return carry

    lax.fori_loop(0, hidden_width // tile, select, 0)
    leaving["rows"].start()
    for copy in copies[1:]:
        copy.wait()

    def second_layer(t, carry):
        cols = lanes_at(t, tile)
        pre = matmul(rows[:nodes, :], root_ref[:, cols]) + matmul(rows[nodes:, :], near_ref[:, cols])
        pre = pre + bias_two_ref[:, cols]
        gate = jax.nn.sigmoid(pre)
        out_ref[:, cols] = (pre * gate).astype(jnp.bfloat16)
        grad = upstream_ref[:, cols].astype(jnp.float32) * gate * (1.0 + pre * (1.0 - gate))
        grad = grad.astype(jnp.bfloat16)
        slope[:, cols] = grad
        bias_grad[0:1, cols] = jnp.sum(grad.astype(jnp.float32), axis=0, keepdims=True)
        return carry

    lax.fori_loop(0, hidden_width // tile, second_layer, 0)
    leaving["slope"].start()
    leaving["out"].start()
    start = (core_ref[0] ^ 1) * nodes
    share = tile // 16

    def sending(t):
        part = pl.ds(t * share, share)
        return pltpu.make_async_copy(sent_ref.at[part], sent_hbm.at[part], sendings.at[t])

    def weight_grads(t, carry):
        left = rows[pl.ds(pl.multiple_of(start, nodes), nodes), lanes_at(t, tile)]
        put_chunks(sent_ref, t, across(left, slope[...]).astype(jnp.bfloat16))
        sending(t).start()
        return carry

    lax.fori_loop(0, hidden_width // tile, weight_grads, 0)
    for copy in leaving.values():
        copy.wait()
    for t in range(hidden_width // tile):
        sending(t).wait()


def kept_kernel(
    core_ref, kept_one_ref, received_one_ref, rows_hbm, slope_hbm, received_hbm, both_ref,
    rows_ref, slope_ref, received_ref, arrivals,
):
    nodes, hidden_width = slope_ref.shape
    tile = 256
    start = pl.ds(pl.multiple_of(core_ref[0] * nodes, nodes), nodes)
    copies = [
        pltpu.make_async_copy(source, target, arrivals.at[number])
        for number, (source, target) in enumerate(
            (
                (rows_hbm.at[start], rows_ref),
                (slope_hbm, slope_ref),
                (received_hbm, received_ref),
            )
        )
    ]
    for copy in copies:
        copy.start()
    copies[0].wait()
    copies[1].wait()
    copies[2].wait()

    def weight_grads(t, carry):
        left = rows_ref[:, lanes_at(t, tile)]
        product = across(left, slope_ref[...])
        for c in range(tile // 16):
            chunk = t * (tile // 16) + c
            for lane in range(hidden_width // LANES):
                at = slice(lane * 16, (lane + 1) * 16)
                mine = product[c * 16 : (c + 1) * 16, lane * LANES : (lane + 1) * LANES]
                other = received_ref[chunk, at, :].astype(jnp.float32)
                both_ref[chunk, at, :] = (mine + other).astype(jnp.bfloat16)
            mine = kept_one_ref[chunk].astype(jnp.float32)
            other = received_one_ref[chunk].astype(jnp.float32)
            both_ref[chunk, LANES:, :] = (mine + other).astype(jnp.bfloat16)
        return carry

    lax.fori_loop(0, hidden_width // tile, weight_grads, 0)


def backward_kernel(
    core_ref, count_ref, bias_two_ref, slope_hbm, root_hbm, near_hbm, flip_hbm, hidden_hbm,
    inputs_flip_hbm, kept_ref, sent_ref, back, bias_grads, slope_ref, root_ref, near_ref, flip_ref,
    hidden_ref, inputs_flip_ref, arrivals,
):
    copies = [
        pltpu.make_async_copy(source, target, arrivals.at[number])
        for number, (source, target) in enumerate(
            (
                (slope_hbm, slope_ref),
                (root_hbm, root_ref),
                (near_hbm, near_ref),
                (flip_hbm, flip_ref),
                (hidden_hbm, hidden_ref),
                (inputs_flip_hbm, inputs_flip_ref),
            )
        )
    ]
    for copy in copies:
        copy.start()
    core = core_ref[0]
    nodes, hidden_width = slope_ref.shape
    tile = 256
    bias_grads[0:1, :] = bias_two_ref[0:1, :]
    inverse = 1.0 / count_ref[...].astype(jnp.float32)

    def through_root(t, carry):
        cols = lanes_at(t, tile)
        back[:nodes, cols] = along(slope_ref[...], root_ref[cols, :]).astype(jnp.bfloat16)
        return carry

    def through_near(t, carry):
        cols = lanes_at(t, tile)
        near = along(slope_ref[...], near_ref[cols, :])
        back[nodes:, cols] = (near * inverse).astype(jnp.bfloat16)
        return carry

    copies[0].wait()
    copies[1].wait()
    lax.fori_loop(0, hidden_width // tile, through_root, 0)
    copies[2].wait()
    lax.fori_loop(0, hidden_width // tile, through_near, 0)
    for copy in copies[3:]:
        copy.wait()

    def first_grads(t, carry):
        cols = lanes_at(t, tile)
        table_grad = matmul(flip_ref[...], back[:, cols])
        grad = table_grad * (1.0 - jnp.exp(-hidden_ref[:, cols].astype(jnp.float32)))
        grad = grad.astype(jnp.bfloat16)
        bias_grads[1:2, cols] = jnp.sum(grad.astype(jnp.float32), axis=0, keepdims=True)
        for place, to_ref in enumerate((kept_ref, sent_ref)):
            which = core ^ place
            left = inputs_flip_ref[pl.ds(pl.multiple_of(which * LANES, LANES), LANES), :]
            product = matmul(left, grad).astype(jnp.bfloat16)
            for c in range(8):
                for lane in range(tile // LANES):
                    chunk = c * 8 + t * (tile // LANES) + lane
                    to_ref[chunk, 0:16, :] = product[
                        c * 16 : (c + 1) * 16, lane * LANES : (lane + 1) * LANES
                    ]
        return carry

    lax.fori_loop(0, hidden_width // tile, first_grads, 0)
    for place, to_ref in enumerate((kept_ref, sent_ref)):
        which = core ^ place
        to_ref[:, 16:, :] = jnp.zeros((to_ref.shape[0], 8, LANES), jnp.bfloat16)
        for lane in range(8):
            cols = slice(lane * LANES, (lane + 1) * LANES)
            row = jnp.where(which == 0, bias_grads[0:1, cols], bias_grads[1:2, cols])
            to_ref[lane, 16:, :] = jnp.broadcast_to(row, (8, LANES)).astype(jnp.bfloat16)


def shaped(*shape, dtype=jnp.bfloat16):
    return jax.ShapeDtypeStruct(shape, dtype)


def spread_kernel(core_ref, z_ref, kept_ref, other_ref, root_ref, near_ref, first_root_ref, first_near_ref, bias_two_ref, bias_one_ref):
    core, z = core_ref[0], z_ref[0]
    step = pl.program_id(0)
    even = core == 0
    for c in range(8):
        for lane in range(8):
            kept = kept_ref[c, lane * 16 : (lane + 1) * 16, :].astype(jnp.float32)
            other = other_ref[c, lane * 16 : (lane + 1) * 16, :].astype(jnp.float32)
            at, cols = slice(c * 16, (c + 1) * 16), slice(lane * LANES, (lane + 1) * LANES)
            root_ref[at, cols] = jnp.where(even, kept, other)
            near_ref[at, cols] = jnp.where(even, other, kept)

    here = lax.shift_right_logical(z, 1) == core
    base = lax.bitwise_and(z, 1) * 4
    for j, to_ref in enumerate((first_root_ref, first_near_ref)):
        for i in range(2):

            @pl.when(step == base + 2 * j + i)
            def _(to_ref=to_ref, i=i):
                for lane in range(8):
                    kept = kept_ref[lane, LANES : LANES + 16, :].astype(jnp.float32)
                    other = other_ref[lane, LANES : LANES + 16, :].astype(jnp.float32)
                    at, cols = slice(i * 16, (i + 1) * 16), slice(lane * LANES, (lane + 1) * LANES)
                    to_ref[at, cols] = jnp.where(here, kept, other)

    @pl.when(step == 0)
    def _():
        for lane in range(8):
            kept = kept_ref[lane, LANES + 16 :, :].astype(jnp.float32)[0:1, :]
            other = other_ref[lane, LANES + 16 :, :].astype(jnp.float32)[0:1, :]
            cols = slice(lane * LANES, (lane + 1) * LANES)
            bias_two_ref[:, cols] = jnp.where(even, kept, other)
            bias_one_ref[:, cols] = jnp.where(even, other, kept)


def spread(core, z, kept, other, hidden_width):
    f32 = jnp.float32
    wide = pl.BlockSpec((LANES, hidden_width), lambda s: (s, 0))
    slab = pl.BlockSpec((32, hidden_width), lambda s: (0, 0))
    line = pl.BlockSpec((1, hidden_width), lambda s: (0, 0))
    block = pl.BlockSpec((8, CHUNK, LANES), lambda s: (s, 0, 0))
    return pl.pallas_call(
        spread_kernel,
        grid=(8,),
        out_shape=(
            shaped(hidden_width, hidden_width, dtype=f32),
            shaped(hidden_width, hidden_width, dtype=f32),
            shaped(32, hidden_width, dtype=f32),
            shaped(32, hidden_width, dtype=f32),
            shaped(1, hidden_width, dtype=f32),
            shaped(1, hidden_width, dtype=f32),
        ),
        in_specs=[SMEM, SMEM, block, block],
        out_specs=(wide, wide, slab, slab, line, line),
        name="spread",
        compiler_params=pltpu.CompilerParams(vmem_limit_bytes=16 << 20),
    )(core, z, kept, other)


def weights_of_pair(own, z):
    first = lax.ppermute(own, "z", [(0, 1), (1, 0), (2, 3), (3, 2)])
    odd = lax.bitwise_and(z, 1) == 1
    return jnp.concatenate([jnp.where(odd, first, own), jnp.where(odd, own, first)], axis=0)


def weights_of_others(pair):
    return lax.ppermute(pair, "z", [(0, 3), (3, 0), (1, 2), (2, 1)])


def exchange(value, axes):
    return lax.all_to_all(value, axes, split_axis=0, concat_axis=0, tiled=True)


def step(
    features,
    first_adjacent,
    first_center,
    first_count,
    owner_map,
    first_root,
    first_near,
    first_bias,
    second_adjacent,
    second_center,
    second_count,
    second_root,
    second_near,
    second_bias,
    upstream,
):
    owners = 128
    hidden_width = first_root.shape[1]
    z = lax.axis_index("z")
    core = lax.axis_index("core")[None]
    pair = weights_of_pair(jnp.concatenate([first_root, first_near], axis=0), z)
    columns = jnp.concatenate([first_adjacent, first_center[:, None]], axis=1).T
    packed = aggregate(features, columns, first_count[None], owner_map[None], owners)
    packed, pair = lax.optimization_barrier((packed, pair))
    other_pair = weights_of_others(pair)
    arrived = exchange(packed, AXES)
    count = second_count[:, None]
    picked, flipped = picks(second_adjacent, second_center[:, None], count, owners * 8)
    slots, depth = picked.shape[1], 2 * pair.shape[0]
    nodes = upstream.shape[0]
    bf16, f32 = jnp.bfloat16, jnp.float32
    bias_grad, layer_output, sent_two, hidden, rows, slope, inputs_flip = call(
        forward_kernel,
        (
            shaped(8, hidden_width, dtype=f32),
            shaped(nodes, hidden_width),
            shaped(64, LANES, LANES),
            shaped(slots, hidden_width),
            shaped(2 * nodes, hidden_width),
            shaped(nodes, hidden_width),
            shaped(depth, slots),
        ),
        12,
        smem=2,
        hbm=4,
        limit=60,
        hbm_outs=6,
        scratch=[
            pltpu.VMEM((slots, depth), bf16),
            pltpu.VMEM(picked.shape, bf16),
            pltpu.VMEM(second_root.shape, bf16),
            pltpu.VMEM(second_near.shape, bf16),
            pltpu.VMEM(upstream.shape, bf16),
            pltpu.VMEM((nodes, hidden_width), bf16),
            pltpu.VMEM((64, LANES, LANES), bf16),
            pltpu.VMEM((slots, hidden_width), bf16),
            pltpu.VMEM((2 * nodes, hidden_width), bf16),
            pltpu.VMEM((nodes, hidden_width), bf16),
            pltpu.VMEM((depth, slots), bf16),
            pltpu.SemaphoreType.DMA((4,)),
            pltpu.SemaphoreType.DMA((5,)),
            pltpu.SemaphoreType.DMA((4,)),
        ],
        flops=6_000_000_000,
        moved=18_000_000,
        exps=3_000_000,
    )(
        core, z[None], arrived, pair, other_pair, first_bias[None], count, second_bias[None],
        picked, second_root, second_near, upstream,
    )
    received = lax.ppermute(sent_two, "core", [(0, 1), (1, 0)])
    kept_one, sent_one = call(
        backward_kernel, (shaped(64, 24, LANES), shaped(64, 24, LANES)), 9, smem=1,
        hbm=6,
        scratch=[
            pltpu.VMEM((2 * nodes, hidden_width), bf16),
            pltpu.VMEM((8, hidden_width), f32),
            pltpu.VMEM((nodes, hidden_width), bf16),
            pltpu.VMEM(second_root.shape, bf16),
            pltpu.VMEM(second_near.shape, bf16),
            pltpu.VMEM(flipped.shape, bf16),
            pltpu.VMEM((slots, hidden_width), bf16),
            pltpu.VMEM((depth, slots), bf16),
            pltpu.SemaphoreType.DMA((6,)),
        ],
        flops=4_700_000_000, moved=12_000_000, exps=1_000_000,
    )(core, count, bias_grad, slope, second_root, second_near, flipped, hidden, inputs_flip)
    received_one = lax.ppermute(sent_one, "core", [(0, 1), (1, 0)])
    (both,) = call(
        kept_kernel, (shaped(64, CHUNK, LANES),), 6, smem=1, hbm=3, limit=24,
        scratch=[
            pltpu.VMEM((nodes, hidden_width), bf16),
            pltpu.VMEM((nodes, hidden_width), bf16),
            pltpu.VMEM((64, LANES, LANES), bf16),
            pltpu.SemaphoreType.DMA((3,)),
        ],
        flops=1_000_000_000, moved=7_000_000,
    )(core, kept_one, received_one, rows, slope, received)
    terms = exchange(both, CHIPS)
    total = jnp.sum(terms.astype(jnp.float32), axis=0).astype(jnp.bfloat16)
    mine = exchange(jnp.broadcast_to(total[None], terms.shape), CHIPS)
    other = lax.ppermute(mine, "core", [(0, 1), (1, 0)])
    root_two, near_two, root_one, near_one, bias_two, bias_one = spread(
        core, z[None], mine, other, hidden_width
    )
    return (layer_output, root_two, near_two, bias_two[0], root_one, near_one, bias_one[0])


def solution(mesh):
    chips = Mesh(mesh.devices.reshape(4, 4, 4, 2), AXES)
    trainer = ("x", "y", "core")
    return jax.shard_map(
        step,
        mesh=chips,
        in_specs=(
            P("z", trainer),
            P(trainer, None),
            P(trainer),
            P(trainer),
            P(trainer),
            P("z", None),
            P("z", None),
            P(),
            P(AXES, None),
            P(AXES),
            P(AXES),
            P(),
            P(),
            P(),
            P(AXES, None),
        ),
        out_specs=(
            P(AXES, None),
            P(),
            P(),
            P(),
            P("z", None),
            P("z", None),
            P(),
        ),
        check_vma=False,
    )
```

```python
import jax
import jax.numpy as jnp
from jax import lax
from jax.experimental import pallas as pl
from jax.experimental.pallas import tpu as pltpu
from jax.sharding import Mesh, PartitionSpec as P


CAP = 32
LANES = 128
AXES = ("z", "x", "y", "core")
CHIPS = ("z", "x", "y")
CHUNK = 152
VMEM = pl.BlockSpec(memory_space=pltpu.VMEM)
ALONG_LANES = lax.GatherDimensionNumbers(
    offset_dims=(),
    collapsed_slice_dims=(1,),
    start_index_map=(1,),
    operand_batching_dims=(0,),
    start_indices_batching_dims=(0,),
)
SMEM = pl.BlockSpec(memory_space=pltpu.SMEM)
HBM = pl.BlockSpec(memory_space=pltpu.HBM)


def lanes_at(at, size=LANES):
    return pl.ds(pl.multiple_of(at * size, size), size)


def across(left, right):
    return lax.dot_general(
        left, right, (((0,), (0,)), ((), ())), preferred_element_type=jnp.float32
    )


def along(left, right):
    return lax.dot_general(
        left, right, (((1,), (1,)), ((), ())), preferred_element_type=jnp.float32
    )


def matmul(left, right):
    return jnp.dot(left, right, preferred_element_type=jnp.float32)


def take_lanes(rows, index):
    return lax.gather(
        rows, index[..., None], ALONG_LANES, (1, 1), mode=lax.GatherScatterMode.PROMISE_IN_BOUNDS
    )


def find(load, high, low, chunks, parts):
    bits = [lax.bitwise_and(high, jnp.int16(1 << b)) != jnp.int16(0) for b in range(5)]

    def among(start, size, bit):
        if size == 1:
            return [take_lanes(load(start, v), low) for v in range(parts)]
        first = among(start, size // 2, bit - 1)
        last = among(start + size // 2, size // 2, bit - 1)
        return [jnp.where(bits[bit], q, p) for p, q in zip(first, last)]

    return among(0, chunks, chunks.bit_length() - 2)


def aggregate_kernel(feat_ref, adj_ref, count_ref, owner_ref, out_ref, index, rows, places, stage, wide):
    width, inputs = feat_ref.shape
    nodes = owner_ref.shape[1]
    owners = out_ref.shape[0]
    fan = adj_ref.shape[0] - 1
    chunks = inputs // LANES
    groups = nodes // LANES
    parts = width // 16
    steps = (fan + 1) // 4
    i16, bf16, f32 = jnp.int16, jnp.bfloat16, jnp.float32
    for g in range(groups):
        for s in range(steps):
            index[g * steps + s, 0:4] = adj_ref[s * 4 : s * 4 + 4, g * LANES : (g + 1) * LANES]

    def one_group(g, carry):
        count = count_ref[:, lanes_at(g)]

        def four(s, total):
            total = list(total)
            for j in range(4):
                at = index[g * steps + s, j : j + 1, :]
                high = jnp.broadcast_to(lax.shift_right_logical(at, 7), (16, LANES)).astype(i16)
                low = jnp.broadcast_to(lax.bitwise_and(at, LANES - 1), (16, LANES)).astype(i16)
                valid = jnp.broadcast_to(s * 4 + j < count, (16, LANES))
                found = find(
                    lambda c, v: feat_ref[v * 16 : (v + 1) * 16, c * LANES : (c + 1) * LANES],
                    high, low, chunks, parts,
                )
                if j == 3:
                    for v in range(parts):
                        rows[v * 16 : (v + 1) * 16, lanes_at(g)] = found[v]
                for v in range(parts):
                    total[v] = total[v] + jnp.where(valid, found[v].astype(f32), 0.0)
            return tuple(total)

        zero = jnp.zeros((16, LANES), f32)
        total = lax.fori_loop(0, steps, four, (zero,) * parts)
        divisor = jnp.broadcast_to(count.astype(f32), (16, LANES))
        for v in range(parts):
            near = (total[v] / divisor).astype(bf16)
            rows[width + v * 16 : width + (v + 1) * 16, lanes_at(g)] = near
        return carry

    lax.fori_loop(0, groups, one_group, 0)

    span = 256
    before = (
        lax.broadcasted_iota(jnp.int32, (span, span), 0)
        < lax.broadcasted_iota(jnp.int32, (span, span), 1)
    ).astype(bf16)
    owner_ids = lax.broadcasted_iota(jnp.int32, (owners, span), 0)
    ranks = lax.broadcasted_iota(jnp.int32, (CAP, span), 0)
    seen = jnp.zeros((owners, 1), f32)
    found_at = jnp.zeros((3 * CAP, owners), f32)
    for b in range(nodes // span):
        hit = owner_ids == owner_ref[:, b * span : (b + 1) * span]
        picked = hit.astype(bf16)
        earlier = matmul(picked, before) + seen
        rank = jnp.sum(jnp.where(hit, earlier, 0.0), axis=0, keepdims=True).astype(jnp.int32)
        seen = seen + jnp.sum(jnp.where(hit, 1.0, 0.0), axis=1, keepdims=True)
        node = lax.broadcasted_iota(jnp.int32, (CAP, span), 1) + b * span
        mine = ranks == rank
        weights = jnp.concatenate(
            [
                jnp.where(mine, lax.shift_right_logical(node, 7), 0).astype(f32),
                jnp.where(mine, lax.bitwise_and(node, LANES - 1), 0).astype(f32),
                jnp.where(mine, 1.0, 0.0),
            ],
            axis=0,
        ).astype(bf16)
        found_at = found_at + along(weights, picked)
    found_at = found_at.astype(jnp.int32)
    for q in range(CAP // 4):
        for kind in range(3):
            at = kind * CAP + q * 4
            places[q, kind * 4 : (kind + 1) * 4] = found_at[at : at + 4]

    half = 2 * width

    def four_ranks(q, carry):
        for j in range(4):
            high = jnp.broadcast_to(places[q, j : j + 1, :], (16, owners)).astype(i16)
            low = jnp.broadcast_to(places[q, 4 + j : 5 + j, :], (16, owners)).astype(i16)
            filled = jnp.broadcast_to(places[q, 8 + j : 9 + j, :], (16, owners)) > 0
            found = find(
                lambda c, v: rows[v * 16 : (v + 1) * 16, c * LANES : (c + 1) * LANES],
                high, low, groups, half // 16,
            )
            for v in range(half // 16):
                at = (j % 2) * half + v * 16
                stage[j // 2, at : at + 16, :] = jnp.where(filled, found[v].astype(f32), 0.0)
        for pair in range(2):
            wide[pl.ds(q * 2 + pair, owners, stride=16), :] = stage[pair].T
        return carry

    lax.fori_loop(0, CAP // 4, four_ranks, 0)

    def finish(t, carry):
        at = pl.ds(pl.multiple_of(t * 8, 8), 8)
        out_ref[at] = wide[lanes_at(t), :].astype(bf16).reshape(8, 16, LANES)
        return carry

    lax.fori_loop(0, owners // 8, finish, 0)


def aggregate(features, adjacent, count, owner, owners):
    width, _ = features.shape
    nodes = owner.shape[1]
    return pl.pallas_call(
        aggregate_kernel,
        out_shape=jax.ShapeDtypeStruct((owners, 16, LANES), jnp.bfloat16),
        in_specs=[VMEM] * 4,
        out_specs=VMEM,
        scratch_shapes=[
            pltpu.VMEM((nodes // LANES * 4, 4, LANES), jnp.int32),
            pltpu.VMEM((2 * width, nodes), jnp.bfloat16),
            pltpu.VMEM((CAP // 4, 12, LANES), jnp.int32),
            pltpu.VMEM((2, 4 * width, owners), jnp.float32),
            pltpu.VMEM((16 * owners, LANES), jnp.float32),
        ],
        name="aggregate",
        compiler_params=pltpu.CompilerParams(vmem_limit_bytes=12 << 20),
        cost_estimate=pl.CostEstimate(flops=40_000_000, bytes_accessed=3_000_000, transcendentals=0),
    )(features, adjacent, count, owner)


def picks_kernel(adj_ref, center_ref, count_ref, out_ref, flip_ref):
    nodes, fan = adj_ref.shape
    slots = out_ref.shape[1]

    def table_row(slot):
        odd = lax.shift_left(lax.bitwise_and(slot, 1), 4)
        pair = lax.bitwise_and(lax.shift_right_logical(slot, 1), 15)
        return lax.bitwise_and(slot, -CAP) + odd + pair

    def one_tile(t, carry):
        at = pl.ds(pl.multiple_of(t * 16, 16), 16)
        number = lax.broadcasted_iota(jnp.int32, (16, fan), 1)
        adjacent = jnp.where(number < count_ref[at, :], table_row(adj_ref[at, :]), -1)
        center = jnp.broadcast_to(table_row(center_ref[at, :]), (16, LANES))
        spread = [jnp.broadcast_to(adjacent[:, k : k + 1], (16, LANES)) for k in range(fan)]
        for c in range(slots // LANES):
            ids = lax.broadcasted_iota(jnp.int32, (16, LANES), 1) + c * LANES
            total = jnp.zeros((16, LANES), jnp.float32)
            for k in range(fan):
                total = total + jnp.where(spread[k] == ids, 1.0, 0.0)
            out_ref[at, c * LANES : (c + 1) * LANES] = jnp.where(center == ids, 1.0, 0.0).astype(
                out_ref.dtype
            )
            low = pl.ds(pl.multiple_of(nodes + t * 16, 16), 16)
            out_ref[low, c * LANES : (c + 1) * LANES] = total.astype(out_ref.dtype)
        return carry

    lax.fori_loop(0, nodes // 16, one_tile, 0)

    def one_flip(t, carry):
        flip_ref[:, lanes_at(t)] = out_ref[lanes_at(t), :].T
        return carry

    lax.fori_loop(0, 2 * nodes // LANES, one_flip, 0)


def picks(adjacent, center, count, slots):
    nodes = adjacent.shape[0]
    return pl.pallas_call(
        picks_kernel,
        out_shape=(
            jax.ShapeDtypeStruct((2 * nodes, slots), jnp.bfloat16),
            jax.ShapeDtypeStruct((slots, 2 * nodes), jnp.bfloat16),
        ),
        in_specs=[VMEM] * 3,
        out_specs=(VMEM, VMEM),
        name="picks",
        compiler_params=pltpu.CompilerParams(vmem_limit_bytes=12 << 20),
        cost_estimate=pl.CostEstimate(flops=20_000_000, bytes_accessed=5_000_000, transcendentals=0),
    )(adjacent, center, count)


def call(kernel, outs, ins, smem=0, hbm=0, scratch=(), limit=16, flops=0, moved=0, exps=0):
    return pl.pallas_call(
        kernel,
        out_shape=outs,
        in_specs=[SMEM] * smem + [VMEM] * (ins - smem - hbm) + [HBM] * hbm,
        out_specs=(VMEM,) * len(outs),
        scratch_shapes=scratch,
        compiler_params=pltpu.CompilerParams(vmem_limit_bytes=limit << 20),
        cost_estimate=pl.CostEstimate(flops=flops, bytes_accessed=moved, transcendentals=exps),
    )


def in_hbm(value):
    return pltpu.with_memory_space_constraint(value, pltpu.HBM)


def put_chunks(to_ref, t, product):
    for c in range(product.shape[0] // 16):
        for lane in range(product.shape[1] // LANES):
            to_ref[t * (product.shape[0] // 16) + c, lane * 16 : (lane + 1) * 16, :] = product[
                c * 16 : (c + 1) * 16, lane * LANES : (lane + 1) * LANES
            ]


def forward_kernel(
    core_ref, z_ref, arrived_ref, pair_ref, other_pair_ref, bias_one_ref, count_ref, bias_two_ref,
    picks_hbm, root_hbm, near_hbm, upstream_hbm, out_ref, sent_ref, hidden, rows, slope,
    inputs_flip, bias_grad, inputs, picks_ref, root_ref, near_ref, upstream_ref, arrivals,
):
    copies = [
        pltpu.make_async_copy(source, target, arrivals.at[number])
        for number, (source, target) in enumerate(
            (
                (picks_hbm, picks_ref),
                (root_hbm, root_ref),
                (near_hbm, near_ref),
                (upstream_hbm, upstream_ref),
            )
        )
    ]
    for copy in copies:
        copy.start()
    slots, depth = inputs.shape
    hidden_width = hidden.shape[1]
    nodes = slope.shape[0]
    quarter = depth // 4
    sources = slots // CAP
    tile = 256

    def one_source(t, carry):
        for e in range(2):
            pieces = [
                arrived_ref[f * sources + t, :, e * quarter : (e + 1) * quarter] for f in range(4)
            ]
            at = pl.ds(pl.multiple_of(t * CAP + e * 16, 16), 16)
            inputs[at, :] = jnp.concatenate(pieces, axis=1)
        return carry

    lax.fori_loop(0, sources, one_source, 0)
    for t in range(slots // tile):
        inputs_flip[:, t * tile : (t + 1) * tile] = inputs[t * tile : (t + 1) * tile, :].T

    late = z_ref[0] >= 2

    def first_layer(t, carry):
        cols = lanes_at(t, tile)
        pair, other = pair_ref[:, cols], other_pair_ref[:, cols]
        pre = matmul(inputs[:, : depth // 2], jnp.where(late, other, pair))
        pre = pre + matmul(inputs[:, depth // 2 :], jnp.where(late, pair, other))
        pre = pre + bias_one_ref[:, cols]
        value = jnp.maximum(pre, 0.0) + jnp.log1p(jnp.exp(-jnp.abs(pre)))
        hidden[:, cols] = value.astype(jnp.bfloat16)
        return carry

    lax.fori_loop(0, hidden_width // tile, first_layer, 0)
    inverse = 1.0 / count_ref[...].astype(jnp.float32)
    copies[0].wait()

    def select(t, carry):
        cols = lanes_at(t, tile)
        rows[:nodes, cols] = matmul(picks_ref[:nodes, :], hidden[:, cols]).astype(jnp.bfloat16)
        total = matmul(picks_ref[nodes:, :], hidden[:, cols])
        rows[nodes:, cols] = (total * inverse).astype(jnp.bfloat16)
        return carry

    lax.fori_loop(0, hidden_width // tile, select, 0)
    for copy in copies[1:]:
        copy.wait()

    def second_layer(t, carry):
        cols = lanes_at(t, tile)
        pre = matmul(rows[:nodes, :], root_ref[:, cols]) + matmul(rows[nodes:, :], near_ref[:, cols])
        pre = pre + bias_two_ref[:, cols]
        gate = jax.nn.sigmoid(pre)
        out_ref[:, cols] = (pre * gate).astype(jnp.bfloat16)
        grad = upstream_ref[:, cols].astype(jnp.float32) * gate * (1.0 + pre * (1.0 - gate))
        grad = grad.astype(jnp.bfloat16)
        slope[:, cols] = grad
        bias_grad[0:1, cols] = jnp.sum(grad.astype(jnp.float32), axis=0, keepdims=True)
        return carry

    lax.fori_loop(0, hidden_width // tile, second_layer, 0)
    start = (core_ref[0] ^ 1) * nodes

    def weight_grads(t, carry):
        left = rows[pl.ds(pl.multiple_of(start, nodes), nodes), lanes_at(t, tile)]
        put_chunks(sent_ref, t, across(left, slope[...]).astype(jnp.bfloat16))
        return carry

    lax.fori_loop(0, hidden_width // tile, weight_grads, 0)


def kept_kernel(
    core_ref, rows_ref, slope_ref, received_ref, kept_one_ref, received_one_ref, both_ref
):
    nodes, hidden_width = slope_ref.shape
    tile = 256
    start = core_ref[0] * nodes

    def weight_grads(t, carry):
        left = rows_ref[pl.ds(pl.multiple_of(start, nodes), nodes), lanes_at(t, tile)]
        product = across(left, slope_ref[...])
        for c in range(tile // 16):
            chunk = t * (tile // 16) + c
            for lane in range(hidden_width // LANES):
                at = slice(lane * 16, (lane + 1) * 16)
                mine = product[c * 16 : (c + 1) * 16, lane * LANES : (lane + 1) * LANES]
                other = received_ref[chunk, at, :].astype(jnp.float32)
                both_ref[chunk, at, :] = (mine + other).astype(jnp.bfloat16)
            mine = kept_one_ref[chunk].astype(jnp.float32)
            other = received_one_ref[chunk].astype(jnp.float32)
            both_ref[chunk, LANES:, :] = (mine + other).astype(jnp.bfloat16)
        return carry

    lax.fori_loop(0, hidden_width // tile, weight_grads, 0)


def backward_kernel(
    core_ref, slope_ref, root_ref, near_ref, count_ref, flip_ref, hidden_ref, inputs_flip_ref,
    bias_two_ref, kept_ref, sent_ref, back, bias_grads,
):
    core = core_ref[0]
    nodes, hidden_width = slope_ref.shape
    tile = 256
    bias_grads[0:1, :] = bias_two_ref[0:1, :]
    inverse = 1.0 / count_ref[...].astype(jnp.float32)

    def backward(t, carry):
        cols = lanes_at(t, tile)
        back[:nodes, cols] = along(slope_ref[...], root_ref[cols, :]).astype(jnp.bfloat16)
        near = along(slope_ref[...], near_ref[cols, :])
        back[nodes:, cols] = (near * inverse).astype(jnp.bfloat16)
        return carry

    lax.fori_loop(0, hidden_width // tile, backward, 0)

    def first_grads(t, carry):
        cols = lanes_at(t, tile)
        table_grad = matmul(flip_ref[...], back[:, cols])
        grad = table_grad * (1.0 - jnp.exp(-hidden_ref[:, cols].astype(jnp.float32)))
        grad = grad.astype(jnp.bfloat16)
        bias_grads[1:2, cols] = jnp.sum(grad.astype(jnp.float32), axis=0, keepdims=True)
        for place, to_ref in enumerate((kept_ref, sent_ref)):
            which = core ^ place
            left = inputs_flip_ref[pl.ds(pl.multiple_of(which * LANES, LANES), LANES), :]
            product = matmul(left, grad).astype(jnp.bfloat16)
            for c in range(8):
                for lane in range(tile // LANES):
                    chunk = c * 8 + t * (tile // LANES) + lane
                    to_ref[chunk, 0:16, :] = product[
                        c * 16 : (c + 1) * 16, lane * LANES : (lane + 1) * LANES
                    ]
        return carry

    lax.fori_loop(0, hidden_width // tile, first_grads, 0)
    for place, to_ref in enumerate((kept_ref, sent_ref)):
        which = core ^ place
        to_ref[:, 16:, :] = jnp.zeros((to_ref.shape[0], 8, LANES), jnp.bfloat16)
        for lane in range(8):
            cols = slice(lane * LANES, (lane + 1) * LANES)
            row = jnp.where(which == 0, bias_grads[0:1, cols], bias_grads[1:2, cols])
            to_ref[lane, 16:, :] = jnp.broadcast_to(row, (8, LANES)).astype(jnp.bfloat16)


def shaped(*shape, dtype=jnp.bfloat16):
    return jax.ShapeDtypeStruct(shape, dtype)


def spread_kernel(core_ref, z_ref, kept_ref, other_ref, root_ref, near_ref, first_root_ref, first_near_ref, bias_two_ref, bias_one_ref):
    core, z = core_ref[0], z_ref[0]
    step = pl.program_id(0)
    even = core == 0
    for c in range(8):
        for lane in range(8):
            kept = kept_ref[c, lane * 16 : (lane + 1) * 16, :].astype(jnp.float32)
            other = other_ref[c, lane * 16 : (lane + 1) * 16, :].astype(jnp.float32)
            at, cols = slice(c * 16, (c + 1) * 16), slice(lane * LANES, (lane + 1) * LANES)
            root_ref[at, cols] = jnp.where(even, kept, other)
            near_ref[at, cols] = jnp.where(even, other, kept)

    here = lax.shift_right_logical(z, 1) == core
    base = lax.bitwise_and(z, 1) * 4
    for j, to_ref in enumerate((first_root_ref, first_near_ref)):
        for i in range(2):

            @pl.when(step == base + 2 * j + i)
            def _(to_ref=to_ref, i=i):
                for lane in range(8):
                    kept = kept_ref[lane, LANES : LANES + 16, :].astype(jnp.float32)
                    other = other_ref[lane, LANES : LANES + 16, :].astype(jnp.float32)
                    at, cols = slice(i * 16, (i + 1) * 16), slice(lane * LANES, (lane + 1) * LANES)
                    to_ref[at, cols] = jnp.where(here, kept, other)

    @pl.when(step == 0)
    def _():
        for lane in range(8):
            kept = kept_ref[lane, LANES + 16 :, :].astype(jnp.float32)[0:1, :]
            other = other_ref[lane, LANES + 16 :, :].astype(jnp.float32)[0:1, :]
            cols = slice(lane * LANES, (lane + 1) * LANES)
            bias_two_ref[:, cols] = jnp.where(even, kept, other)
            bias_one_ref[:, cols] = jnp.where(even, other, kept)


def spread(core, z, kept, other, hidden_width):
    f32 = jnp.float32
    wide = pl.BlockSpec((LANES, hidden_width), lambda s: (s, 0))
    slab = pl.BlockSpec((32, hidden_width), lambda s: (0, 0))
    line = pl.BlockSpec((1, hidden_width), lambda s: (0, 0))
    block = pl.BlockSpec((8, CHUNK, LANES), lambda s: (s, 0, 0))
    return pl.pallas_call(
        spread_kernel,
        grid=(8,),
        out_shape=(
            shaped(hidden_width, hidden_width, dtype=f32),
            shaped(hidden_width, hidden_width, dtype=f32),
            shaped(32, hidden_width, dtype=f32),
            shaped(32, hidden_width, dtype=f32),
            shaped(1, hidden_width, dtype=f32),
            shaped(1, hidden_width, dtype=f32),
        ),
        in_specs=[SMEM, SMEM, block, block],
        out_specs=(wide, wide, slab, slab, line, line),
        name="spread",
        compiler_params=pltpu.CompilerParams(vmem_limit_bytes=16 << 20),
    )(core, z, kept, other)


def weights_of_pair(own, z):
    first = lax.ppermute(own, "z", [(0, 1), (1, 0), (2, 3), (3, 2)])
    odd = lax.bitwise_and(z, 1) == 1
    return jnp.concatenate([jnp.where(odd, first, own), jnp.where(odd, own, first)], axis=0)


def weights_of_others(pair):
    return lax.ppermute(pair, "z", [(0, 3), (3, 0), (1, 2), (2, 1)])


def exchange(value, axes):
    return lax.all_to_all(value, axes, split_axis=0, concat_axis=0, tiled=True)


def step(
    features,
    first_adjacent,
    first_center,
    first_count,
    owner_map,
    first_root,
    first_near,
    first_bias,
    second_adjacent,
    second_center,
    second_count,
    second_root,
    second_near,
    second_bias,
    upstream,
):
    owners = 128
    hidden_width = first_root.shape[1]
    z = lax.axis_index("z")
    core = lax.axis_index("core")[None]
    pair = weights_of_pair(jnp.concatenate([first_root, first_near], axis=0), z)
    columns = jnp.concatenate([first_adjacent, first_center[:, None]], axis=1).T
    packed = aggregate(features, columns, first_count[None], owner_map[None], owners)
    packed, pair = lax.optimization_barrier((packed, pair))
    other_pair = weights_of_others(pair)
    arrived = exchange(packed, AXES)
    count = second_count[:, None]
    picked, flipped = picks(second_adjacent, second_center[:, None], count, owners * 8)
    slots, depth = picked.shape[1], 2 * pair.shape[0]
    nodes = upstream.shape[0]
    layer_output, sent_two, hidden, rows, slope, inputs_flip, bias_grad = call(
        forward_kernel,
        (
            shaped(nodes, hidden_width),
            shaped(64, LANES, LANES),
            shaped(slots, hidden_width),
            shaped(2 * nodes, hidden_width),
            shaped(nodes, hidden_width),
            shaped(depth, slots),
            shaped(8, hidden_width, dtype=jnp.float32),
        ),
        12,
        smem=2,
        hbm=4,
        scratch=[
            pltpu.VMEM((slots, depth), jnp.bfloat16),
            pltpu.VMEM(picked.shape, jnp.bfloat16),
            pltpu.VMEM(second_root.shape, jnp.bfloat16),
            pltpu.VMEM(second_near.shape, jnp.bfloat16),
            pltpu.VMEM(upstream.shape, jnp.bfloat16),
            pltpu.SemaphoreType.DMA((4,)),
        ],
        limit=24,
        flops=6_000_000_000,
        moved=18_000_000,
        exps=3_000_000,
    )(
        core, z[None], arrived, pair, other_pair, first_bias[None], count, second_bias[None],
        in_hbm(picked), in_hbm(second_root), in_hbm(second_near), in_hbm(upstream),
    )
    received = lax.ppermute(sent_two, "core", [(0, 1), (1, 0)])
    kept_one, sent_one = call(
        backward_kernel, (shaped(64, 24, LANES), shaped(64, 24, LANES)), 9, smem=1,
        scratch=[
            pltpu.VMEM((2 * nodes, hidden_width), jnp.bfloat16),
            pltpu.VMEM((8, hidden_width), jnp.float32),
        ],
        limit=24, flops=4_700_000_000, moved=12_000_000, exps=1_000_000,
    )(core, slope, second_root, second_near, count, flipped, hidden, inputs_flip, bias_grad)
    received_one = lax.ppermute(sent_one, "core", [(0, 1), (1, 0)])
    (both,) = call(
        kept_kernel, (shaped(64, CHUNK, LANES),), 6, smem=1, limit=20,
        flops=1_000_000_000, moved=7_000_000,
    )(core, rows, slope, received, kept_one, received_one)
    terms = exchange(both, CHIPS)
    total = jnp.sum(terms.astype(jnp.float32), axis=0).astype(jnp.bfloat16)
    mine = exchange(jnp.broadcast_to(total[None], terms.shape), CHIPS)
    other = lax.ppermute(mine, "core", [(0, 1), (1, 0)])
    root_two, near_two, root_one, near_one, bias_two, bias_one = spread(
        core, z[None], mine, other, hidden_width
    )
    return (layer_output, root_two, near_two, bias_two[0], root_one, near_one, bias_one[0])


def solution(mesh):
    chips = Mesh(mesh.devices.reshape(4, 4, 4, 2), AXES)
    trainer = ("x", "y", "core")
    return jax.shard_map(
        step,
        mesh=chips,
        in_specs=(
            P("z", trainer),
            P(trainer, None),
            P(trainer),
            P(trainer),
            P(trainer),
            P("z", None),
            P("z", None),
            P(),
            P(AXES, None),
            P(AXES),
            P(AXES),
            P(),
            P(),
            P(),
            P(AXES, None),
        ),
        out_specs=(
            P(AXES, None),
            P(),
            P(),
            P(),
            P("z", None),
            P("z", None),
            P(),
        ),
        check_vma=False,
    )
```

```python
import jax
import jax.numpy as jnp
from jax import lax
from jax.experimental import pallas as pl
from jax.experimental.pallas import tpu as pltpu
from jax.sharding import Mesh, PartitionSpec as P


CAP = 32
LANES = 128
AXES = ("z", "x", "y", "core")
CHIPS = ("z", "x", "y")
CHUNK = 152
VMEM = pl.BlockSpec(memory_space=pltpu.VMEM)
ALONG_LANES = lax.GatherDimensionNumbers(
    offset_dims=(),
    collapsed_slice_dims=(1,),
    start_index_map=(1,),
    operand_batching_dims=(0,),
    start_indices_batching_dims=(0,),
)
SMEM = pl.BlockSpec(memory_space=pltpu.SMEM)
HBM = pl.BlockSpec(memory_space=pltpu.HBM)


def lanes_at(at, size=LANES):
    return pl.ds(pl.multiple_of(at * size, size), size)


def across(left, right):
    return lax.dot_general(
        left, right, (((0,), (0,)), ((), ())), preferred_element_type=jnp.float32
    )


def along(left, right):
    return lax.dot_general(
        left, right, (((1,), (1,)), ((), ())), preferred_element_type=jnp.float32
    )


def matmul(left, right):
    return jnp.dot(left, right, preferred_element_type=jnp.float32)


def take_lanes(rows, index):
    return lax.gather(
        rows, index[..., None], ALONG_LANES, (1, 1), mode=lax.GatherScatterMode.PROMISE_IN_BOUNDS
    )


def find(load, high, low, chunks, parts):
    bits = [lax.bitwise_and(high, jnp.int16(1 << b)) != jnp.int16(0) for b in range(5)]

    def among(start, size, bit):
        if size == 1:
            return [take_lanes(load(start, v), low) for v in range(parts)]
        first = among(start, size // 2, bit - 1)
        last = among(start + size // 2, size // 2, bit - 1)
        return [jnp.where(bits[bit], q, p) for p, q in zip(first, last)]

    return among(0, chunks, chunks.bit_length() - 2)


def aggregate_kernel(feat_ref, adj_ref, count_ref, owner_ref, out_ref, index, counts, rows, places, stage, wide):
    width, inputs = feat_ref.shape
    nodes = owner_ref.shape[1]
    owners = out_ref.shape[0]
    fan = adj_ref.shape[0] - 1
    chunks = inputs // LANES
    groups = nodes // LANES
    parts = width // 16
    steps = (fan + 1) // 4
    i16, i32, bf16, f32 = jnp.int16, jnp.int32, jnp.bfloat16, jnp.float32
    span = 256
    before = (
        lax.broadcasted_iota(i32, (span, span), 0) < lax.broadcasted_iota(i32, (span, span), 1)
    ).astype(bf16)

    def ones(hit, axis):
        return jnp.sum(jnp.where(hit, 1.0, 0.0), axis=axis, keepdims=True)

    kinds = lax.broadcasted_iota(i32, (16, span), 0)
    blocks = [slice(b * span, (b + 1) * span) for b in range(nodes // span)]
    start = jnp.zeros((16, 1), f32)
    for at in blocks:
        start = start + ones(fan - count_ref[:, at] < kinds, 1)
    order, seen = [], start
    for at in blocks:
        hit = fan - count_ref[:, at] == kinds
        earlier = matmul(hit.astype(bf16), before) + seen
        order.append(jnp.sum(jnp.where(hit, earlier, 0.0), axis=0, keepdims=True).astype(i32))
        seen = seen + ones(hit, 1)
    node_at = jnp.zeros((2 * groups, LANES), f32)
    group_ids = lax.broadcasted_iota(i32, (groups, span), 0)
    lane_ids = lax.broadcasted_iota(i32, (LANES, span), 0)
    for b, place in enumerate(order):
        node = lax.broadcasted_iota(i32, (groups, span), 1) + b * span
        mine = group_ids == lax.shift_right_logical(place, 7)
        weights = jnp.concatenate(
            [
                jnp.where(mine, lax.shift_right_logical(node, 7), 0).astype(f32),
                jnp.where(mine, lax.bitwise_and(node, LANES - 1), 0).astype(f32),
            ],
            axis=0,
        ).astype(bf16)
        picked = (lane_ids == lax.bitwise_and(place, LANES - 1)).astype(bf16)
        node_at = node_at + along(weights, picked)
    node_at = node_at.astype(i32)
    for g in range(groups):
        high = jnp.broadcast_to(node_at[g : g + 1], (16, LANES)).astype(i16)
        low = jnp.broadcast_to(node_at[groups + g : groups + g + 1], (16, LANES)).astype(i16)
        (columns,) = find(
            lambda c, v: adj_ref[:, c * LANES : (c + 1) * LANES].astype(i16), high, low, groups, 1
        )
        columns = columns.astype(i32)
        for s in range(steps):
            index[g * steps + s, 0:4] = columns[s * 4 : s * 4 + 4]
        place = lax.broadcasted_iota(i32, (16, LANES), 1) + g * LANES
        counts[g] = (fan + 1) - ones(start.astype(i32) <= place, 0).astype(i32)

    def one_group(g, carry):
        count = counts[g]

        def four(s, total, first):
            total = list(total)
            for j in range(4):
                at = index[g * steps + s, j : j + 1, :]
                high = jnp.broadcast_to(lax.shift_right_logical(at, 7), (16, LANES)).astype(i16)
                low = jnp.broadcast_to(lax.bitwise_and(at, LANES - 1), (16, LANES)).astype(i16)
                found = find(
                    lambda c, v: feat_ref[v * 16 : (v + 1) * 16, c * LANES : (c + 1) * LANES],
                    high, low, chunks, parts,
                )
                if first and j == 0:
                    for v in range(parts):
                        rows[v * 16 : (v + 1) * 16, lanes_at(g)] = found[v]
                    continue
                valid = jnp.broadcast_to(s * 4 + j <= count, (16, LANES))
                for v in range(parts):
                    total[v] = total[v] + jnp.where(valid, found[v].astype(f32), 0.0)
            return tuple(total)

        total = four(0, (jnp.zeros((16, LANES), f32),) * parts, True)
        needed = lax.shift_right_logical(jnp.max(count) + 4, 2)
        total = lax.fori_loop(1, needed, lambda s, t: four(s, t, False), total)
        divisor = jnp.broadcast_to(count.astype(f32), (16, LANES))
        for v in range(parts):
            near = (total[v] / divisor).astype(bf16)
            rows[width + v * 16 : width + (v + 1) * 16, lanes_at(g)] = near
        return carry

    lax.fori_loop(0, groups, one_group, 0)

    owner_ids = lax.broadcasted_iota(i32, (owners, span), 0)
    ranks = lax.broadcasted_iota(i32, (CAP, span), 0)
    seen = jnp.zeros((owners, 1), f32)
    found_at = jnp.zeros((3 * CAP, owners), f32)
    for at, place in zip(blocks, order):
        hit = owner_ids == owner_ref[:, at]
        picked = hit.astype(bf16)
        earlier = matmul(picked, before) + seen
        rank = jnp.sum(jnp.where(hit, earlier, 0.0), axis=0, keepdims=True).astype(i32)
        seen = seen + ones(hit, 1)
        mine = ranks == rank
        weights = jnp.concatenate(
            [
                jnp.where(mine, lax.shift_right_logical(place, 7), 0).astype(f32),
                jnp.where(mine, lax.bitwise_and(place, LANES - 1), 0).astype(f32),
                jnp.where(mine, 1.0, 0.0),
            ],
            axis=0,
        ).astype(bf16)
        found_at = found_at + along(weights, picked)
    found_at = found_at.astype(i32)
    for q in range(CAP // 4):
        for kind in range(3):
            at = kind * CAP + q * 4
            places[q, kind * 4 : (kind + 1) * 4] = found_at[at : at + 4]

    half = 2 * width

    def four_ranks(q, carry):
        for j in range(4):
            high = jnp.broadcast_to(places[q, j : j + 1, :], (16, owners)).astype(i16)
            low = jnp.broadcast_to(places[q, 4 + j : 5 + j, :], (16, owners)).astype(i16)
            filled = jnp.broadcast_to(places[q, 8 + j : 9 + j, :], (16, owners)) > 0
            found = find(
                lambda c, v: rows[v * 16 : (v + 1) * 16, c * LANES : (c + 1) * LANES],
                high, low, groups, half // 16,
            )
            for v in range(half // 16):
                at = (j % 2) * half + v * 16
                stage[j // 2, at : at + 16, :] = jnp.where(filled, found[v].astype(f32), 0.0)
        for pair in range(2):
            wide[pl.ds(q * 2 + pair, owners, stride=16), :] = stage[pair].T
        return carry

    lax.fori_loop(0, CAP // 4, four_ranks, 0)

    def finish(t, carry):
        at = pl.ds(pl.multiple_of(t * 8, 8), 8)
        out_ref[at] = wide[lanes_at(t), :].astype(bf16).reshape(8, 16, LANES)
        return carry

    lax.fori_loop(0, owners // 8, finish, 0)


def aggregate(features, adjacent, count, owner, owners):
    width, _ = features.shape
    nodes = owner.shape[1]
    return pl.pallas_call(
        aggregate_kernel,
        out_shape=jax.ShapeDtypeStruct((owners, 16, LANES), jnp.bfloat16),
        in_specs=[VMEM] * 4,
        out_specs=VMEM,
        scratch_shapes=[
            pltpu.VMEM((nodes // LANES * 4, 4, LANES), jnp.int32),
            pltpu.VMEM((nodes // LANES, 1, LANES), jnp.int32),
            pltpu.VMEM((2 * width, nodes), jnp.bfloat16),
            pltpu.VMEM((CAP // 4, 12, LANES), jnp.int32),
            pltpu.VMEM((2, 4 * width, owners), jnp.float32),
            pltpu.VMEM((16 * owners, LANES), jnp.float32),
        ],
        name="aggregate",
        compiler_params=pltpu.CompilerParams(vmem_limit_bytes=12 << 20),
        cost_estimate=pl.CostEstimate(flops=40_000_000, bytes_accessed=3_000_000, transcendentals=0),
    )(features, adjacent, count, owner)


def picks_kernel(adj_ref, center_ref, count_ref, out_ref, flip_ref):
    nodes, fan = adj_ref.shape
    slots = out_ref.shape[1]

    def table_row(slot):
        odd = lax.shift_left(lax.bitwise_and(slot, 1), 4)
        pair = lax.bitwise_and(lax.shift_right_logical(slot, 1), 15)
        return lax.bitwise_and(slot, -CAP) + odd + pair

    def one_tile(t, carry):
        at = pl.ds(pl.multiple_of(t * 16, 16), 16)
        number = lax.broadcasted_iota(jnp.int32, (16, fan), 1)
        adjacent = jnp.where(number < count_ref[at, :], table_row(adj_ref[at, :]), -1)
        center = jnp.broadcast_to(table_row(center_ref[at, :]), (16, LANES))
        spread = [jnp.broadcast_to(adjacent[:, k : k + 1], (16, LANES)) for k in range(fan)]
        for c in range(slots // LANES):
            ids = lax.broadcasted_iota(jnp.int32, (16, LANES), 1) + c * LANES
            total = jnp.zeros((16, LANES), jnp.float32)
            for k in range(fan):
                total = total + jnp.where(spread[k] == ids, 1.0, 0.0)
            out_ref[at, c * LANES : (c + 1) * LANES] = jnp.where(center == ids, 1.0, 0.0).astype(
                out_ref.dtype
            )
            low = pl.ds(pl.multiple_of(nodes + t * 16, 16), 16)
            out_ref[low, c * LANES : (c + 1) * LANES] = total.astype(out_ref.dtype)
        return carry

    lax.fori_loop(0, nodes // 16, one_tile, 0)

    def one_flip(t, carry):
        flip_ref[:, lanes_at(t)] = out_ref[lanes_at(t), :].T
        return carry

    lax.fori_loop(0, 2 * nodes // LANES, one_flip, 0)


def picks(adjacent, center, count, slots):
    nodes = adjacent.shape[0]
    return pl.pallas_call(
        picks_kernel,
        out_shape=(
            jax.ShapeDtypeStruct((2 * nodes, slots), jnp.bfloat16),
            jax.ShapeDtypeStruct((slots, 2 * nodes), jnp.bfloat16),
        ),
        in_specs=[VMEM] * 3,
        out_specs=(VMEM, VMEM),
        name="picks",
        compiler_params=pltpu.CompilerParams(vmem_limit_bytes=12 << 20),
        cost_estimate=pl.CostEstimate(flops=20_000_000, bytes_accessed=5_000_000, transcendentals=0),
    )(adjacent, center, count)


def call(kernel, outs, ins, smem=0, hbm=0, scratch=(), limit=16, flops=0, moved=0, exps=0):
    return pl.pallas_call(
        kernel,
        out_shape=outs,
        in_specs=[SMEM] * smem + [VMEM] * (ins - smem - hbm) + [HBM] * hbm,
        out_specs=(VMEM,) * len(outs),
        scratch_shapes=scratch,
        compiler_params=pltpu.CompilerParams(vmem_limit_bytes=limit << 20),
        cost_estimate=pl.CostEstimate(flops=flops, bytes_accessed=moved, transcendentals=exps),
    )


def in_hbm(value):
    return pltpu.with_memory_space_constraint(value, pltpu.HBM)


def put_chunks(to_ref, t, product):
    for c in range(product.shape[0] // 16):
        for lane in range(product.shape[1] // LANES):
            to_ref[t * (product.shape[0] // 16) + c, lane * 16 : (lane + 1) * 16, :] = product[
                c * 16 : (c + 1) * 16, lane * LANES : (lane + 1) * LANES
            ]


def forward_kernel(
    core_ref, z_ref, arrived_ref, pair_ref, other_pair_ref, bias_one_ref, count_ref, bias_two_ref,
    picks_hbm, root_hbm, near_hbm, upstream_hbm, out_ref, sent_ref, hidden, rows, slope,
    inputs_flip, bias_grad, inputs, picks_ref, root_ref, near_ref, upstream_ref, arrivals,
):
    copies = [
        pltpu.make_async_copy(source, target, arrivals.at[number])
        for number, (source, target) in enumerate(
            (
                (picks_hbm, picks_ref),
                (root_hbm, root_ref),
                (near_hbm, near_ref),
                (upstream_hbm, upstream_ref),
            )
        )
    ]
    for copy in copies:
        copy.start()
    slots, depth = inputs.shape
    hidden_width = hidden.shape[1]
    nodes = slope.shape[0]
    quarter = depth // 4
    sources = slots // CAP
    tile = 256

    def one_source(t, carry):
        for e in range(2):
            pieces = [
                arrived_ref[f * sources + t, :, e * quarter : (e + 1) * quarter] for f in range(4)
            ]
            at = pl.ds(pl.multiple_of(t * CAP + e * 16, 16), 16)
            inputs[at, :] = jnp.concatenate(pieces, axis=1)
        return carry

    lax.fori_loop(0, sources, one_source, 0)
    for t in range(slots // tile):
        inputs_flip[:, t * tile : (t + 1) * tile] = inputs[t * tile : (t + 1) * tile, :].T

    late = z_ref[0] >= 2

    def first_layer(t, carry):
        cols = lanes_at(t, tile)
        pair, other = pair_ref[:, cols], other_pair_ref[:, cols]
        pre = matmul(inputs[:, : depth // 2], jnp.where(late, other, pair))
        pre = pre + matmul(inputs[:, depth // 2 :], jnp.where(late, pair, other))
        pre = pre + bias_one_ref[:, cols]
        value = jnp.maximum(pre, 0.0) + jnp.log1p(jnp.exp(-jnp.abs(pre)))
        hidden[:, cols] = value.astype(jnp.bfloat16)
        return carry

    lax.fori_loop(0, hidden_width // tile, first_layer, 0)
    inverse = 1.0 / count_ref[...].astype(jnp.float32)
    copies[0].wait()

    def select(t, carry):
        cols = lanes_at(t, tile)
        rows[:nodes, cols] = matmul(picks_ref[:nodes, :], hidden[:, cols]).astype(jnp.bfloat16)
        total = matmul(picks_ref[nodes:, :], hidden[:, cols])
        rows[nodes:, cols] = (total * inverse).astype(jnp.bfloat16)
        return carry

    lax.fori_loop(0, hidden_width // tile, select, 0)
    for copy in copies[1:]:
        copy.wait()

    def second_layer(t, carry):
        cols = lanes_at(t, tile)
        pre = matmul(rows[:nodes, :], root_ref[:, cols]) + matmul(rows[nodes:, :], near_ref[:, cols])
        pre = pre + bias_two_ref[:, cols]
        gate = jax.nn.sigmoid(pre)
        out_ref[:, cols] = (pre * gate).astype(jnp.bfloat16)
        grad = upstream_ref[:, cols].astype(jnp.float32) * gate * (1.0 + pre * (1.0 - gate))
        grad = grad.astype(jnp.bfloat16)
        slope[:, cols] = grad
        bias_grad[0:1, cols] = jnp.sum(grad.astype(jnp.float32), axis=0, keepdims=True)
        return carry

    lax.fori_loop(0, hidden_width // tile, second_layer, 0)
    start = (core_ref[0] ^ 1) * nodes

    def weight_grads(t, carry):
        left = rows[pl.ds(pl.multiple_of(start, nodes), nodes), lanes_at(t, tile)]
        put_chunks(sent_ref, t, across(left, slope[...]).astype(jnp.bfloat16))
        return carry

    lax.fori_loop(0, hidden_width // tile, weight_grads, 0)


def kept_kernel(
    core_ref, rows_ref, slope_ref, received_ref, kept_one_ref, received_one_ref, both_ref
):
    nodes, hidden_width = slope_ref.shape
    tile = 256
    start = core_ref[0] * nodes

    def weight_grads(t, carry):
        left = rows_ref[pl.ds(pl.multiple_of(start, nodes), nodes), lanes_at(t, tile)]
        product = across(left, slope_ref[...])
        for c in range(tile // 16):
            chunk = t * (tile // 16) + c
            for lane in range(hidden_width // LANES):
                at = slice(lane * 16, (lane + 1) * 16)
                mine = product[c * 16 : (c + 1) * 16, lane * LANES : (lane + 1) * LANES]
                other = received_ref[chunk, at, :].astype(jnp.float32)
                both_ref[chunk, at, :] = (mine + other).astype(jnp.bfloat16)
            mine = kept_one_ref[chunk].astype(jnp.float32)
            other = received_one_ref[chunk].astype(jnp.float32)
            both_ref[chunk, LANES:, :] = (mine + other).astype(jnp.bfloat16)
        return carry

    lax.fori_loop(0, hidden_width // tile, weight_grads, 0)


def backward_kernel(
    core_ref, slope_ref, root_ref, near_ref, count_ref, flip_ref, hidden_ref, inputs_flip_ref,
    bias_two_ref, kept_ref, sent_ref, back, bias_grads,
):
    core = core_ref[0]
    nodes, hidden_width = slope_ref.shape
    tile = 256
    bias_grads[0:1, :] = bias_two_ref[0:1, :]
    inverse = 1.0 / count_ref[...].astype(jnp.float32)

    def backward(t, carry):
        cols = lanes_at(t, tile)
        back[:nodes, cols] = along(slope_ref[...], root_ref[cols, :]).astype(jnp.bfloat16)
        near = along(slope_ref[...], near_ref[cols, :])
        back[nodes:, cols] = (near * inverse).astype(jnp.bfloat16)
        return carry

    lax.fori_loop(0, hidden_width // tile, backward, 0)

    def first_grads(t, carry):
        cols = lanes_at(t, tile)
        table_grad = matmul(flip_ref[...], back[:, cols])
        grad = table_grad * (1.0 - jnp.exp(-hidden_ref[:, cols].astype(jnp.float32)))
        grad = grad.astype(jnp.bfloat16)
        bias_grads[1:2, cols] = jnp.sum(grad.astype(jnp.float32), axis=0, keepdims=True)
        for place, to_ref in enumerate((kept_ref, sent_ref)):
            which = core ^ place
            left = inputs_flip_ref[pl.ds(pl.multiple_of(which * LANES, LANES), LANES), :]
            product = matmul(left, grad).astype(jnp.bfloat16)
            for c in range(8):
                for lane in range(tile // LANES):
                    chunk = c * 8 + t * (tile // LANES) + lane
                    to_ref[chunk, 0:16, :] = product[
                        c * 16 : (c + 1) * 16, lane * LANES : (lane + 1) * LANES
                    ]
        return carry

    lax.fori_loop(0, hidden_width // tile, first_grads, 0)
    for place, to_ref in enumerate((kept_ref, sent_ref)):
        which = core ^ place
        to_ref[:, 16:, :] = jnp.zeros((to_ref.shape[0], 8, LANES), jnp.bfloat16)
        for lane in range(8):
            cols = slice(lane * LANES, (lane + 1) * LANES)
            row = jnp.where(which == 0, bias_grads[0:1, cols], bias_grads[1:2, cols])
            to_ref[lane, 16:, :] = jnp.broadcast_to(row, (8, LANES)).astype(jnp.bfloat16)


def shaped(*shape, dtype=jnp.bfloat16):
    return jax.ShapeDtypeStruct(shape, dtype)


def spread_kernel(core_ref, z_ref, kept_ref, other_ref, root_ref, near_ref, first_root_ref, first_near_ref, bias_two_ref, bias_one_ref):
    core, z = core_ref[0], z_ref[0]
    step = pl.program_id(0)
    even = core == 0
    for c in range(8):
        for lane in range(8):
            kept = kept_ref[c, lane * 16 : (lane + 1) * 16, :].astype(jnp.float32)
            other = other_ref[c, lane * 16 : (lane + 1) * 16, :].astype(jnp.float32)
            at, cols = slice(c * 16, (c + 1) * 16), slice(lane * LANES, (lane + 1) * LANES)
            root_ref[at, cols] = jnp.where(even, kept, other)
            near_ref[at, cols] = jnp.where(even, other, kept)

    here = lax.shift_right_logical(z, 1) == core
    base = lax.bitwise_and(z, 1) * 4
    for j, to_ref in enumerate((first_root_ref, first_near_ref)):
        for i in range(2):

            @pl.when(step == base + 2 * j + i)
            def _(to_ref=to_ref, i=i):
                for lane in range(8):
                    kept = kept_ref[lane, LANES : LANES + 16, :].astype(jnp.float32)
                    other = other_ref[lane, LANES : LANES + 16, :].astype(jnp.float32)
                    at, cols = slice(i * 16, (i + 1) * 16), slice(lane * LANES, (lane + 1) * LANES)
                    to_ref[at, cols] = jnp.where(here, kept, other)

    @pl.when(step == 0)
    def _():
        for lane in range(8):
            kept = kept_ref[lane, LANES + 16 :, :].astype(jnp.float32)[0:1, :]
            other = other_ref[lane, LANES + 16 :, :].astype(jnp.float32)[0:1, :]
            cols = slice(lane * LANES, (lane + 1) * LANES)
            bias_two_ref[:, cols] = jnp.where(even, kept, other)
            bias_one_ref[:, cols] = jnp.where(even, other, kept)


def spread(core, z, kept, other, hidden_width):
    f32 = jnp.float32
    wide = pl.BlockSpec((LANES, hidden_width), lambda s: (s, 0))
    slab = pl.BlockSpec((32, hidden_width), lambda s: (0, 0))
    line = pl.BlockSpec((1, hidden_width), lambda s: (0, 0))
    block = pl.BlockSpec((8, CHUNK, LANES), lambda s: (s, 0, 0))
    return pl.pallas_call(
        spread_kernel,
        grid=(8,),
        out_shape=(
            shaped(hidden_width, hidden_width, dtype=f32),
            shaped(hidden_width, hidden_width, dtype=f32),
            shaped(32, hidden_width, dtype=f32),
            shaped(32, hidden_width, dtype=f32),
            shaped(1, hidden_width, dtype=f32),
            shaped(1, hidden_width, dtype=f32),
        ),
        in_specs=[SMEM, SMEM, block, block],
        out_specs=(wide, wide, slab, slab, line, line),
        name="spread",
        compiler_params=pltpu.CompilerParams(vmem_limit_bytes=16 << 20),
    )(core, z, kept, other)


def weights_of_pair(own, z):
    first = lax.ppermute(own, "z", [(0, 1), (1, 0), (2, 3), (3, 2)])
    odd = lax.bitwise_and(z, 1) == 1
    return jnp.concatenate([jnp.where(odd, first, own), jnp.where(odd, own, first)], axis=0)


def weights_of_others(pair):
    return lax.ppermute(pair, "z", [(0, 3), (3, 0), (1, 2), (2, 1)])


def exchange(value, axes):
    return lax.all_to_all(value, axes, split_axis=0, concat_axis=0, tiled=True)


def step(
    features,
    first_adjacent,
    first_center,
    first_count,
    owner_map,
    first_root,
    first_near,
    first_bias,
    second_adjacent,
    second_center,
    second_count,
    second_root,
    second_near,
    second_bias,
    upstream,
):
    owners = 128
    hidden_width = first_root.shape[1]
    z = lax.axis_index("z")
    core = lax.axis_index("core")[None]
    pair = weights_of_pair(jnp.concatenate([first_root, first_near], axis=0), z)
    columns = jnp.concatenate([first_center[:, None], first_adjacent], axis=1).T
    packed = aggregate(features, columns, first_count[None], owner_map[None], owners)
    packed, pair = lax.optimization_barrier((packed, pair))
    other_pair = weights_of_others(pair)
    arrived = exchange(packed, AXES)
    count = second_count[:, None]
    picked, flipped = picks(second_adjacent, second_center[:, None], count, owners * 8)
    slots, depth = picked.shape[1], 2 * pair.shape[0]
    nodes = upstream.shape[0]
    layer_output, sent_two, hidden, rows, slope, inputs_flip, bias_grad = call(
        forward_kernel,
        (
            shaped(nodes, hidden_width),
            shaped(64, LANES, LANES),
            shaped(slots, hidden_width),
            shaped(2 * nodes, hidden_width),
            shaped(nodes, hidden_width),
            shaped(depth, slots),
            shaped(8, hidden_width, dtype=jnp.float32),
        ),
        12,
        smem=2,
        hbm=4,
        scratch=[
            pltpu.VMEM((slots, depth), jnp.bfloat16),
            pltpu.VMEM(picked.shape, jnp.bfloat16),
            pltpu.VMEM(second_root.shape, jnp.bfloat16),
            pltpu.VMEM(second_near.shape, jnp.bfloat16),
            pltpu.VMEM(upstream.shape, jnp.bfloat16),
            pltpu.SemaphoreType.DMA((4,)),
        ],
        limit=24,
        flops=6_000_000_000,
        moved=18_000_000,
        exps=3_000_000,
    )(
        core, z[None], arrived, pair, other_pair, first_bias[None], count, second_bias[None],
        in_hbm(picked), in_hbm(second_root), in_hbm(second_near), in_hbm(upstream),
    )
    received = lax.ppermute(sent_two, "core", [(0, 1), (1, 0)])
    kept_one, sent_one = call(
        backward_kernel, (shaped(64, 24, LANES), shaped(64, 24, LANES)), 9, smem=1,
        scratch=[
            pltpu.VMEM((2 * nodes, hidden_width), jnp.bfloat16),
            pltpu.VMEM((8, hidden_width), jnp.float32),
        ],
        limit=24, flops=4_700_000_000, moved=12_000_000, exps=1_000_000,
    )(core, slope, second_root, second_near, count, flipped, hidden, inputs_flip, bias_grad)
    received_one = lax.ppermute(sent_one, "core", [(0, 1), (1, 0)])
    (both,) = call(
        kept_kernel, (shaped(64, CHUNK, LANES),), 6, smem=1, limit=20,
        flops=1_000_000_000, moved=7_000_000,
    )(core, rows, slope, received, kept_one, received_one)
    terms = exchange(both, CHIPS)
    total = jnp.sum(terms.astype(jnp.float32), axis=0).astype(jnp.bfloat16)
    mine = exchange(jnp.broadcast_to(total[None], terms.shape), CHIPS)
    other = lax.ppermute(mine, "core", [(0, 1), (1, 0)])
    root_two, near_two, root_one, near_one, bias_two, bias_one = spread(
        core, z[None], mine, other, hidden_width
    )
    return (layer_output, root_two, near_two, bias_two[0], root_one, near_one, bias_one[0])


def solution(mesh):
    chips = Mesh(mesh.devices.reshape(4, 4, 4, 2), AXES)
    trainer = ("x", "y", "core")
    return jax.shard_map(
        step,
        mesh=chips,
        in_specs=(
            P("z", trainer),
            P(trainer, None),
            P(trainer),
            P(trainer),
            P(trainer),
            P("z", None),
            P("z", None),
            P(),
            P(AXES, None),
            P(AXES),
            P(AXES),
            P(),
            P(),
            P(),
            P(AXES, None),
        ),
        out_specs=(
            P(AXES, None),
            P(),
            P(),
            P(),
            P("z", None),
            P("z", None),
            P(),
        ),
        check_vma=False,
    )
```

```python
import jax
import jax.numpy as jnp
from jax import lax
from jax.experimental import pallas as pl
from jax.experimental.pallas import tpu as pltpu
from jax.sharding import Mesh, PartitionSpec as P


CAP = 32
LANES = 128
AXES = ("z", "x", "y", "core")
CHIPS = ("z", "x", "y")
CHUNK = 152
VMEM = pl.BlockSpec(memory_space=pltpu.VMEM)
ALONG_LANES = lax.GatherDimensionNumbers(
    offset_dims=(),
    collapsed_slice_dims=(1,),
    start_index_map=(1,),
    operand_batching_dims=(0,),
    start_indices_batching_dims=(0,),
)
SMEM = pl.BlockSpec(memory_space=pltpu.SMEM)
HBM = pl.BlockSpec(memory_space=pltpu.HBM)


def lanes_at(at, size=LANES):
    return pl.ds(pl.multiple_of(at * size, size), size)


def across(left, right):
    return lax.dot_general(
        left, right, (((0,), (0,)), ((), ())), preferred_element_type=jnp.float32
    )


def along(left, right):
    return lax.dot_general(
        left, right, (((1,), (1,)), ((), ())), preferred_element_type=jnp.float32
    )


def matmul(left, right):
    return jnp.dot(left, right, preferred_element_type=jnp.float32)


def take_lanes(rows, index):
    return lax.gather(
        rows, index[..., None], ALONG_LANES, (1, 1), mode=lax.GatherScatterMode.PROMISE_IN_BOUNDS
    )


def find(load, high, low, chunks, parts):
    bits = [lax.bitwise_and(high, jnp.int16(1 << b)) != jnp.int16(0) for b in range(5)]

    def among(start, size, bit):
        if size == 1:
            return [take_lanes(load(start, v), low) for v in range(parts)]
        first = among(start, size // 2, bit - 1)
        last = among(start + size // 2, size // 2, bit - 1)
        return [jnp.where(bits[bit], q, p) for p, q in zip(first, last)]

    return among(0, chunks, chunks.bit_length() - 2)


def aggregate_kernel(
    adj_ref, feat_hbm, count_hbm, owner_hbm, out_ref, index, counts, rows, places, stage, wide,
    feat_ref, count_ref, owner_ref, arrivals,
):
    copies = [
        pltpu.make_async_copy(source, target, arrivals.at[number])
        for number, (source, target) in enumerate(
            ((count_hbm, count_ref), (owner_hbm, owner_ref), (feat_hbm, feat_ref))
        )
    ]
    for copy in copies:
        copy.start()
    copies[0].wait()
    width, inputs = feat_ref.shape
    nodes = owner_ref.shape[1]
    owners = out_ref.shape[0]
    fan = adj_ref.shape[0] - 1
    chunks = inputs // LANES
    groups = nodes // LANES
    parts = width // 16
    steps = (fan + 1) // 4
    i16, i32, bf16, f32 = jnp.int16, jnp.int32, jnp.bfloat16, jnp.float32
    span = 256
    before = (
        lax.broadcasted_iota(i32, (span, span), 0) < lax.broadcasted_iota(i32, (span, span), 1)
    ).astype(bf16)

    def ones(hit, axis):
        return jnp.sum(jnp.where(hit, 1.0, 0.0), axis=axis, keepdims=True)

    kinds = lax.broadcasted_iota(i32, (16, span), 0)
    blocks = [slice(b * span, (b + 1) * span) for b in range(nodes // span)]
    start = jnp.zeros((16, 1), f32)
    for at in blocks:
        start = start + ones(fan - count_ref[:, at] < kinds, 1)
    order, seen = [], start
    for at in blocks:
        hit = fan - count_ref[:, at] == kinds
        earlier = matmul(hit.astype(bf16), before) + seen
        order.append(jnp.sum(jnp.where(hit, earlier, 0.0), axis=0, keepdims=True).astype(i32))
        seen = seen + ones(hit, 1)
    node_at = jnp.zeros((2 * groups, LANES), f32)
    group_ids = lax.broadcasted_iota(i32, (groups, span), 0)
    lane_ids = lax.broadcasted_iota(i32, (LANES, span), 0)
    for b, place in enumerate(order):
        node = lax.broadcasted_iota(i32, (groups, span), 1) + b * span
        mine = group_ids == lax.shift_right_logical(place, 7)
        weights = jnp.concatenate(
            [
                jnp.where(mine, lax.shift_right_logical(node, 7), 0).astype(f32),
                jnp.where(mine, lax.bitwise_and(node, LANES - 1), 0).astype(f32),
            ],
            axis=0,
        ).astype(bf16)
        picked = (lane_ids == lax.bitwise_and(place, LANES - 1)).astype(bf16)
        node_at = node_at + along(weights, picked)
    node_at = node_at.astype(i32)
    for g in range(groups):
        high = jnp.broadcast_to(node_at[g : g + 1], (16, LANES)).astype(i16)
        low = jnp.broadcast_to(node_at[groups + g : groups + g + 1], (16, LANES)).astype(i16)
        (columns,) = find(
            lambda c, v: adj_ref[:, c * LANES : (c + 1) * LANES].astype(i16), high, low, groups, 1
        )
        columns = columns.astype(i32)
        for s in range(steps):
            index[g * steps + s, 0:4] = columns[s * 4 : s * 4 + 4]
        place = lax.broadcasted_iota(i32, (16, LANES), 1) + g * LANES
        counts[g] = (fan + 1) - ones(start.astype(i32) <= place, 0).astype(i32)

    copies[1].wait()
    copies[2].wait()

    def one_group(g, carry):
        count = counts[g]

        def four(s, total, first):
            total = list(total)
            for j in range(4):
                at = index[g * steps + s, j : j + 1, :]
                high = jnp.broadcast_to(lax.shift_right_logical(at, 7), (16, LANES)).astype(i16)
                low = jnp.broadcast_to(lax.bitwise_and(at, LANES - 1), (16, LANES)).astype(i16)
                found = find(
                    lambda c, v: feat_ref[v * 16 : (v + 1) * 16, c * LANES : (c + 1) * LANES],
                    high, low, chunks, parts,
                )
                if first and j == 0:
                    for v in range(parts):
                        rows[v * 16 : (v + 1) * 16, lanes_at(g)] = found[v]
                    continue
                valid = jnp.broadcast_to(s * 4 + j <= count, (16, LANES))
                for v in range(parts):
                    total[v] = total[v] + jnp.where(valid, found[v].astype(f32), 0.0)
            return tuple(total)

        total = four(0, (jnp.zeros((16, LANES), f32),) * parts, True)
        needed = lax.shift_right_logical(jnp.max(count) + 4, 2)
        total = lax.fori_loop(1, needed, lambda s, t: four(s, t, False), total)
        divisor = jnp.broadcast_to(count.astype(f32), (16, LANES))
        for v in range(parts):
            near = (total[v] / divisor).astype(bf16)
            rows[width + v * 16 : width + (v + 1) * 16, lanes_at(g)] = near
        return carry

    lax.fori_loop(0, groups, one_group, 0)

    owner_ids = lax.broadcasted_iota(i32, (owners, span), 0)
    ranks = lax.broadcasted_iota(i32, (CAP, span), 0)
    seen = jnp.zeros((owners, 1), f32)
    found_at = jnp.zeros((3 * CAP, owners), f32)
    for at, place in zip(blocks, order):
        hit = owner_ids == owner_ref[:, at]
        picked = hit.astype(bf16)
        earlier = matmul(picked, before) + seen
        rank = jnp.sum(jnp.where(hit, earlier, 0.0), axis=0, keepdims=True).astype(i32)
        seen = seen + ones(hit, 1)
        mine = ranks == rank
        weights = jnp.concatenate(
            [
                jnp.where(mine, lax.shift_right_logical(place, 7), 0).astype(f32),
                jnp.where(mine, lax.bitwise_and(place, LANES - 1), 0).astype(f32),
                jnp.where(mine, 1.0, 0.0),
            ],
            axis=0,
        ).astype(bf16)
        found_at = found_at + along(weights, picked)
    found_at = found_at.astype(i32)
    for q in range(CAP // 4):
        for kind in range(3):
            at = kind * CAP + q * 4
            places[q, kind * 4 : (kind + 1) * 4] = found_at[at : at + 4]

    half = 2 * width

    def four_ranks(q, carry):
        for j in range(4):
            high = jnp.broadcast_to(places[q, j : j + 1, :], (16, owners)).astype(i16)
            low = jnp.broadcast_to(places[q, 4 + j : 5 + j, :], (16, owners)).astype(i16)
            filled = jnp.broadcast_to(places[q, 8 + j : 9 + j, :], (16, owners)) > 0
            found = find(
                lambda c, v: rows[v * 16 : (v + 1) * 16, c * LANES : (c + 1) * LANES],
                high, low, groups, half // 16,
            )
            for v in range(half // 16):
                at = (j % 2) * half + v * 16
                stage[j // 2, at : at + 16, :] = jnp.where(filled, found[v].astype(f32), 0.0)
        for pair in range(2):
            wide[pl.ds(q * 2 + pair, owners, stride=16), :] = stage[pair].T
        return carry

    lax.fori_loop(0, CAP // 4, four_ranks, 0)

    def finish(t, carry):
        at = pl.ds(pl.multiple_of(t * 8, 8), 8)
        out_ref[at] = wide[lanes_at(t), :].astype(bf16).reshape(8, 16, LANES)
        return carry

    lax.fori_loop(0, owners // 8, finish, 0)


def aggregate(features, adjacent, count, owner, owners):
    width, _ = features.shape
    nodes = owner.shape[1]
    return pl.pallas_call(
        aggregate_kernel,
        out_shape=jax.ShapeDtypeStruct((owners, 16, LANES), jnp.bfloat16),
        in_specs=[VMEM] + [HBM] * 3,
        out_specs=VMEM,
        scratch_shapes=[
            pltpu.VMEM((nodes // LANES * 4, 4, LANES), jnp.int32),
            pltpu.VMEM((nodes // LANES, 1, LANES), jnp.int32),
            pltpu.VMEM((2 * width, nodes), jnp.bfloat16),
            pltpu.VMEM((CAP // 4, 12, LANES), jnp.int32),
            pltpu.VMEM((2, 4 * width, owners), jnp.float32),
            pltpu.VMEM((16 * owners, LANES), jnp.float32),
            pltpu.VMEM(features.shape, jnp.bfloat16),
            pltpu.VMEM(count.shape, jnp.int32),
            pltpu.VMEM(owner.shape, jnp.int32),
            pltpu.SemaphoreType.DMA((3,)),
        ],
        name="aggregate",
        compiler_params=pltpu.CompilerParams(vmem_limit_bytes=12 << 20),
        cost_estimate=pl.CostEstimate(flops=40_000_000, bytes_accessed=3_000_000, transcendentals=0),
    )(adjacent, in_hbm(features), in_hbm(count), in_hbm(owner))


def picks_kernel(adj_ref, center_ref, count_ref, out_ref, flip_ref):
    nodes, fan = adj_ref.shape
    slots = out_ref.shape[1]

    def table_row(slot):
        odd = lax.shift_left(lax.bitwise_and(slot, 1), 4)
        pair = lax.bitwise_and(lax.shift_right_logical(slot, 1), 15)
        return lax.bitwise_and(slot, -CAP) + odd + pair

    def one_tile(t, carry):
        at = pl.ds(pl.multiple_of(t * 16, 16), 16)
        number = lax.broadcasted_iota(jnp.int32, (16, fan), 1)
        adjacent = jnp.where(number < count_ref[at, :], table_row(adj_ref[at, :]), -1)
        center = jnp.broadcast_to(table_row(center_ref[at, :]), (16, LANES))
        spread = [jnp.broadcast_to(adjacent[:, k : k + 1], (16, LANES)) for k in range(fan)]
        for c in range(slots // LANES):
            ids = lax.broadcasted_iota(jnp.int32, (16, LANES), 1) + c * LANES
            total = jnp.zeros((16, LANES), jnp.float32)
            for k in range(fan):
                total = total + jnp.where(spread[k] == ids, 1.0, 0.0)
            out_ref[at, c * LANES : (c + 1) * LANES] = jnp.where(center == ids, 1.0, 0.0).astype(
                out_ref.dtype
            )
            low = pl.ds(pl.multiple_of(nodes + t * 16, 16), 16)
            out_ref[low, c * LANES : (c + 1) * LANES] = total.astype(out_ref.dtype)
        return carry

    lax.fori_loop(0, nodes // 16, one_tile, 0)

    def one_flip(t, carry):
        flip_ref[:, lanes_at(t)] = out_ref[lanes_at(t), :].T
        return carry

    lax.fori_loop(0, 2 * nodes // LANES, one_flip, 0)


def picks(adjacent, center, count, slots):
    nodes = adjacent.shape[0]
    return pl.pallas_call(
        picks_kernel,
        out_shape=(
            jax.ShapeDtypeStruct((2 * nodes, slots), jnp.bfloat16),
            jax.ShapeDtypeStruct((slots, 2 * nodes), jnp.bfloat16),
        ),
        in_specs=[VMEM] * 3,
        out_specs=(VMEM, VMEM),
        name="picks",
        compiler_params=pltpu.CompilerParams(vmem_limit_bytes=12 << 20),
        cost_estimate=pl.CostEstimate(flops=20_000_000, bytes_accessed=5_000_000, transcendentals=0),
    )(adjacent, center, count)


def call(kernel, outs, ins, smem=0, hbm=0, scratch=(), limit=16, flops=0, moved=0, exps=0):
    return pl.pallas_call(
        kernel,
        out_shape=outs,
        in_specs=[SMEM] * smem + [VMEM] * (ins - smem - hbm) + [HBM] * hbm,
        out_specs=(VMEM,) * len(outs),
        scratch_shapes=scratch,
        compiler_params=pltpu.CompilerParams(vmem_limit_bytes=limit << 20),
        cost_estimate=pl.CostEstimate(flops=flops, bytes_accessed=moved, transcendentals=exps),
    )


def in_hbm(value):
    return pltpu.with_memory_space_constraint(value, pltpu.HBM)


def put_chunks(to_ref, t, product):
    for c in range(product.shape[0] // 16):
        for lane in range(product.shape[1] // LANES):
            to_ref[t * (product.shape[0] // 16) + c, lane * 16 : (lane + 1) * 16, :] = product[
                c * 16 : (c + 1) * 16, lane * LANES : (lane + 1) * LANES
            ]


def forward_kernel(
    core_ref, z_ref, arrived_ref, pair_ref, other_pair_ref, bias_one_ref, count_ref, bias_two_ref,
    picks_hbm, root_hbm, near_hbm, upstream_hbm, out_ref, sent_ref, hidden, rows, slope,
    inputs_flip, bias_grad, inputs, picks_ref, root_ref, near_ref, upstream_ref, arrivals,
):
    copies = [
        pltpu.make_async_copy(source, target, arrivals.at[number])
        for number, (source, target) in enumerate(
            (
                (picks_hbm, picks_ref),
                (root_hbm, root_ref),
                (near_hbm, near_ref),
                (upstream_hbm, upstream_ref),
            )
        )
    ]
    for copy in copies:
        copy.start()
    slots, depth = inputs.shape
    hidden_width = hidden.shape[1]
    nodes = slope.shape[0]
    quarter = depth // 4
    sources = slots // CAP
    tile = 256

    def one_source(t, carry):
        for e in range(2):
            pieces = [
                arrived_ref[f * sources + t, :, e * quarter : (e + 1) * quarter] for f in range(4)
            ]
            at = pl.ds(pl.multiple_of(t * CAP + e * 16, 16), 16)
            inputs[at, :] = jnp.concatenate(pieces, axis=1)
        return carry

    lax.fori_loop(0, sources, one_source, 0)
    for t in range(slots // tile):
        inputs_flip[:, t * tile : (t + 1) * tile] = inputs[t * tile : (t + 1) * tile, :].T

    late = z_ref[0] >= 2

    def first_layer(t, carry):
        cols = lanes_at(t, tile)
        pair, other = pair_ref[:, cols], other_pair_ref[:, cols]
        pre = matmul(inputs[:, : depth // 2], jnp.where(late, other, pair))
        pre = pre + matmul(inputs[:, depth // 2 :], jnp.where(late, pair, other))
        pre = pre + bias_one_ref[:, cols]
        value = jnp.maximum(pre, 0.0) + jnp.log1p(jnp.exp(-jnp.abs(pre)))
        hidden[:, cols] = value.astype(jnp.bfloat16)
        return carry

    lax.fori_loop(0, hidden_width // tile, first_layer, 0)
    inverse = 1.0 / count_ref[...].astype(jnp.float32)
    copies[0].wait()

    def select(t, carry):
        cols = lanes_at(t, tile)
        rows[:nodes, cols] = matmul(picks_ref[:nodes, :], hidden[:, cols]).astype(jnp.bfloat16)
        total = matmul(picks_ref[nodes:, :], hidden[:, cols])
        rows[nodes:, cols] = (total * inverse).astype(jnp.bfloat16)
        return carry

    lax.fori_loop(0, hidden_width // tile, select, 0)
    for copy in copies[1:]:
        copy.wait()

    def second_layer(t, carry):
        cols = lanes_at(t, tile)
        pre = matmul(rows[:nodes, :], root_ref[:, cols]) + matmul(rows[nodes:, :], near_ref[:, cols])
        pre = pre + bias_two_ref[:, cols]
        gate = jax.nn.sigmoid(pre)
        out_ref[:, cols] = (pre * gate).astype(jnp.bfloat16)
        grad = upstream_ref[:, cols].astype(jnp.float32) * gate * (1.0 + pre * (1.0 - gate))
        grad = grad.astype(jnp.bfloat16)
        slope[:, cols] = grad
        bias_grad[0:1, cols] = jnp.sum(grad.astype(jnp.float32), axis=0, keepdims=True)
        return carry

    lax.fori_loop(0, hidden_width // tile, second_layer, 0)
    start = (core_ref[0] ^ 1) * nodes

    def weight_grads(t, carry):
        left = rows[pl.ds(pl.multiple_of(start, nodes), nodes), lanes_at(t, tile)]
        put_chunks(sent_ref, t, across(left, slope[...]).astype(jnp.bfloat16))
        return carry

    lax.fori_loop(0, hidden_width // tile, weight_grads, 0)


def kept_kernel(
    core_ref, rows_ref, slope_ref, received_ref, kept_one_ref, received_one_ref, both_ref
):
    nodes, hidden_width = slope_ref.shape
    tile = 256
    start = core_ref[0] * nodes

    def weight_grads(t, carry):
        left = rows_ref[pl.ds(pl.multiple_of(start, nodes), nodes), lanes_at(t, tile)]
        product = across(left, slope_ref[...])
        for c in range(tile // 16):
            chunk = t * (tile // 16) + c
            for lane in range(hidden_width // LANES):
                at = slice(lane * 16, (lane + 1) * 16)
                mine = product[c * 16 : (c + 1) * 16, lane * LANES : (lane + 1) * LANES]
                other = received_ref[chunk, at, :].astype(jnp.float32)
                both_ref[chunk, at, :] = (mine + other).astype(jnp.bfloat16)
            mine = kept_one_ref[chunk].astype(jnp.float32)
            other = received_one_ref[chunk].astype(jnp.float32)
            both_ref[chunk, LANES:, :] = (mine + other).astype(jnp.bfloat16)
        return carry

    lax.fori_loop(0, hidden_width // tile, weight_grads, 0)


def backward_kernel(
    core_ref, slope_ref, root_ref, near_ref, count_ref, flip_ref, hidden_ref, inputs_flip_ref,
    bias_two_ref, kept_ref, sent_ref, back, bias_grads,
):
    core = core_ref[0]
    nodes, hidden_width = slope_ref.shape
    tile = 256
    bias_grads[0:1, :] = bias_two_ref[0:1, :]
    inverse = 1.0 / count_ref[...].astype(jnp.float32)

    def backward(t, carry):
        cols = lanes_at(t, tile)
        back[:nodes, cols] = along(slope_ref[...], root_ref[cols, :]).astype(jnp.bfloat16)
        near = along(slope_ref[...], near_ref[cols, :])
        back[nodes:, cols] = (near * inverse).astype(jnp.bfloat16)
        return carry

    lax.fori_loop(0, hidden_width // tile, backward, 0)

    def first_grads(t, carry):
        cols = lanes_at(t, tile)
        table_grad = matmul(flip_ref[...], back[:, cols])
        grad = table_grad * (1.0 - jnp.exp(-hidden_ref[:, cols].astype(jnp.float32)))
        grad = grad.astype(jnp.bfloat16)
        bias_grads[1:2, cols] = jnp.sum(grad.astype(jnp.float32), axis=0, keepdims=True)
        for place, to_ref in enumerate((kept_ref, sent_ref)):
            which = core ^ place
            left = inputs_flip_ref[pl.ds(pl.multiple_of(which * LANES, LANES), LANES), :]
            product = matmul(left, grad).astype(jnp.bfloat16)
            for c in range(8):
                for lane in range(tile // LANES):
                    chunk = c * 8 + t * (tile // LANES) + lane
                    to_ref[chunk, 0:16, :] = product[
                        c * 16 : (c + 1) * 16, lane * LANES : (lane + 1) * LANES
                    ]
        return carry

    lax.fori_loop(0, hidden_width // tile, first_grads, 0)
    for place, to_ref in enumerate((kept_ref, sent_ref)):
        which = core ^ place
        to_ref[:, 16:, :] = jnp.zeros((to_ref.shape[0], 8, LANES), jnp.bfloat16)
        for lane in range(8):
            cols = slice(lane * LANES, (lane + 1) * LANES)
            row = jnp.where(which == 0, bias_grads[0:1, cols], bias_grads[1:2, cols])
            to_ref[lane, 16:, :] = jnp.broadcast_to(row, (8, LANES)).astype(jnp.bfloat16)


def shaped(*shape, dtype=jnp.bfloat16):
    return jax.ShapeDtypeStruct(shape, dtype)


def widen(from_ref, wide, root_hbm, near_hbm, to_root, sent):
    tiles = wide.shape[0] // LANES

    def copy(t, target):
        return pltpu.make_async_copy(wide.at[lanes_at(t)], target.at[lanes_at(t)], sent.at[t])

    def one_tile(t, carry):
        for c in range(8):
            at = pl.ds(pl.multiple_of(t * LANES + c * 16, 16), 16)
            for lane in range(8):
                piece = from_ref[t * 8 + c, lane * 16 : (lane + 1) * 16, :]
                wide[at, lane * LANES : (lane + 1) * LANES] = piece.astype(jnp.float32)

        @pl.when(to_root)
        def _():
            copy(t, root_hbm).start()

        @pl.when(jnp.logical_not(to_root))
        def _():
            copy(t, near_hbm).start()

        return carry

    lax.fori_loop(0, tiles, one_tile, 0)

    def finish():
        @pl.when(to_root)
        def _():
            for t in range(tiles):
                copy(t, root_hbm).wait()

        @pl.when(jnp.logical_not(to_root))
        def _():
            for t in range(tiles):
                copy(t, near_hbm).wait()

    return finish


def own_half_kernel(core_ref, kept_ref, root_hbm, near_hbm, wide, sent):
    widen(kept_ref, wide, root_hbm, near_hbm, core_ref[0] == 0, sent)()


def other_half_kernel(
    core_ref, z_ref, kept_ref, other_ref, root_in, near_in, root_hbm, near_hbm, first_root_ref,
    first_near_ref, bias_two_ref, bias_one_ref, wide, sent,
):
    del root_in, near_in
    core, z = core_ref[0], z_ref[0]
    even = core == 0
    finish = widen(other_ref, wide, root_hbm, near_hbm, core != 0, sent)
    here = lax.shift_right_logical(z, 1) == core
    base = lax.bitwise_and(z, 1) * 4
    for j, to_ref in enumerate((first_root_ref, first_near_ref)):
        for i in range(2):
            for lane in range(8):
                chunk = (base + 2 * j + i) * 8 + lane
                kept = kept_ref[chunk, LANES : LANES + 16, :].astype(jnp.float32)
                other = other_ref[chunk, LANES : LANES + 16, :].astype(jnp.float32)
                at, cols = slice(i * 16, (i + 1) * 16), slice(lane * LANES, (lane + 1) * LANES)
                to_ref[at, cols] = jnp.where(here, kept, other)
    for lane in range(8):
        kept = kept_ref[lane, LANES + 16 :, :].astype(jnp.float32)[0:1, :]
        other = other_ref[lane, LANES + 16 :, :].astype(jnp.float32)[0:1, :]
        cols = slice(lane * LANES, (lane + 1) * LANES)
        bias_two_ref[:, cols] = jnp.where(even, kept, other)
        bias_one_ref[:, cols] = jnp.where(even, other, kept)
    finish()


def spread(core, z, kept, hidden_width):
    f32 = jnp.float32
    square = shaped(hidden_width, hidden_width, dtype=f32)
    slab = shaped(32, hidden_width, dtype=f32)
    line = shaped(1, hidden_width, dtype=f32)
    scratch = [pltpu.VMEM(square.shape, f32), pltpu.SemaphoreType.DMA((hidden_width // LANES,))]
    other = lax.ppermute(kept, "core", [(0, 1), (1, 0)])
    root, near = pl.pallas_call(
        own_half_kernel,
        out_shape=(square, square),
        in_specs=[SMEM, VMEM],
        out_specs=(HBM, HBM),
        scratch_shapes=scratch,
        name="own_half",
        compiler_params=pltpu.CompilerParams(vmem_limit_bytes=8 << 20),
        cost_estimate=pl.CostEstimate(flops=1_000_000, bytes_accessed=7_000_000, transcendentals=0),
    )(core, kept)
    return pl.pallas_call(
        other_half_kernel,
        out_shape=(square, square, slab, slab, line, line),
        in_specs=[SMEM, SMEM, VMEM, VMEM, HBM, HBM],
        out_specs=(HBM, HBM) + (VMEM,) * 4,
        scratch_shapes=scratch,
        input_output_aliases={4: 0, 5: 1},
        name="other_half",
        compiler_params=pltpu.CompilerParams(vmem_limit_bytes=8 << 20),
        cost_estimate=pl.CostEstimate(flops=1_000_000, bytes_accessed=9_000_000, transcendentals=0),
    )(core, z, kept, other, root, near)


def weights_of_pair(own, z):
    first = lax.ppermute(own, "z", [(0, 1), (1, 0), (2, 3), (3, 2)])
    odd = lax.bitwise_and(z, 1) == 1
    return jnp.concatenate([jnp.where(odd, first, own), jnp.where(odd, own, first)], axis=0)


def weights_of_others(pair):
    return lax.ppermute(pair, "z", [(0, 3), (3, 0), (1, 2), (2, 1)])


def exchange(value, axes):
    return lax.all_to_all(value, axes, split_axis=0, concat_axis=0, tiled=True)


def step(
    features,
    first_adjacent,
    first_center,
    first_count,
    owner_map,
    first_root,
    first_near,
    first_bias,
    second_adjacent,
    second_center,
    second_count,
    second_root,
    second_near,
    second_bias,
    upstream,
):
    owners = 128
    hidden_width = first_root.shape[1]
    z = lax.axis_index("z")
    core = lax.axis_index("core")[None]
    pair = weights_of_pair(jnp.concatenate([first_root, first_near], axis=0), z)
    columns = jnp.concatenate([first_center[:, None], first_adjacent], axis=1).T
    packed = aggregate(features, columns, first_count[None], owner_map[None], owners)
    packed, pair = lax.optimization_barrier((packed, pair))
    other_pair = weights_of_others(pair)
    arrived = exchange(packed, AXES)
    count = second_count[:, None]
    picked, flipped = picks(second_adjacent, second_center[:, None], count, owners * 8)
    slots, depth = picked.shape[1], 2 * pair.shape[0]
    nodes = upstream.shape[0]
    layer_output, sent_two, hidden, rows, slope, inputs_flip, bias_grad = call(
        forward_kernel,
        (
            shaped(nodes, hidden_width),
            shaped(64, LANES, LANES),
            shaped(slots, hidden_width),
            shaped(2 * nodes, hidden_width),
            shaped(nodes, hidden_width),
            shaped(depth, slots),
            shaped(8, hidden_width, dtype=jnp.float32),
        ),
        12,
        smem=2,
        hbm=4,
        scratch=[
            pltpu.VMEM((slots, depth), jnp.bfloat16),
            pltpu.VMEM(picked.shape, jnp.bfloat16),
            pltpu.VMEM(second_root.shape, jnp.bfloat16),
            pltpu.VMEM(second_near.shape, jnp.bfloat16),
            pltpu.VMEM(upstream.shape, jnp.bfloat16),
            pltpu.SemaphoreType.DMA((4,)),
        ],
        limit=24,
        flops=6_000_000_000,
        moved=18_000_000,
        exps=3_000_000,
    )(
        core, z[None], arrived, pair, other_pair, first_bias[None], count, second_bias[None],
        in_hbm(picked), in_hbm(second_root), in_hbm(second_near), in_hbm(upstream),
    )
    received = lax.ppermute(sent_two, "core", [(0, 1), (1, 0)])
    kept_one, sent_one = call(
        backward_kernel, (shaped(64, 24, LANES), shaped(64, 24, LANES)), 9, smem=1,
        scratch=[
            pltpu.VMEM((2 * nodes, hidden_width), jnp.bfloat16),
            pltpu.VMEM((8, hidden_width), jnp.float32),
        ],
        limit=24, flops=4_700_000_000, moved=12_000_000, exps=1_000_000,
    )(core, slope, second_root, second_near, count, flipped, hidden, inputs_flip, bias_grad)
    received_one = lax.ppermute(sent_one, "core", [(0, 1), (1, 0)])
    (both,) = call(
        kept_kernel, (shaped(64, CHUNK, LANES),), 6, smem=1, limit=20,
        flops=1_000_000_000, moved=7_000_000,
    )(core, rows, slope, received, kept_one, received_one)
    terms = exchange(both, CHIPS)
    total = jnp.sum(terms.astype(jnp.float32), axis=0).astype(jnp.bfloat16)
    mine = exchange(jnp.broadcast_to(total[None], terms.shape), CHIPS)
    root_two, near_two, root_one, near_one, bias_two, bias_one = spread(
        core, z[None], mine, hidden_width
    )
    return (layer_output, root_two, near_two, bias_two[0], root_one, near_one, bias_one[0])


def solution(mesh):
    chips = Mesh(mesh.devices.reshape(4, 4, 4, 2), AXES)
    trainer = ("x", "y", "core")
    return jax.shard_map(
        step,
        mesh=chips,
        in_specs=(
            P("z", trainer),
            P(trainer, None),
            P(trainer),
            P(trainer),
            P(trainer),
            P("z", None),
            P("z", None),
            P(),
            P(AXES, None),
            P(AXES),
            P(AXES),
            P(),
            P(),
            P(),
            P(AXES, None),
        ),
        out_specs=(
            P(AXES, None),
            P(),
            P(),
            P(),
            P("z", None),
            P("z", None),
            P(),
        ),
        check_vma=False,
    )
```

```python
import jax
import jax.numpy as jnp
from jax import lax
from jax.experimental import pallas as pl
from jax.experimental.pallas import tpu as pltpu
from jax.sharding import Mesh, PartitionSpec as P


CAP = 32
LANES = 128
AXES = ("z", "x", "y", "core")
CHIPS = ("z", "x", "y")
CHUNK = 152
VMEM = pl.BlockSpec(memory_space=pltpu.VMEM)
ALONG_LANES = lax.GatherDimensionNumbers(
    offset_dims=(),
    collapsed_slice_dims=(1,),
    start_index_map=(1,),
    operand_batching_dims=(0,),
    start_indices_batching_dims=(0,),
)
SMEM = pl.BlockSpec(memory_space=pltpu.SMEM)
HBM = pl.BlockSpec(memory_space=pltpu.HBM)


def lanes_at(at, size=LANES):
    if isinstance(at, int):
        return slice(at * size, (at + 1) * size)
    return pl.ds(pl.multiple_of(at * size, size), size)


def across(left, right):
    return lax.dot_general(
        left, right, (((0,), (0,)), ((), ())), preferred_element_type=jnp.float32
    )


def along(left, right):
    return lax.dot_general(
        left, right, (((1,), (1,)), ((), ())), preferred_element_type=jnp.float32
    )


def matmul(left, right):
    return jnp.dot(left, right, preferred_element_type=jnp.float32)


def take_lanes(rows, index):
    return lax.gather(
        rows, index[..., None], ALONG_LANES, (1, 1), mode=lax.GatherScatterMode.PROMISE_IN_BOUNDS
    )


def find(load, high, low, chunks, parts):
    bits = [lax.bitwise_and(high, jnp.int16(1 << b)) != jnp.int16(0) for b in range(5)]

    def among(start, size, bit):
        if size == 1:
            return [take_lanes(load(start, v), low) for v in range(parts)]
        first = among(start, size // 2, bit - 1)
        last = among(start + size // 2, size // 2, bit - 1)
        return [jnp.where(bits[bit], q, p) for p, q in zip(first, last)]

    return among(0, chunks, chunks.bit_length() - 2)


def aggregate_kernel(
    adj_ref, feat_hbm, count_hbm, owner_hbm, out_ref, index, counts, rows, places, stage, wide,
    feat_ref, count_ref, owner_ref, arrivals,
):
    copies = [
        pltpu.make_async_copy(source, target, arrivals.at[number])
        for number, (source, target) in enumerate(
            ((count_hbm, count_ref), (owner_hbm, owner_ref), (feat_hbm, feat_ref))
        )
    ]
    for copy in copies:
        copy.start()
    copies[0].wait()
    width, inputs = feat_ref.shape
    nodes = owner_ref.shape[1]
    owners = out_ref.shape[0]
    fan = adj_ref.shape[0] - 1
    chunks = inputs // LANES
    groups = nodes // LANES
    parts = width // 16
    steps = (fan + 1) // 4
    i16, i32, bf16, f32 = jnp.int16, jnp.int32, jnp.bfloat16, jnp.float32
    span = 256
    before = (
        lax.broadcasted_iota(i32, (span, span), 0) < lax.broadcasted_iota(i32, (span, span), 1)
    ).astype(bf16)

    def ones(hit, axis):
        return jnp.sum(jnp.where(hit, 1.0, 0.0), axis=axis, keepdims=True)

    kinds = lax.broadcasted_iota(i32, (16, span), 0)
    blocks = [slice(b * span, (b + 1) * span) for b in range(nodes // span)]
    start = jnp.zeros((16, 1), f32)
    for at in blocks:
        start = start + ones(fan - count_ref[:, at] < kinds, 1)
    order, seen = [], start
    for at in blocks:
        hit = fan - count_ref[:, at] == kinds
        earlier = matmul(hit.astype(bf16), before) + seen
        order.append(jnp.sum(jnp.where(hit, earlier, 0.0), axis=0, keepdims=True).astype(i32))
        seen = seen + ones(hit, 1)
    node_at = jnp.zeros((2 * groups, LANES), f32)
    group_ids = lax.broadcasted_iota(i32, (groups, span), 0)
    lane_ids = lax.broadcasted_iota(i32, (LANES, span), 0)
    for b, place in enumerate(order):
        node = lax.broadcasted_iota(i32, (groups, span), 1) + b * span
        mine = group_ids == lax.shift_right_logical(place, 7)
        weights = jnp.concatenate(
            [
                jnp.where(mine, lax.shift_right_logical(node, 7), 0).astype(f32),
                jnp.where(mine, lax.bitwise_and(node, LANES - 1), 0).astype(f32),
            ],
            axis=0,
        ).astype(bf16)
        picked = (lane_ids == lax.bitwise_and(place, LANES - 1)).astype(bf16)
        node_at = node_at + along(weights, picked)
    node_at = node_at.astype(i32)
    for g in range(groups):
        high = jnp.broadcast_to(node_at[g : g + 1], (16, LANES)).astype(i16)
        low = jnp.broadcast_to(node_at[groups + g : groups + g + 1], (16, LANES)).astype(i16)
        (columns,) = find(
            lambda c, v: adj_ref[:, c * LANES : (c + 1) * LANES].astype(i16), high, low, groups, 1
        )
        columns = columns.astype(i32)
        for s in range(steps):
            index[g * steps + s, 0:4] = columns[s * 4 : s * 4 + 4]
        place = lax.broadcasted_iota(i32, (16, LANES), 1) + g * LANES
        counts[g] = (fan + 1) - ones(start.astype(i32) <= place, 0).astype(i32)

    copies[1].wait()
    copies[2].wait()

    def one_group(g, carry):
        count = counts[g]

        def four(s, total, first):
            total = list(total)
            for j in range(4):
                at = index[g * steps + s, j : j + 1, :]
                high = jnp.broadcast_to(lax.shift_right_logical(at, 7), (16, LANES)).astype(i16)
                low = jnp.broadcast_to(lax.bitwise_and(at, LANES - 1), (16, LANES)).astype(i16)
                found = find(
                    lambda c, v: feat_ref[v * 16 : (v + 1) * 16, c * LANES : (c + 1) * LANES],
                    high, low, chunks, parts,
                )
                if first and j == 0:
                    for v in range(parts):
                        rows[v * 16 : (v + 1) * 16, lanes_at(g)] = found[v]
                    continue
                valid = jnp.broadcast_to(s * 4 + j <= count, (16, LANES))
                for v in range(parts):
                    total[v] = total[v] + jnp.where(valid, found[v].astype(f32), 0.0)
            return tuple(total)

        total = four(0, (jnp.zeros((16, LANES), f32),) * parts, True)
        needed = lax.shift_right_logical(jnp.max(count) + 4, 2)
        total = lax.fori_loop(1, needed, lambda s, t: four(s, t, False), total)
        divisor = jnp.broadcast_to(count.astype(f32), (16, LANES))
        for v in range(parts):
            near = (total[v] / divisor).astype(bf16)
            rows[width + v * 16 : width + (v + 1) * 16, lanes_at(g)] = near
        return carry

    lax.fori_loop(0, groups, one_group, 0)

    owner_ids = lax.broadcasted_iota(i32, (owners, span), 0)
    ranks = lax.broadcasted_iota(i32, (CAP, span), 0)
    seen = jnp.zeros((owners, 1), f32)
    found_at = jnp.zeros((3 * CAP, owners), f32)
    for at, place in zip(blocks, order):
        hit = owner_ids == owner_ref[:, at]
        picked = hit.astype(bf16)
        earlier = matmul(picked, before) + seen
        rank = jnp.sum(jnp.where(hit, earlier, 0.0), axis=0, keepdims=True).astype(i32)
        seen = seen + ones(hit, 1)
        mine = ranks == rank
        weights = jnp.concatenate(
            [
                jnp.where(mine, lax.shift_right_logical(place, 7), 0).astype(f32),
                jnp.where(mine, lax.bitwise_and(place, LANES - 1), 0).astype(f32),
                jnp.where(mine, 1.0, 0.0),
            ],
            axis=0,
        ).astype(bf16)
        found_at = found_at + along(weights, picked)
    found_at = found_at.astype(i32)
    for q in range(CAP // 4):
        for kind in range(3):
            at = kind * CAP + q * 4
            places[q, kind * 4 : (kind + 1) * 4] = found_at[at : at + 4]

    half = 2 * width

    def four_ranks(q, carry):
        for j in range(4):
            high = jnp.broadcast_to(places[q, j : j + 1, :], (16, owners)).astype(i16)
            low = jnp.broadcast_to(places[q, 4 + j : 5 + j, :], (16, owners)).astype(i16)
            filled = jnp.broadcast_to(places[q, 8 + j : 9 + j, :], (16, owners)) > 0
            found = find(
                lambda c, v: rows[v * 16 : (v + 1) * 16, c * LANES : (c + 1) * LANES],
                high, low, groups, half // 16,
            )
            for v in range(half // 16):
                at = (j % 2) * half + v * 16
                stage[j // 2, at : at + 16, :] = jnp.where(filled, found[v].astype(f32), 0.0)
        for pair in range(2):
            wide[pl.ds(q * 2 + pair, owners, stride=16), :] = stage[pair].T
        return carry

    lax.fori_loop(0, CAP // 4, four_ranks, 0)

    def finish(t, carry):
        at = pl.ds(pl.multiple_of(t * 8, 8), 8)
        out_ref[at] = wide[lanes_at(t), :].astype(bf16).reshape(8, 16, LANES)
        return carry

    lax.fori_loop(0, owners // 8, finish, 0)


def aggregate(features, adjacent, count, owner, owners):
    width, _ = features.shape
    nodes = owner.shape[1]
    return pl.pallas_call(
        aggregate_kernel,
        out_shape=jax.ShapeDtypeStruct((owners, 16, LANES), jnp.bfloat16),
        in_specs=[VMEM] + [HBM] * 3,
        out_specs=VMEM,
        scratch_shapes=[
            pltpu.VMEM((nodes // LANES * 4, 4, LANES), jnp.int32),
            pltpu.VMEM((nodes // LANES, 1, LANES), jnp.int32),
            pltpu.VMEM((2 * width, nodes), jnp.bfloat16),
            pltpu.VMEM((CAP // 4, 12, LANES), jnp.int32),
            pltpu.VMEM((2, 4 * width, owners), jnp.float32),
            pltpu.VMEM((16 * owners, LANES), jnp.float32),
            pltpu.VMEM(features.shape, jnp.bfloat16),
            pltpu.VMEM(count.shape, jnp.int32),
            pltpu.VMEM(owner.shape, jnp.int32),
            pltpu.SemaphoreType.DMA((3,)),
        ],
        name="aggregate",
        compiler_params=pltpu.CompilerParams(vmem_limit_bytes=12 << 20),
        cost_estimate=pl.CostEstimate(flops=40_000_000, bytes_accessed=3_000_000, transcendentals=0),
    )(adjacent, in_hbm(features), in_hbm(count), in_hbm(owner))


def picks_kernel(adj_ref, center_ref, count_ref, out_ref, flip_ref):
    nodes, fan = adj_ref.shape
    slots = out_ref.shape[1]

    def table_row(slot):
        odd = lax.shift_left(lax.bitwise_and(slot, 1), 4)
        pair = lax.bitwise_and(lax.shift_right_logical(slot, 1), 15)
        return lax.bitwise_and(slot, -CAP) + odd + pair

    def one_tile(t, carry):
        at = pl.ds(pl.multiple_of(t * 16, 16), 16)
        number = lax.broadcasted_iota(jnp.int32, (16, fan), 1)
        adjacent = jnp.where(number < count_ref[at, :], table_row(adj_ref[at, :]), -1)
        center = jnp.broadcast_to(table_row(center_ref[at, :]), (16, LANES))
        spread = [jnp.broadcast_to(adjacent[:, k : k + 1], (16, LANES)) for k in range(fan)]
        for c in range(slots // LANES):
            ids = lax.broadcasted_iota(jnp.int32, (16, LANES), 1) + c * LANES
            total = jnp.zeros((16, LANES), jnp.float32)
            for k in range(fan):
                total = total + jnp.where(spread[k] == ids, 1.0, 0.0)
            out_ref[at, c * LANES : (c + 1) * LANES] = jnp.where(center == ids, 1.0, 0.0).astype(
                out_ref.dtype
            )
            low = pl.ds(pl.multiple_of(nodes + t * 16, 16), 16)
            out_ref[low, c * LANES : (c + 1) * LANES] = total.astype(out_ref.dtype)
        return carry

    lax.fori_loop(0, nodes // 16, one_tile, 0)

    def one_flip(t, carry):
        flip_ref[:, lanes_at(t)] = out_ref[lanes_at(t), :].T
        return carry

    lax.fori_loop(0, 2 * nodes // LANES, one_flip, 0)


def picks(adjacent, center, count, slots):
    nodes = adjacent.shape[0]
    return pl.pallas_call(
        picks_kernel,
        out_shape=(
            jax.ShapeDtypeStruct((2 * nodes, slots), jnp.bfloat16),
            jax.ShapeDtypeStruct((slots, 2 * nodes), jnp.bfloat16),
        ),
        in_specs=[VMEM] * 3,
        out_specs=(VMEM, VMEM),
        name="picks",
        compiler_params=pltpu.CompilerParams(vmem_limit_bytes=12 << 20),
        cost_estimate=pl.CostEstimate(flops=20_000_000, bytes_accessed=5_000_000, transcendentals=0),
    )(adjacent, center, count)


def call(kernel, outs, ins, smem=0, hbm=0, scratch=(), limit=16, flops=0, moved=0, exps=0):
    return pl.pallas_call(
        kernel,
        out_shape=outs,
        in_specs=[SMEM] * smem + [VMEM] * (ins - smem - hbm) + [HBM] * hbm,
        out_specs=(VMEM,) * len(outs),
        scratch_shapes=scratch,
        compiler_params=pltpu.CompilerParams(vmem_limit_bytes=limit << 20),
        cost_estimate=pl.CostEstimate(flops=flops, bytes_accessed=moved, transcendentals=exps),
    )


def in_hbm(value):
    return pltpu.with_memory_space_constraint(value, pltpu.HBM)


def put_chunks(to_ref, t, product):
    for c in range(product.shape[0] // 16):
        for lane in range(product.shape[1] // LANES):
            to_ref[t * (product.shape[0] // 16) + c, lane * 16 : (lane + 1) * 16, :] = product[
                c * 16 : (c + 1) * 16, lane * LANES : (lane + 1) * LANES
            ]


def forward_kernel(
    core_ref, z_ref, arrived_ref, pair_ref, other_pair_ref, bias_one_ref, count_ref, bias_two_ref,
    picks_hbm, root_hbm, near_hbm, upstream_hbm, out_ref, sent_ref, hidden, rows, slope,
    inputs_flip, bias_grad, inputs, picks_ref, root_ref, near_ref, upstream_ref, arrivals,
):
    copies = [
        pltpu.make_async_copy(source, target, arrivals.at[number])
        for number, (source, target) in enumerate(
            (
                (picks_hbm, picks_ref),
                (root_hbm, root_ref),
                (near_hbm, near_ref),
                (upstream_hbm, upstream_ref),
            )
        )
    ]
    for copy in copies:
        copy.start()
    slots, depth = inputs.shape
    hidden_width = hidden.shape[1]
    nodes = slope.shape[0]
    quarter = depth // 4
    sources = slots // CAP
    tile = 256

    def one_source(t, carry):
        for e in range(2):
            pieces = [
                arrived_ref[f * sources + t, :, e * quarter : (e + 1) * quarter] for f in range(4)
            ]
            at = pl.ds(pl.multiple_of(t * CAP + e * 16, 16), 16)
            inputs[at, :] = jnp.concatenate(pieces, axis=1)
        return carry

    lax.fori_loop(0, sources, one_source, 0)
    for t in range(slots // tile):
        inputs_flip[:, t * tile : (t + 1) * tile] = inputs[t * tile : (t + 1) * tile, :].T

    late = z_ref[0] >= 2

    def first_layer(t, carry):
        cols = lanes_at(t, tile)
        pair, other = pair_ref[:, cols], other_pair_ref[:, cols]
        pre = matmul(inputs[:, : depth // 2], jnp.where(late, other, pair))
        pre = pre + matmul(inputs[:, depth // 2 :], jnp.where(late, pair, other))
        pre = pre + bias_one_ref[:, cols]
        value = jnp.maximum(pre, 0.0) + jnp.log1p(jnp.exp(-jnp.abs(pre)))
        hidden[:, cols] = value.astype(jnp.bfloat16)
        return carry

    inverse = 1.0 / count_ref[...].astype(jnp.float32)

    def select(t, carry):
        cols = lanes_at(t, tile)
        rows[:nodes, cols] = matmul(picks_ref[:nodes, :], hidden[:, cols]).astype(jnp.bfloat16)
        total = matmul(picks_ref[nodes:, :], hidden[:, cols])
        rows[nodes:, cols] = (total * inverse).astype(jnp.bfloat16)
        return carry

    first_layer(0, 0)
    copies[0].wait()
    for t in range(1, hidden_width // tile):
        first_layer(t, 0)
        select(t - 1, 0)
    select(hidden_width // tile - 1, 0)
    for copy in copies[1:]:
        copy.wait()

    def second_layer(t, carry):
        cols = lanes_at(t, tile)
        pre = matmul(rows[:nodes, :], root_ref[:, cols]) + matmul(rows[nodes:, :], near_ref[:, cols])
        pre = pre + bias_two_ref[:, cols]
        gate = jax.nn.sigmoid(pre)
        out_ref[:, cols] = (pre * gate).astype(jnp.bfloat16)
        grad = upstream_ref[:, cols].astype(jnp.float32) * gate * (1.0 + pre * (1.0 - gate))
        grad = grad.astype(jnp.bfloat16)
        slope[:, cols] = grad
        bias_grad[0:1, cols] = jnp.sum(grad.astype(jnp.float32), axis=0, keepdims=True)
        return carry

    for t in range(hidden_width // tile):
        second_layer(t, 0)
    start = (core_ref[0] ^ 1) * nodes

    def weight_grads(t, carry):
        left = rows[pl.ds(pl.multiple_of(start, nodes), nodes), lanes_at(t, tile)]
        put_chunks(sent_ref, t, across(left, slope[...]).astype(jnp.bfloat16))
        return carry

    lax.fori_loop(0, hidden_width // tile, weight_grads, 0)


def kept_kernel(
    core_ref, rows_ref, slope_ref, received_ref, kept_one_ref, received_one_ref, both_ref
):
    nodes, hidden_width = slope_ref.shape
    tile = 256
    start = core_ref[0] * nodes

    def weight_grads(t, carry):
        left = rows_ref[pl.ds(pl.multiple_of(start, nodes), nodes), lanes_at(t, tile)]
        product = across(left, slope_ref[...])
        for c in range(tile // 16):
            chunk = t * (tile // 16) + c
            for lane in range(hidden_width // LANES):
                at = slice(lane * 16, (lane + 1) * 16)
                mine = product[c * 16 : (c + 1) * 16, lane * LANES : (lane + 1) * LANES]
                other = received_ref[chunk, at, :].astype(jnp.float32)
                both_ref[chunk, at, :] = (mine + other).astype(jnp.bfloat16)
            mine = kept_one_ref[chunk].astype(jnp.float32)
            other = received_one_ref[chunk].astype(jnp.float32)
            both_ref[chunk, LANES:, :] = (mine + other).astype(jnp.bfloat16)
        return carry

    lax.fori_loop(0, hidden_width // tile, weight_grads, 0)


def backward_kernel(
    core_ref, slope_ref, root_ref, near_ref, count_ref, flip_ref, hidden_ref, inputs_flip_ref,
    bias_two_ref, kept_ref, sent_ref, back, bias_grads,
):
    core = core_ref[0]
    nodes, hidden_width = slope_ref.shape
    tile = 256
    bias_grads[0:1, :] = bias_two_ref[0:1, :]
    inverse = 1.0 / count_ref[...].astype(jnp.float32)

    def backward(t, carry):
        cols = lanes_at(t, tile)
        back[:nodes, cols] = along(slope_ref[...], root_ref[cols, :]).astype(jnp.bfloat16)
        near = along(slope_ref[...], near_ref[cols, :])
        back[nodes:, cols] = (near * inverse).astype(jnp.bfloat16)
        return carry

    lax.fori_loop(0, hidden_width // tile, backward, 0)

    def first_grads(t, carry):
        cols = lanes_at(t, tile)
        table_grad = matmul(flip_ref[...], back[:, cols])
        grad = table_grad * (1.0 - jnp.exp(-hidden_ref[:, cols].astype(jnp.float32)))
        grad = grad.astype(jnp.bfloat16)
        bias_grads[1:2, cols] = jnp.sum(grad.astype(jnp.float32), axis=0, keepdims=True)
        product = matmul(inputs_flip_ref[...], grad).astype(jnp.bfloat16)
        low, high = product[:LANES], product[LANES:]
        mine, partner = jnp.where(core == 0, low, high), jnp.where(core == 0, high, low)
        for to_ref, product in ((kept_ref, mine), (sent_ref, partner)):
            for c in range(8):
                for lane in range(tile // LANES):
                    chunk = c * 8 + t * (tile // LANES) + lane
                    to_ref[chunk, 0:16, :] = product[
                        c * 16 : (c + 1) * 16, lane * LANES : (lane + 1) * LANES
                    ]
        return carry

    for t in range(hidden_width // tile):
        first_grads(t, 0)
    for place, to_ref in enumerate((kept_ref, sent_ref)):
        which = core ^ place
        to_ref[:, 16:, :] = jnp.zeros((to_ref.shape[0], 8, LANES), jnp.bfloat16)
        for lane in range(8):
            cols = slice(lane * LANES, (lane + 1) * LANES)
            row = jnp.where(which == 0, bias_grads[0:1, cols], bias_grads[1:2, cols])
            to_ref[lane, 16:, :] = jnp.broadcast_to(row, (8, LANES)).astype(jnp.bfloat16)


def shaped(*shape, dtype=jnp.bfloat16):
    return jax.ShapeDtypeStruct(shape, dtype)


def widen(from_ref, wide, root_hbm, near_hbm, to_root, sent):
    tiles = wide.shape[0] // LANES

    def copy(t, target):
        return pltpu.make_async_copy(wide.at[lanes_at(t)], target.at[lanes_at(t)], sent.at[t])

    def one_tile(t, carry):
        for c in range(8):
            at = pl.ds(pl.multiple_of(t * LANES + c * 16, 16), 16)
            for lane in range(8):
                piece = from_ref[t * 8 + c, lane * 16 : (lane + 1) * 16, :]
                wide[at, lane * LANES : (lane + 1) * LANES] = piece.astype(jnp.float32)

        @pl.when(to_root)
        def _():
            copy(t, root_hbm).start()

        @pl.when(jnp.logical_not(to_root))
        def _():
            copy(t, near_hbm).start()

        return carry

    lax.fori_loop(0, tiles, one_tile, 0)

    def finish():
        @pl.when(to_root)
        def _():
            for t in range(tiles):
                copy(t, root_hbm).wait()

        @pl.when(jnp.logical_not(to_root))
        def _():
            for t in range(tiles):
                copy(t, near_hbm).wait()

    return finish


def own_half_kernel(core_ref, kept_ref, root_hbm, near_hbm, wide, sent):
    widen(kept_ref, wide, root_hbm, near_hbm, core_ref[0] == 0, sent)()


def other_half_kernel(
    core_ref, z_ref, kept_ref, other_ref, root_in, near_in, root_hbm, near_hbm, first_root_ref,
    first_near_ref, bias_two_ref, bias_one_ref, wide, sent,
):
    del root_in, near_in
    core, z = core_ref[0], z_ref[0]
    even = core == 0
    finish = widen(other_ref, wide, root_hbm, near_hbm, core != 0, sent)
    here = lax.shift_right_logical(z, 1) == core
    base = lax.bitwise_and(z, 1) * 4
    for j, to_ref in enumerate((first_root_ref, first_near_ref)):
        for i in range(2):
            for lane in range(8):
                chunk = (base + 2 * j + i) * 8 + lane
                kept = kept_ref[chunk, LANES : LANES + 16, :].astype(jnp.float32)
                other = other_ref[chunk, LANES : LANES + 16, :].astype(jnp.float32)
                at, cols = slice(i * 16, (i + 1) * 16), slice(lane * LANES, (lane + 1) * LANES)
                to_ref[at, cols] = jnp.where(here, kept, other)
    for lane in range(8):
        kept = kept_ref[lane, LANES + 16 :, :].astype(jnp.float32)[0:1, :]
        other = other_ref[lane, LANES + 16 :, :].astype(jnp.float32)[0:1, :]
        cols = slice(lane * LANES, (lane + 1) * LANES)
        bias_two_ref[:, cols] = jnp.where(even, kept, other)
        bias_one_ref[:, cols] = jnp.where(even, other, kept)
    finish()


def spread(core, z, kept, hidden_width):
    f32 = jnp.float32
    square = shaped(hidden_width, hidden_width, dtype=f32)
    slab = shaped(32, hidden_width, dtype=f32)
    line = shaped(1, hidden_width, dtype=f32)
    scratch = [pltpu.VMEM(square.shape, f32), pltpu.SemaphoreType.DMA((hidden_width // LANES,))]
    other = lax.ppermute(kept, "core", [(0, 1), (1, 0)])
    root, near = pl.pallas_call(
        own_half_kernel,
        out_shape=(square, square),
        in_specs=[SMEM, VMEM],
        out_specs=(HBM, HBM),
        scratch_shapes=scratch,
        name="own_half",
        compiler_params=pltpu.CompilerParams(vmem_limit_bytes=8 << 20),
        cost_estimate=pl.CostEstimate(flops=1_000_000, bytes_accessed=7_000_000, transcendentals=0),
    )(core, kept)
    return pl.pallas_call(
        other_half_kernel,
        out_shape=(square, square, slab, slab, line, line),
        in_specs=[SMEM, SMEM, VMEM, VMEM, HBM, HBM],
        out_specs=(HBM, HBM) + (VMEM,) * 4,
        scratch_shapes=scratch,
        input_output_aliases={4: 0, 5: 1},
        name="other_half",
        compiler_params=pltpu.CompilerParams(vmem_limit_bytes=8 << 20),
        cost_estimate=pl.CostEstimate(flops=1_000_000, bytes_accessed=9_000_000, transcendentals=0),
    )(core, z, kept, other, root, near)


def weights_of_pair(own, z):
    first = lax.ppermute(own, "z", [(0, 1), (1, 0), (2, 3), (3, 2)])
    odd = lax.bitwise_and(z, 1) == 1
    return jnp.concatenate([jnp.where(odd, first, own), jnp.where(odd, own, first)], axis=0)


def weights_of_others(pair):
    return lax.ppermute(pair, "z", [(0, 3), (3, 0), (1, 2), (2, 1)])


def exchange(value, axes):
    return lax.all_to_all(value, axes, split_axis=0, concat_axis=0, tiled=True)


def step(
    features,
    first_adjacent,
    first_center,
    first_count,
    owner_map,
    first_root,
    first_near,
    first_bias,
    second_adjacent,
    second_center,
    second_count,
    second_root,
    second_near,
    second_bias,
    upstream,
):
    owners = 128
    hidden_width = first_root.shape[1]
    z = lax.axis_index("z")
    core = lax.axis_index("core")[None]
    pair = weights_of_pair(jnp.concatenate([first_root, first_near], axis=0), z)
    columns = jnp.concatenate([first_center[:, None], first_adjacent], axis=1).T
    packed = aggregate(features, columns, first_count[None], owner_map[None], owners)
    packed, pair = lax.optimization_barrier((packed, pair))
    other_pair = weights_of_others(pair)
    arrived = exchange(packed, AXES)
    count = second_count[:, None]
    picked, flipped = picks(second_adjacent, second_center[:, None], count, owners * 8)
    slots, depth = picked.shape[1], 2 * pair.shape[0]
    nodes = upstream.shape[0]
    layer_output, sent_two, hidden, rows, slope, inputs_flip, bias_grad = call(
        forward_kernel,
        (
            shaped(nodes, hidden_width),
            shaped(64, LANES, LANES),
            shaped(slots, hidden_width),
            shaped(2 * nodes, hidden_width),
            shaped(nodes, hidden_width),
            shaped(depth, slots),
            shaped(8, hidden_width, dtype=jnp.float32),
        ),
        12,
        smem=2,
        hbm=4,
        scratch=[
            pltpu.VMEM((slots, depth), jnp.bfloat16),
            pltpu.VMEM(picked.shape, jnp.bfloat16),
            pltpu.VMEM(second_root.shape, jnp.bfloat16),
            pltpu.VMEM(second_near.shape, jnp.bfloat16),
            pltpu.VMEM(upstream.shape, jnp.bfloat16),
            pltpu.SemaphoreType.DMA((4,)),
        ],
        limit=24,
        flops=6_000_000_000,
        moved=18_000_000,
        exps=3_000_000,
    )(
        core, z[None], arrived, pair, other_pair, first_bias[None], count, second_bias[None],
        in_hbm(picked), in_hbm(second_root), in_hbm(second_near), in_hbm(upstream),
    )
    received = lax.ppermute(sent_two, "core", [(0, 1), (1, 0)])
    kept_one, sent_one = call(
        backward_kernel, (shaped(64, 24, LANES), shaped(64, 24, LANES)), 9, smem=1,
        scratch=[
            pltpu.VMEM((2 * nodes, hidden_width), jnp.bfloat16),
            pltpu.VMEM((8, hidden_width), jnp.float32),
        ],
        limit=24, flops=4_700_000_000, moved=12_000_000, exps=1_000_000,
    )(core, slope, second_root, second_near, count, flipped, hidden, inputs_flip, bias_grad)
    received_one = lax.ppermute(sent_one, "core", [(0, 1), (1, 0)])
    (both,) = call(
        kept_kernel, (shaped(64, CHUNK, LANES),), 6, smem=1, limit=20,
        flops=1_000_000_000, moved=7_000_000,
    )(core, rows, slope, received, kept_one, received_one)
    terms = exchange(both, CHIPS)
    total = jnp.sum(terms.astype(jnp.float32), axis=0).astype(jnp.bfloat16)
    mine = exchange(jnp.broadcast_to(total[None], terms.shape), CHIPS)
    root_two, near_two, root_one, near_one, bias_two, bias_one = spread(
        core, z[None], mine, hidden_width
    )
    return (layer_output, root_two, near_two, bias_two[0], root_one, near_one, bias_one[0])


def solution(mesh):
    chips = Mesh(mesh.devices.reshape(4, 4, 4, 2), AXES)
    trainer = ("x", "y", "core")
    return jax.shard_map(
        step,
        mesh=chips,
        in_specs=(
            P("z", trainer),
            P(trainer, None),
            P(trainer),
            P(trainer),
            P(trainer),
            P("z", None),
            P("z", None),
            P(),
            P(AXES, None),
            P(AXES),
            P(AXES),
            P(),
            P(),
            P(),
            P(AXES, None),
        ),
        out_specs=(
            P(AXES, None),
            P(),
            P(),
            P(),
            P("z", None),
            P("z", None),
            P(),
        ),
        check_vma=False,
    )
```

```python
import jax
import jax.numpy as jnp
from jax import lax
from jax.experimental import pallas as pl
from jax.experimental.pallas import tpu as pltpu
from jax.sharding import Mesh, PartitionSpec as P


CAP = 32
LANES = 128
AXES = ("z", "x", "y", "core")
CHIPS = ("z", "x", "y")
CHUNK = 152
VMEM = pl.BlockSpec(memory_space=pltpu.VMEM)
ALONG_LANES = lax.GatherDimensionNumbers(
    offset_dims=(),
    collapsed_slice_dims=(1,),
    start_index_map=(1,),
    operand_batching_dims=(0,),
    start_indices_batching_dims=(0,),
)
SMEM = pl.BlockSpec(memory_space=pltpu.SMEM)
HBM = pl.BlockSpec(memory_space=pltpu.HBM)


def lanes_at(at, size=LANES):
    if isinstance(at, int):
        return slice(at * size, (at + 1) * size)
    return pl.ds(pl.multiple_of(at * size, size), size)


def across(left, right):
    return lax.dot_general(
        left, right, (((0,), (0,)), ((), ())), preferred_element_type=jnp.float32
    )


def along(left, right):
    return lax.dot_general(
        left, right, (((1,), (1,)), ((), ())), preferred_element_type=jnp.float32
    )


def matmul(left, right):
    return jnp.dot(left, right, preferred_element_type=jnp.float32)


def take_lanes(rows, index):
    return lax.gather(
        rows, index[..., None], ALONG_LANES, (1, 1), mode=lax.GatherScatterMode.PROMISE_IN_BOUNDS
    )


def find(load, high, low, chunks, parts):
    bits = [lax.bitwise_and(high, jnp.int16(1 << b)) != jnp.int16(0) for b in range(5)]

    def among(start, size, bit):
        if size == 1:
            return [take_lanes(load(start, v), low) for v in range(parts)]
        first = among(start, size // 2, bit - 1)
        last = among(start + size // 2, size // 2, bit - 1)
        return [jnp.where(bits[bit], q, p) for p, q in zip(first, last)]

    return among(0, chunks, chunks.bit_length() - 2)


def aggregate_kernel(
    adj_ref, feat_hbm, count_hbm, owner_hbm, out_ref, index, counts, rows, places, stage, wide,
    feat_ref, count_ref, owner_ref, arrivals,
):
    copies = [
        pltpu.make_async_copy(source, target, arrivals.at[number])
        for number, (source, target) in enumerate(
            ((count_hbm, count_ref), (owner_hbm, owner_ref), (feat_hbm, feat_ref))
        )
    ]
    for copy in copies:
        copy.start()
    copies[0].wait()
    width, inputs = feat_ref.shape
    nodes = owner_ref.shape[1]
    owners = out_ref.shape[0]
    fan = adj_ref.shape[0] - 1
    chunks = inputs // LANES
    groups = nodes // LANES
    parts = width // 16
    steps = (fan + 1) // 4
    i16, i32, bf16, f32 = jnp.int16, jnp.int32, jnp.bfloat16, jnp.float32
    span = 256
    before = (
        lax.broadcasted_iota(i32, (span, span), 0) < lax.broadcasted_iota(i32, (span, span), 1)
    ).astype(bf16)

    def ones(hit, axis):
        return jnp.sum(jnp.where(hit, 1.0, 0.0), axis=axis, keepdims=True)

    kinds = lax.broadcasted_iota(i32, (16, span), 0)
    blocks = [slice(b * span, (b + 1) * span) for b in range(nodes // span)]
    start = jnp.zeros((16, 1), f32)
    for at in blocks:
        start = start + ones(fan - count_ref[:, at] < kinds, 1)
    order, seen = [], start
    for at in blocks:
        hit = fan - count_ref[:, at] == kinds
        earlier = matmul(hit.astype(bf16), before) + seen
        order.append(jnp.sum(jnp.where(hit, earlier, 0.0), axis=0, keepdims=True).astype(i32))
        seen = seen + ones(hit, 1)
    node_at = jnp.zeros((2 * groups, LANES), f32)
    group_ids = lax.broadcasted_iota(i32, (groups, span), 0)
    lane_ids = lax.broadcasted_iota(i32, (LANES, span), 0)
    for b, place in enumerate(order):
        node = lax.broadcasted_iota(i32, (groups, span), 1) + b * span
        mine = group_ids == lax.shift_right_logical(place, 7)
        weights = jnp.concatenate(
            [
                jnp.where(mine, lax.shift_right_logical(node, 7), 0).astype(f32),
                jnp.where(mine, lax.bitwise_and(node, LANES - 1), 0).astype(f32),
            ],
            axis=0,
        ).astype(bf16)
        picked = (lane_ids == lax.bitwise_and(place, LANES - 1)).astype(bf16)
        node_at = node_at + along(weights, picked)
    node_at = node_at.astype(i32)
    for g in range(groups):
        high = jnp.broadcast_to(node_at[g : g + 1], (16, LANES)).astype(i16)
        low = jnp.broadcast_to(node_at[groups + g : groups + g + 1], (16, LANES)).astype(i16)
        (columns,) = find(
            lambda c, v: adj_ref[:, c * LANES : (c + 1) * LANES].astype(i16), high, low, groups, 1
        )
        columns = columns.astype(i32)
        for s in range(steps):
            index[g * steps + s, 0:4] = columns[s * 4 : s * 4 + 4]
        place = lax.broadcasted_iota(i32, (16, LANES), 1) + g * LANES
        counts[g] = (fan + 1) - ones(start.astype(i32) <= place, 0).astype(i32)

    copies[1].wait()
    copies[2].wait()

    def one_group(g, carry):
        count = counts[g]

        def four(s, total):
            total = list(total)
            for j in range(4):
                at = index[g * steps + s, j : j + 1, :]
                high = jnp.broadcast_to(lax.shift_right_logical(at, 7), (16, LANES)).astype(i16)
                low = jnp.broadcast_to(lax.bitwise_and(at, LANES - 1), (16, LANES)).astype(i16)
                found = find(
                    lambda c, v: feat_ref[v * 16 : (v + 1) * 16, c * LANES : (c + 1) * LANES],
                    high, low, chunks, parts,
                )
                valid = jnp.broadcast_to(s * 4 + j <= count, (16, LANES))
                if j == 0:
                    valid = valid & (s > 0)
                    for v in range(parts):
                        held = rows[v * 16 : (v + 1) * 16, lanes_at(g)]
                        rows[v * 16 : (v + 1) * 16, lanes_at(g)] = jnp.where(s == 0, found[v], held)
                for v in range(parts):
                    total[v] = total[v] + jnp.where(valid, found[v].astype(f32), 0.0)
            return tuple(total)

        needed = lax.shift_right_logical(jnp.max(count) + 4, 2)
        total = lax.fori_loop(0, needed, four, (jnp.zeros((16, LANES), f32),) * parts)
        divisor = jnp.broadcast_to(count.astype(f32), (16, LANES))
        for v in range(parts):
            near = (total[v] / divisor).astype(bf16)
            rows[width + v * 16 : width + (v + 1) * 16, lanes_at(g)] = near
        return carry

    lax.fori_loop(0, groups, one_group, 0)

    owner_ids = lax.broadcasted_iota(i32, (owners, span), 0)
    ranks = lax.broadcasted_iota(i32, (CAP, span), 0)
    seen = jnp.zeros((owners, 1), f32)
    found_at = jnp.zeros((3 * CAP, owners), f32)
    for at, place in zip(blocks, order):
        hit = owner_ids == owner_ref[:, at]
        picked = hit.astype(bf16)
        earlier = matmul(picked, before) + seen
        rank = jnp.sum(jnp.where(hit, earlier, 0.0), axis=0, keepdims=True).astype(i32)
        seen = seen + ones(hit, 1)
        mine = ranks == rank
        weights = jnp.concatenate(
            [
                jnp.where(mine, lax.shift_right_logical(place, 7), 0).astype(f32),
                jnp.where(mine, lax.bitwise_and(place, LANES - 1), 0).astype(f32),
                jnp.where(mine, 1.0, 0.0),
            ],
            axis=0,
        ).astype(bf16)
        found_at = found_at + along(weights, picked)
    found_at = found_at.astype(i32)
    for q in range(CAP // 4):
        for kind in range(3):
            at = kind * CAP + q * 4
            places[q, kind * 4 : (kind + 1) * 4] = found_at[at : at + 4]

    half = 2 * width

    def four_ranks(q, carry):
        for j in range(4):
            high = jnp.broadcast_to(places[q, j : j + 1, :], (16, owners)).astype(i16)
            low = jnp.broadcast_to(places[q, 4 + j : 5 + j, :], (16, owners)).astype(i16)
            filled = jnp.broadcast_to(places[q, 8 + j : 9 + j, :], (16, owners)) > 0
            found = find(
                lambda c, v: rows[v * 16 : (v + 1) * 16, c * LANES : (c + 1) * LANES],
                high, low, groups, half // 16,
            )
            for v in range(half // 16):
                at = (j % 2) * half + v * 16
                stage[j // 2, at : at + 16, :] = jnp.where(filled, found[v].astype(f32), 0.0)
        for pair in range(2):
            wide[pl.ds(q * 2 + pair, owners, stride=16), :] = stage[pair].T
        return carry

    lax.fori_loop(0, CAP // 4, four_ranks, 0)

    def finish(t, carry):
        at = pl.ds(pl.multiple_of(t * 8, 8), 8)
        out_ref[at] = wide[lanes_at(t), :].astype(bf16).reshape(8, 16, LANES)
        return carry

    lax.fori_loop(0, owners // 8, finish, 0)


def aggregate(features, adjacent, count, owner, owners):
    width, _ = features.shape
    nodes = owner.shape[1]
    return pl.pallas_call(
        aggregate_kernel,
        out_shape=jax.ShapeDtypeStruct((owners, 16, LANES), jnp.bfloat16),
        in_specs=[VMEM] + [HBM] * 3,
        out_specs=VMEM,
        scratch_shapes=[
            pltpu.VMEM((nodes // LANES * 4, 4, LANES), jnp.int32),
            pltpu.VMEM((nodes // LANES, 1, LANES), jnp.int32),
            pltpu.VMEM((2 * width, nodes), jnp.bfloat16),
            pltpu.VMEM((CAP // 4, 12, LANES), jnp.int32),
            pltpu.VMEM((2, 4 * width, owners), jnp.float32),
            pltpu.VMEM((16 * owners, LANES), jnp.float32),
            pltpu.VMEM(features.shape, jnp.bfloat16),
            pltpu.VMEM(count.shape, jnp.int32),
            pltpu.VMEM(owner.shape, jnp.int32),
            pltpu.SemaphoreType.DMA((3,)),
        ],
        name="aggregate",
        compiler_params=pltpu.CompilerParams(vmem_limit_bytes=12 << 20),
        cost_estimate=pl.CostEstimate(flops=40_000_000, bytes_accessed=3_000_000, transcendentals=0),
    )(adjacent, in_hbm(features), in_hbm(count), in_hbm(owner))


def picks_kernel(adj_ref, center_ref, count_ref, out_ref, flip_ref):
    nodes, fan = adj_ref.shape
    slots = out_ref.shape[1]

    def table_row(slot):
        odd = lax.shift_left(lax.bitwise_and(slot, 1), 4)
        pair = lax.bitwise_and(lax.shift_right_logical(slot, 1), 15)
        return lax.bitwise_and(slot, -CAP) + odd + pair

    def one_tile(t, carry):
        at = pl.ds(pl.multiple_of(t * 16, 16), 16)
        number = lax.broadcasted_iota(jnp.int32, (16, fan), 1)
        adjacent = jnp.where(number < count_ref[at, :], table_row(adj_ref[at, :]), -1)
        center = jnp.broadcast_to(table_row(center_ref[at, :]), (16, LANES))
        spread = [jnp.broadcast_to(adjacent[:, k : k + 1], (16, LANES)) for k in range(fan)]
        for c in range(slots // LANES):
            ids = lax.broadcasted_iota(jnp.int32, (16, LANES), 1) + c * LANES
            total = jnp.zeros((16, LANES), jnp.float32)
            for k in range(fan):
                total = total + jnp.where(spread[k] == ids, 1.0, 0.0)
            out_ref[at, c * LANES : (c + 1) * LANES] = jnp.where(center == ids, 1.0, 0.0).astype(
                out_ref.dtype
            )
            low = pl.ds(pl.multiple_of(nodes + t * 16, 16), 16)
            out_ref[low, c * LANES : (c + 1) * LANES] = total.astype(out_ref.dtype)
        return carry

    lax.fori_loop(0, nodes // 16, one_tile, 0)

    def one_flip(t, carry):
        flip_ref[:, lanes_at(t)] = out_ref[lanes_at(t), :].T
        return carry

    lax.fori_loop(0, 2 * nodes // LANES, one_flip, 0)


def picks(adjacent, center, count, slots):
    nodes = adjacent.shape[0]
    return pl.pallas_call(
        picks_kernel,
        out_shape=(
            jax.ShapeDtypeStruct((2 * nodes, slots), jnp.bfloat16),
            jax.ShapeDtypeStruct((slots, 2 * nodes), jnp.bfloat16),
        ),
        in_specs=[VMEM] * 3,
        out_specs=(VMEM, VMEM),
        name="picks",
        compiler_params=pltpu.CompilerParams(vmem_limit_bytes=12 << 20),
        cost_estimate=pl.CostEstimate(flops=20_000_000, bytes_accessed=5_000_000, transcendentals=0),
    )(adjacent, center, count)


def call(kernel, outs, ins, smem=0, hbm=0, scratch=(), limit=16, flops=0, moved=0, exps=0):
    return pl.pallas_call(
        kernel,
        out_shape=outs,
        in_specs=[SMEM] * smem + [VMEM] * (ins - smem - hbm) + [HBM] * hbm,
        out_specs=(VMEM,) * len(outs),
        scratch_shapes=scratch,
        compiler_params=pltpu.CompilerParams(vmem_limit_bytes=limit << 20),
        cost_estimate=pl.CostEstimate(flops=flops, bytes_accessed=moved, transcendentals=exps),
    )


def in_hbm(value):
    return pltpu.with_memory_space_constraint(value, pltpu.HBM)


def put_chunks(to_ref, t, product):
    for c in range(product.shape[0] // 16):
        for lane in range(product.shape[1] // LANES):
            to_ref[t * (product.shape[0] // 16) + c, lane * 16 : (lane + 1) * 16, :] = product[
                c * 16 : (c + 1) * 16, lane * LANES : (lane + 1) * LANES
            ]


def forward_kernel(
    core_ref, z_ref, arrived_ref, pair_ref, other_pair_ref, bias_one_ref, count_ref, bias_two_ref,
    picks_hbm, root_hbm, near_hbm, upstream_hbm, out_ref, sent_ref, hidden, rows, slope,
    inputs_flip, bias_grad, inputs, picks_ref, root_ref, near_ref, upstream_ref, arrivals,
):
    copies = [
        pltpu.make_async_copy(source, target, arrivals.at[number])
        for number, (source, target) in enumerate(
            (
                (picks_hbm, picks_ref),
                (root_hbm, root_ref),
                (near_hbm, near_ref),
                (upstream_hbm, upstream_ref),
            )
        )
    ]
    for copy in copies:
        copy.start()
    slots, depth = inputs.shape
    hidden_width = hidden.shape[1]
    nodes = slope.shape[0]
    quarter = depth // 4
    sources = slots // CAP
    tile = 256

    def one_source(t, carry):
        for e in range(2):
            pieces = [
                arrived_ref[f * sources + t, :, e * quarter : (e + 1) * quarter] for f in range(4)
            ]
            at = pl.ds(pl.multiple_of(t * CAP + e * 16, 16), 16)
            inputs[at, :] = jnp.concatenate(pieces, axis=1)
        return carry

    lax.fori_loop(0, sources, one_source, 0)
    for t in range(slots // tile):
        inputs_flip[:, t * tile : (t + 1) * tile] = inputs[t * tile : (t + 1) * tile, :].T

    late = z_ref[0] >= 2

    def first_layer(t, carry):
        cols = lanes_at(t, tile)
        pair, other = pair_ref[:, cols], other_pair_ref[:, cols]
        pre = matmul(inputs[:, : depth // 2], jnp.where(late, other, pair))
        pre = pre + matmul(inputs[:, depth // 2 :], jnp.where(late, pair, other))
        pre = pre + bias_one_ref[:, cols]
        value = jnp.maximum(pre, 0.0) + jnp.log1p(jnp.exp(-jnp.abs(pre)))
        hidden[:, cols] = value.astype(jnp.bfloat16)
        return carry

    inverse = 1.0 / count_ref[...].astype(jnp.float32)

    def select(t, carry):
        cols = lanes_at(t, tile)
        rows[:nodes, cols] = matmul(picks_ref[:nodes, :], hidden[:, cols]).astype(jnp.bfloat16)
        total = matmul(picks_ref[nodes:, :], hidden[:, cols])
        rows[nodes:, cols] = (total * inverse).astype(jnp.bfloat16)
        return carry

    first_layer(0, 0)
    copies[0].wait()
    for t in range(1, hidden_width // tile):
        first_layer(t, 0)
        select(t - 1, 0)
    select(hidden_width // tile - 1, 0)
    for copy in copies[1:]:
        copy.wait()

    def second_layer(t, carry):
        cols = lanes_at(t, tile)
        pre = matmul(rows[:nodes, :], root_ref[:, cols]) + matmul(rows[nodes:, :], near_ref[:, cols])
        pre = pre + bias_two_ref[:, cols]
        gate = jax.nn.sigmoid(pre)
        out_ref[:, cols] = (pre * gate).astype(jnp.bfloat16)
        grad = upstream_ref[:, cols].astype(jnp.float32) * gate * (1.0 + pre * (1.0 - gate))
        grad = grad.astype(jnp.bfloat16)
        slope[:, cols] = grad
        bias_grad[0:1, cols] = jnp.sum(grad.astype(jnp.float32), axis=0, keepdims=True)
        return carry

    for t in range(hidden_width // tile):
        second_layer(t, 0)
    start = (core_ref[0] ^ 1) * nodes

    def weight_grads(t, carry):
        left = rows[pl.ds(pl.multiple_of(start, nodes), nodes), lanes_at(t, tile)]
        put_chunks(sent_ref, t, across(left, slope[...]).astype(jnp.bfloat16))
        return carry

    lax.fori_loop(0, hidden_width // tile, weight_grads, 0)


def kept_kernel(
    core_ref, rows_ref, slope_ref, received_ref, kept_one_ref, received_one_ref, both_ref
):
    nodes, hidden_width = slope_ref.shape
    tile = 256
    start = core_ref[0] * nodes

    def weight_grads(t, carry):
        left = rows_ref[pl.ds(pl.multiple_of(start, nodes), nodes), lanes_at(t, tile)]
        product = across(left, slope_ref[...])
        for c in range(tile // 16):
            chunk = t * (tile // 16) + c
            for lane in range(hidden_width // LANES):
                at = slice(lane * 16, (lane + 1) * 16)
                mine = product[c * 16 : (c + 1) * 16, lane * LANES : (lane + 1) * LANES]
                other = received_ref[chunk, at, :].astype(jnp.float32)
                both_ref[chunk, at, :] = (mine + other).astype(jnp.bfloat16)
            mine = kept_one_ref[chunk].astype(jnp.float32)
            other = received_one_ref[chunk].astype(jnp.float32)
            both_ref[chunk, LANES:, :] = (mine + other).astype(jnp.bfloat16)
        return carry

    lax.fori_loop(0, hidden_width // tile, weight_grads, 0)


def backward_kernel(
    core_ref, slope_ref, root_ref, near_ref, count_ref, flip_ref, hidden_ref, inputs_flip_ref,
    bias_two_ref, kept_ref, sent_ref, back, bias_grads,
):
    core = core_ref[0]
    nodes, hidden_width = slope_ref.shape
    tile = 256
    bias_grads[0:1, :] = bias_two_ref[0:1, :]
    inverse = 1.0 / count_ref[...].astype(jnp.float32)

    def backward(t, carry):
        cols = lanes_at(t, tile)
        back[:nodes, cols] = along(slope_ref[...], root_ref[cols, :]).astype(jnp.bfloat16)
        near = along(slope_ref[...], near_ref[cols, :])
        back[nodes:, cols] = (near * inverse).astype(jnp.bfloat16)
        return carry

    lax.fori_loop(0, hidden_width // tile, backward, 0)

    def first_grads(t, carry):
        cols = lanes_at(t, tile)
        table_grad = matmul(flip_ref[...], back[:, cols])
        grad = table_grad * (1.0 - jnp.exp(-hidden_ref[:, cols].astype(jnp.float32)))
        grad = grad.astype(jnp.bfloat16)
        bias_grads[1:2, cols] = jnp.sum(grad.astype(jnp.float32), axis=0, keepdims=True)
        product = matmul(inputs_flip_ref[...], grad).astype(jnp.bfloat16)
        low, high = product[:LANES], product[LANES:]
        mine, partner = jnp.where(core == 0, low, high), jnp.where(core == 0, high, low)
        for to_ref, product in ((kept_ref, mine), (sent_ref, partner)):
            for c in range(8):
                for lane in range(tile // LANES):
                    chunk = c * 8 + t * (tile // LANES) + lane
                    to_ref[chunk, 0:16, :] = product[
                        c * 16 : (c + 1) * 16, lane * LANES : (lane + 1) * LANES
                    ]
        return carry

    lax.fori_loop(0, hidden_width // tile, first_grads, 0)
    for place, to_ref in enumerate((kept_ref, sent_ref)):
        which = core ^ place
        to_ref[:, 16:, :] = jnp.zeros((to_ref.shape[0], 8, LANES), jnp.bfloat16)
        for lane in range(8):
            cols = slice(lane * LANES, (lane + 1) * LANES)
            row = jnp.where(which == 0, bias_grads[0:1, cols], bias_grads[1:2, cols])
            to_ref[lane, 16:, :] = jnp.broadcast_to(row, (8, LANES)).astype(jnp.bfloat16)


def shaped(*shape, dtype=jnp.bfloat16):
    return jax.ShapeDtypeStruct(shape, dtype)


def widen(from_ref, wide, root_hbm, near_hbm, to_root, sent):
    tiles = wide.shape[0] // LANES

    def copy(t, target):
        return pltpu.make_async_copy(wide.at[lanes_at(t)], target.at[lanes_at(t)], sent.at[t])

    def one_tile(t, carry):
        for c in range(8):
            at = pl.ds(pl.multiple_of(t * LANES + c * 16, 16), 16)
            for lane in range(8):
                piece = from_ref[t * 8 + c, lane * 16 : (lane + 1) * 16, :]
                wide[at, lane * LANES : (lane + 1) * LANES] = piece.astype(jnp.float32)

        @pl.when(to_root)
        def _():
            copy(t, root_hbm).start()

        @pl.when(jnp.logical_not(to_root))
        def _():
            copy(t, near_hbm).start()

        return carry

    lax.fori_loop(0, tiles, one_tile, 0)

    def finish():
        @pl.when(to_root)
        def _():
            for t in range(tiles):
                copy(t, root_hbm).wait()

        @pl.when(jnp.logical_not(to_root))
        def _():
            for t in range(tiles):
                copy(t, near_hbm).wait()

    return finish


def own_half_kernel(core_ref, kept_ref, root_hbm, near_hbm, wide, sent):
    widen(kept_ref, wide, root_hbm, near_hbm, core_ref[0] == 0, sent)()


def other_half_kernel(
    core_ref, z_ref, kept_ref, other_ref, root_in, near_in, root_hbm, near_hbm, first_root_ref,
    first_near_ref, bias_two_ref, bias_one_ref, wide, sent,
):
    del root_in, near_in
    core, z = core_ref[0], z_ref[0]
    even = core == 0
    finish = widen(other_ref, wide, root_hbm, near_hbm, core != 0, sent)
    here = lax.shift_right_logical(z, 1) == core
    base = lax.bitwise_and(z, 1) * 4
    for j, to_ref in enumerate((first_root_ref, first_near_ref)):
        for i in range(2):
            for lane in range(8):
                chunk = (base + 2 * j + i) * 8 + lane
                kept = kept_ref[chunk, LANES : LANES + 16, :].astype(jnp.float32)
                other = other_ref[chunk, LANES : LANES + 16, :].astype(jnp.float32)
                at, cols = slice(i * 16, (i + 1) * 16), slice(lane * LANES, (lane + 1) * LANES)
                to_ref[at, cols] = jnp.where(here, kept, other)
    for lane in range(8):
        kept = kept_ref[lane, LANES + 16 :, :].astype(jnp.float32)[0:1, :]
        other = other_ref[lane, LANES + 16 :, :].astype(jnp.float32)[0:1, :]
        cols = slice(lane * LANES, (lane + 1) * LANES)
        bias_two_ref[:, cols] = jnp.where(even, kept, other)
        bias_one_ref[:, cols] = jnp.where(even, other, kept)
    finish()


def spread(core, z, kept, hidden_width):
    f32 = jnp.float32
    square = shaped(hidden_width, hidden_width, dtype=f32)
    slab = shaped(32, hidden_width, dtype=f32)
    line = shaped(1, hidden_width, dtype=f32)
    scratch = [pltpu.VMEM(square.shape, f32), pltpu.SemaphoreType.DMA((hidden_width // LANES,))]
    other = lax.ppermute(kept, "core", [(0, 1), (1, 0)])
    root, near = pl.pallas_call(
        own_half_kernel,
        out_shape=(square, square),
        in_specs=[SMEM, VMEM],
        out_specs=(HBM, HBM),
        scratch_shapes=scratch,
        name="own_half",
        compiler_params=pltpu.CompilerParams(vmem_limit_bytes=8 << 20),
        cost_estimate=pl.CostEstimate(flops=1_000_000, bytes_accessed=7_000_000, transcendentals=0),
    )(core, kept)
    return pl.pallas_call(
        other_half_kernel,
        out_shape=(square, square, slab, slab, line, line),
        in_specs=[SMEM, SMEM, VMEM, VMEM, HBM, HBM],
        out_specs=(HBM, HBM) + (VMEM,) * 4,
        scratch_shapes=scratch,
        input_output_aliases={4: 0, 5: 1},
        name="other_half",
        compiler_params=pltpu.CompilerParams(vmem_limit_bytes=8 << 20),
        cost_estimate=pl.CostEstimate(flops=1_000_000, bytes_accessed=9_000_000, transcendentals=0),
    )(core, z, kept, other, root, near)


def weights_of_pair(own, z):
    first = lax.ppermute(own, "z", [(0, 1), (1, 0), (2, 3), (3, 2)])
    odd = lax.bitwise_and(z, 1) == 1
    return jnp.concatenate([jnp.where(odd, first, own), jnp.where(odd, own, first)], axis=0)


def weights_of_others(pair):
    return lax.ppermute(pair, "z", [(0, 3), (3, 0), (1, 2), (2, 1)])


def exchange(value, axes):
    return lax.all_to_all(value, axes, split_axis=0, concat_axis=0, tiled=True)


def step(
    features,
    first_adjacent,
    first_center,
    first_count,
    owner_map,
    first_root,
    first_near,
    first_bias,
    second_adjacent,
    second_center,
    second_count,
    second_root,
    second_near,
    second_bias,
    upstream,
):
    owners = 128
    hidden_width = first_root.shape[1]
    z = lax.axis_index("z")
    core = lax.axis_index("core")[None]
    pair = weights_of_pair(jnp.concatenate([first_root, first_near], axis=0), z)
    columns = jnp.concatenate([first_center[:, None], first_adjacent], axis=1).T
    packed = aggregate(features, columns, first_count[None], owner_map[None], owners)
    packed, pair = lax.optimization_barrier((packed, pair))
    other_pair = weights_of_others(pair)
    arrived = exchange(packed, AXES)
    count = second_count[:, None]
    picked, flipped = picks(second_adjacent, second_center[:, None], count, owners * 8)
    slots, depth = picked.shape[1], 2 * pair.shape[0]
    nodes = upstream.shape[0]
    layer_output, sent_two, hidden, rows, slope, inputs_flip, bias_grad = call(
        forward_kernel,
        (
            shaped(nodes, hidden_width),
            shaped(64, LANES, LANES),
            shaped(slots, hidden_width),
            shaped(2 * nodes, hidden_width),
            shaped(nodes, hidden_width),
            shaped(depth, slots),
            shaped(8, hidden_width, dtype=jnp.float32),
        ),
        12,
        smem=2,
        hbm=4,
        scratch=[
            pltpu.VMEM((slots, depth), jnp.bfloat16),
            pltpu.VMEM(picked.shape, jnp.bfloat16),
            pltpu.VMEM(second_root.shape, jnp.bfloat16),
            pltpu.VMEM(second_near.shape, jnp.bfloat16),
            pltpu.VMEM(upstream.shape, jnp.bfloat16),
            pltpu.SemaphoreType.DMA((4,)),
        ],
        limit=24,
        flops=6_000_000_000,
        moved=18_000_000,
        exps=3_000_000,
    )(
        core, z[None], arrived, pair, other_pair, first_bias[None], count, second_bias[None],
        in_hbm(picked), in_hbm(second_root), in_hbm(second_near), in_hbm(upstream),
    )
    received = lax.ppermute(sent_two, "core", [(0, 1), (1, 0)])
    kept_one, sent_one = call(
        backward_kernel, (shaped(64, 24, LANES), shaped(64, 24, LANES)), 9, smem=1,
        scratch=[
            pltpu.VMEM((2 * nodes, hidden_width), jnp.bfloat16),
            pltpu.VMEM((8, hidden_width), jnp.float32),
        ],
        limit=24, flops=4_700_000_000, moved=12_000_000, exps=1_000_000,
    )(core, slope, second_root, second_near, count, flipped, hidden, inputs_flip, bias_grad)
    received_one = lax.ppermute(sent_one, "core", [(0, 1), (1, 0)])
    (both,) = call(
        kept_kernel, (shaped(64, CHUNK, LANES),), 6, smem=1, limit=20,
        flops=1_000_000_000, moved=7_000_000,
    )(core, rows, slope, received, kept_one, received_one)
    terms = exchange(both, CHIPS)
    total = jnp.sum(terms.astype(jnp.float32), axis=0).astype(jnp.bfloat16)
    mine = exchange(jnp.broadcast_to(total[None], terms.shape), CHIPS)
    root_two, near_two, root_one, near_one, bias_two, bias_one = spread(
        core, z[None], mine, hidden_width
    )
    return (layer_output, root_two, near_two, bias_two[0], root_one, near_one, bias_one[0])


def solution(mesh):
    chips = Mesh(mesh.devices.reshape(4, 4, 4, 2), AXES)
    trainer = ("x", "y", "core")
    return jax.shard_map(
        step,
        mesh=chips,
        in_specs=(
            P("z", trainer),
            P(trainer, None),
            P(trainer),
            P(trainer),
            P(trainer),
            P("z", None),
            P("z", None),
            P(),
            P(AXES, None),
            P(AXES),
            P(AXES),
            P(),
            P(),
            P(),
            P(AXES, None),
        ),
        out_specs=(
            P(AXES, None),
            P(),
            P(),
            P(),
            P("z", None),
            P("z", None),
            P(),
        ),
        check_vma=False,
    )
```

```python
import jax
import jax.numpy as jnp
from jax import lax
from jax.experimental import pallas as pl
from jax.experimental.pallas import tpu as pltpu
from jax.sharding import Mesh, PartitionSpec as P


CAP = 32
LANES = 128
AXES = ("z", "x", "y", "core")
CHIPS = ("z", "x", "y")
CHUNK = 152
VMEM = pl.BlockSpec(memory_space=pltpu.VMEM)
ALONG_LANES = lax.GatherDimensionNumbers(
    offset_dims=(),
    collapsed_slice_dims=(1,),
    start_index_map=(1,),
    operand_batching_dims=(0,),
    start_indices_batching_dims=(0,),
)
SMEM = pl.BlockSpec(memory_space=pltpu.SMEM)
HBM = pl.BlockSpec(memory_space=pltpu.HBM)


def lanes_at(at, size=LANES):
    if isinstance(at, int):
        return slice(at * size, (at + 1) * size)
    return pl.ds(pl.multiple_of(at * size, size), size)


def across(left, right):
    return lax.dot_general(
        left, right, (((0,), (0,)), ((), ())), preferred_element_type=jnp.float32
    )


def along(left, right):
    return lax.dot_general(
        left, right, (((1,), (1,)), ((), ())), preferred_element_type=jnp.float32
    )


def matmul(left, right):
    return jnp.dot(left, right, preferred_element_type=jnp.float32)


def take_lanes(rows, index):
    return lax.gather(
        rows, index[..., None], ALONG_LANES, (1, 1), mode=lax.GatherScatterMode.PROMISE_IN_BOUNDS
    )


def find(load, high, low, chunks, parts):
    bits = [lax.bitwise_and(high, jnp.int16(1 << b)) != jnp.int16(0) for b in range(5)]

    def among(start, size, bit):
        if size == 1:
            return [take_lanes(load(start, v), low) for v in range(parts)]
        first = among(start, size // 2, bit - 1)
        last = among(start + size // 2, size // 2, bit - 1)
        return [jnp.where(bits[bit], q, p) for p, q in zip(first, last)]

    return among(0, chunks, chunks.bit_length() - 2)


def aggregate_kernel(
    adj_ref, feat_hbm, count_hbm, owner_hbm, out_ref, index, counts, rows, places, stage, wide,
    feat_ref, count_ref, owner_ref, arrivals,
):
    copies = [
        pltpu.make_async_copy(source, target, arrivals.at[number])
        for number, (source, target) in enumerate(
            ((count_hbm, count_ref), (owner_hbm, owner_ref), (feat_hbm, feat_ref))
        )
    ]
    for copy in copies:
        copy.start()
    copies[0].wait()
    width, inputs = feat_ref.shape
    nodes = owner_ref.shape[1]
    owners = out_ref.shape[0]
    fan = adj_ref.shape[0] - 1
    chunks = inputs // LANES
    groups = nodes // LANES
    parts = width // 16
    steps = (fan + 1) // 4
    i16, i32, bf16, f32 = jnp.int16, jnp.int32, jnp.bfloat16, jnp.float32
    span = 256
    before = (
        lax.broadcasted_iota(i32, (span, span), 0) < lax.broadcasted_iota(i32, (span, span), 1)
    ).astype(bf16)

    def ones(hit, axis):
        return jnp.sum(jnp.where(hit, 1.0, 0.0), axis=axis, keepdims=True)

    kinds = lax.broadcasted_iota(i32, (16, span), 0)
    blocks = [slice(b * span, (b + 1) * span) for b in range(nodes // span)]
    start = jnp.zeros((16, 1), f32)
    for at in blocks:
        start = start + ones(fan - count_ref[:, at] < kinds, 1)
    order, seen = [], start
    for at in blocks:
        hit = fan - count_ref[:, at] == kinds
        earlier = matmul(hit.astype(bf16), before) + seen
        order.append(jnp.sum(jnp.where(hit, earlier, 0.0), axis=0, keepdims=True).astype(i32))
        seen = seen + ones(hit, 1)
    node_at = jnp.zeros((2 * groups, LANES), f32)
    group_ids = lax.broadcasted_iota(i32, (groups, span), 0)
    lane_ids = lax.broadcasted_iota(i32, (LANES, span), 0)
    for b, place in enumerate(order):
        node = lax.broadcasted_iota(i32, (groups, span), 1) + b * span
        mine = group_ids == lax.shift_right_logical(place, 7)
        weights = jnp.concatenate(
            [
                jnp.where(mine, lax.shift_right_logical(node, 7), 0).astype(f32),
                jnp.where(mine, lax.bitwise_and(node, LANES - 1), 0).astype(f32),
            ],
            axis=0,
        ).astype(bf16)
        picked = (lane_ids == lax.bitwise_and(place, LANES - 1)).astype(bf16)
        node_at = node_at + along(weights, picked)
    node_at = node_at.astype(i32)
    for g in range(groups):
        high = jnp.broadcast_to(node_at[g : g + 1], (16, LANES)).astype(i16)
        low = jnp.broadcast_to(node_at[groups + g : groups + g + 1], (16, LANES)).astype(i16)
        (columns,) = find(
            lambda c, v: adj_ref[:, c * LANES : (c + 1) * LANES].astype(i16), high, low, groups, 1
        )
        columns = columns.astype(i32)
        for s in range(steps):
            index[g * steps + s, 0:4] = columns[s * 4 : s * 4 + 4]
        place = lax.broadcasted_iota(i32, (16, LANES), 1) + g * LANES
        counts[g] = (fan + 1) - ones(start.astype(i32) <= place, 0).astype(i32)

    copies[1].wait()
    copies[2].wait()

    def one_group(g, carry):
        count = counts[g]

        def four(s, total, first):
            total = list(total)
            for j in range(4):
                at = index[g * steps + s, j : j + 1, :]
                high = jnp.broadcast_to(lax.shift_right_logical(at, 7), (16, LANES)).astype(i16)
                low = jnp.broadcast_to(lax.bitwise_and(at, LANES - 1), (16, LANES)).astype(i16)
                found = find(
                    lambda c, v: feat_ref[v * 16 : (v + 1) * 16, c * LANES : (c + 1) * LANES],
                    high, low, chunks, parts,
                )
                if first and j == 0:
                    for v in range(parts):
                        rows[v * 16 : (v + 1) * 16, lanes_at(g)] = found[v]
                    continue
                valid = jnp.broadcast_to(s * 4 + j <= count, (16, LANES))
                for v in range(parts):
                    total[v] = total[v] + jnp.where(valid, found[v].astype(f32), 0.0)
            return tuple(total)

        total = four(0, (jnp.zeros((16, LANES), f32),) * parts, True)
        needed = lax.shift_right_logical(jnp.max(count) + 4, 2)
        total = lax.fori_loop(1, needed, lambda s, t: four(s, t, False), total)
        divisor = jnp.broadcast_to(count.astype(f32), (16, LANES))
        for v in range(parts):
            near = (total[v] / divisor).astype(bf16)
            rows[width + v * 16 : width + (v + 1) * 16, lanes_at(g)] = near
        return carry

    lax.fori_loop(0, groups, one_group, 0)

    owner_ids = lax.broadcasted_iota(i32, (owners, span), 0)
    ranks = lax.broadcasted_iota(i32, (CAP, span), 0)
    seen = jnp.zeros((owners, 1), f32)
    found_at = jnp.zeros((3 * CAP, owners), f32)
    for at, place in zip(blocks, order):
        hit = owner_ids == owner_ref[:, at]
        picked = hit.astype(bf16)
        earlier = matmul(picked, before) + seen
        rank = jnp.sum(jnp.where(hit, earlier, 0.0), axis=0, keepdims=True).astype(i32)
        seen = seen + ones(hit, 1)
        mine = ranks == rank
        weights = jnp.concatenate(
            [
                jnp.where(mine, lax.shift_right_logical(place, 7), 0).astype(f32),
                jnp.where(mine, lax.bitwise_and(place, LANES - 1), 0).astype(f32),
                jnp.where(mine, 1.0, 0.0),
            ],
            axis=0,
        ).astype(bf16)
        found_at = found_at + along(weights, picked)
    found_at = found_at.astype(i32)
    for q in range(CAP // 4):
        for kind in range(3):
            at = kind * CAP + q * 4
            places[q, kind * 4 : (kind + 1) * 4] = found_at[at : at + 4]

    half = 2 * width

    def four_ranks(q, carry):
        for j in range(4):
            high = jnp.broadcast_to(places[q, j : j + 1, :], (16, owners)).astype(i16)
            low = jnp.broadcast_to(places[q, 4 + j : 5 + j, :], (16, owners)).astype(i16)
            filled = jnp.broadcast_to(places[q, 8 + j : 9 + j, :], (16, owners)) > 0
            found = find(
                lambda c, v: rows[v * 16 : (v + 1) * 16, c * LANES : (c + 1) * LANES],
                high, low, groups, half // 16,
            )
            for v in range(half // 16):
                at = (j % 2) * half + v * 16
                stage[j // 2, at : at + 16, :] = jnp.where(filled, found[v].astype(f32), 0.0)
        for pair in range(2):
            wide[pl.ds(q * 2 + pair, owners, stride=16), :] = stage[pair].T
        return carry

    lax.fori_loop(0, CAP // 4, four_ranks, 0)

    def finish(t, carry):
        at = pl.ds(pl.multiple_of(t * 8, 8), 8)
        out_ref[at] = wide[lanes_at(t), :].astype(bf16).reshape(8, 16, LANES)
        return carry

    lax.fori_loop(0, owners // 8, finish, 0)


def aggregate(features, adjacent, count, owner, owners):
    width, _ = features.shape
    nodes = owner.shape[1]
    return pl.pallas_call(
        aggregate_kernel,
        out_shape=jax.ShapeDtypeStruct((owners, 16, LANES), jnp.bfloat16),
        in_specs=[VMEM] + [HBM] * 3,
        out_specs=VMEM,
        scratch_shapes=[
            pltpu.VMEM((nodes // LANES * 4, 4, LANES), jnp.int32),
            pltpu.VMEM((nodes // LANES, 1, LANES), jnp.int32),
            pltpu.VMEM((2 * width, nodes), jnp.bfloat16),
            pltpu.VMEM((CAP // 4, 12, LANES), jnp.int32),
            pltpu.VMEM((2, 4 * width, owners), jnp.float32),
            pltpu.VMEM((16 * owners, LANES), jnp.float32),
            pltpu.VMEM(features.shape, jnp.bfloat16),
            pltpu.VMEM(count.shape, jnp.int32),
            pltpu.VMEM(owner.shape, jnp.int32),
            pltpu.SemaphoreType.DMA((3,)),
        ],
        name="aggregate",
        compiler_params=pltpu.CompilerParams(vmem_limit_bytes=12 << 20),
        cost_estimate=pl.CostEstimate(flops=40_000_000, bytes_accessed=3_000_000, transcendentals=0),
    )(adjacent, in_hbm(features), in_hbm(count), in_hbm(owner))


def picks_kernel(adj_ref, center_ref, count_ref, out_ref, flip_ref):
    nodes, fan = adj_ref.shape
    slots = out_ref.shape[1]

    def table_row(slot):
        odd = lax.shift_left(lax.bitwise_and(slot, 1), 4)
        pair = lax.bitwise_and(lax.shift_right_logical(slot, 1), 15)
        return lax.bitwise_and(slot, -CAP) + odd + pair

    def one_tile(t, carry):
        at = pl.ds(pl.multiple_of(t * 16, 16), 16)
        number = lax.broadcasted_iota(jnp.int32, (16, fan), 1)
        adjacent = jnp.where(number < count_ref[at, :], table_row(adj_ref[at, :]), -1)
        center = jnp.broadcast_to(table_row(center_ref[at, :]), (16, LANES))
        spread = [jnp.broadcast_to(adjacent[:, k : k + 1], (16, LANES)) for k in range(fan)]
        for c in range(slots // LANES):
            ids = lax.broadcasted_iota(jnp.int32, (16, LANES), 1) + c * LANES
            total = jnp.zeros((16, LANES), jnp.float32)
            for k in range(fan):
                total = total + jnp.where(spread[k] == ids, 1.0, 0.0)
            out_ref[at, c * LANES : (c + 1) * LANES] = jnp.where(center == ids, 1.0, 0.0).astype(
                out_ref.dtype
            )
            low = pl.ds(pl.multiple_of(nodes + t * 16, 16), 16)
            out_ref[low, c * LANES : (c + 1) * LANES] = total.astype(out_ref.dtype)
        return carry

    lax.fori_loop(0, nodes // 16, one_tile, 0)

    def one_flip(t, carry):
        flip_ref[:, lanes_at(t)] = out_ref[lanes_at(t), :].T
        return carry

    lax.fori_loop(0, 2 * nodes // LANES, one_flip, 0)


def picks(adjacent, center, count, slots):
    nodes = adjacent.shape[0]
    return pl.pallas_call(
        picks_kernel,
        out_shape=(
            jax.ShapeDtypeStruct((2 * nodes, slots), jnp.bfloat16),
            jax.ShapeDtypeStruct((slots, 2 * nodes), jnp.bfloat16),
        ),
        in_specs=[VMEM] * 3,
        out_specs=(VMEM, VMEM),
        name="picks",
        compiler_params=pltpu.CompilerParams(vmem_limit_bytes=12 << 20),
        cost_estimate=pl.CostEstimate(flops=20_000_000, bytes_accessed=5_000_000, transcendentals=0),
    )(adjacent, center, count)


def call(kernel, outs, ins, smem=0, hbm=0, scratch=(), limit=16, flops=0, moved=0, exps=0):
    return pl.pallas_call(
        kernel,
        out_shape=outs,
        in_specs=[SMEM] * smem + [VMEM] * (ins - smem - hbm) + [HBM] * hbm,
        out_specs=(VMEM,) * len(outs),
        scratch_shapes=scratch,
        compiler_params=pltpu.CompilerParams(vmem_limit_bytes=limit << 20),
        cost_estimate=pl.CostEstimate(flops=flops, bytes_accessed=moved, transcendentals=exps),
    )


def in_hbm(value):
    return pltpu.with_memory_space_constraint(value, pltpu.HBM)


def put_chunks(to_ref, t, product):
    for c in range(product.shape[0] // 16):
        for lane in range(product.shape[1] // LANES):
            to_ref[t * (product.shape[0] // 16) + c, lane * 16 : (lane + 1) * 16, :] = product[
                c * 16 : (c + 1) * 16, lane * LANES : (lane + 1) * LANES
            ]


def forward_kernel(
    core_ref, z_ref, arrived_ref, pair_ref, other_pair_ref, bias_one_ref, count_ref, bias_two_ref,
    picks_hbm, root_hbm, near_hbm, upstream_hbm, out_ref, sent_ref, hidden, rows, slope,
    inputs_flip, bias_grad, inputs, picks_ref, root_ref, near_ref, upstream_ref, arrivals,
):
    copies = [
        pltpu.make_async_copy(source, target, arrivals.at[number])
        for number, (source, target) in enumerate(
            (
                (picks_hbm, picks_ref),
                (root_hbm, root_ref),
                (near_hbm, near_ref),
                (upstream_hbm, upstream_ref),
            )
        )
    ]
    for copy in copies:
        copy.start()
    slots, depth = inputs.shape
    hidden_width = hidden.shape[1]
    nodes = slope.shape[0]
    quarter = depth // 4
    sources = slots // CAP
    tile = 256

    def one_source(t, carry):
        for e in range(2):
            pieces = [
                arrived_ref[f * sources + t, :, e * quarter : (e + 1) * quarter] for f in range(4)
            ]
            at = pl.ds(pl.multiple_of(t * CAP + e * 16, 16), 16)
            inputs[at, :] = jnp.concatenate(pieces, axis=1)
        return carry

    lax.fori_loop(0, sources, one_source, 0)
    for t in range(slots // tile):
        inputs_flip[:, t * tile : (t + 1) * tile] = inputs[t * tile : (t + 1) * tile, :].T

    late = z_ref[0] >= 2

    def first_layer(t, carry):
        cols = lanes_at(t, tile)
        pair, other = pair_ref[:, cols], other_pair_ref[:, cols]
        pre = matmul(inputs[:, : depth // 2], jnp.where(late, other, pair))
        pre = pre + matmul(inputs[:, depth // 2 :], jnp.where(late, pair, other))
        pre = pre + bias_one_ref[:, cols]
        value = jnp.maximum(pre, 0.0) + jnp.log1p(jnp.exp(-jnp.abs(pre)))
        hidden[:, cols] = value.astype(jnp.bfloat16)
        return carry

    inverse = 1.0 / count_ref[...].astype(jnp.float32)

    def select(t, carry):
        cols = lanes_at(t, tile)
        rows[:nodes, cols] = matmul(picks_ref[:nodes, :], hidden[:, cols]).astype(jnp.bfloat16)
        total = matmul(picks_ref[nodes:, :], hidden[:, cols])
        rows[nodes:, cols] = (total * inverse).astype(jnp.bfloat16)
        return carry

    lax.fori_loop(0, hidden_width // tile, first_layer, 0)
    copies[0].wait()
    lax.fori_loop(0, hidden_width // tile, select, 0)
    for copy in copies[1:]:
        copy.wait()

    def second_layer(t, carry):
        cols = lanes_at(t, tile)
        pre = matmul(rows[:nodes, :], root_ref[:, cols]) + matmul(rows[nodes:, :], near_ref[:, cols])
        pre = pre + bias_two_ref[:, cols]
        gate = jax.nn.sigmoid(pre)
        out_ref[:, cols] = (pre * gate).astype(jnp.bfloat16)
        grad = upstream_ref[:, cols].astype(jnp.float32) * gate * (1.0 + pre * (1.0 - gate))
        grad = grad.astype(jnp.bfloat16)
        slope[:, cols] = grad
        bias_grad[0:1, cols] = jnp.sum(grad.astype(jnp.float32), axis=0, keepdims=True)
        return carry

    for t in range(hidden_width // tile):
        second_layer(t, 0)
    start = (core_ref[0] ^ 1) * nodes

    def weight_grads(t, carry):
        left = rows[pl.ds(pl.multiple_of(start, nodes), nodes), lanes_at(t, tile)]
        put_chunks(sent_ref, t, across(left, slope[...]).astype(jnp.bfloat16))
        return carry

    lax.fori_loop(0, hidden_width // tile, weight_grads, 0)


def kept_kernel(
    core_ref, rows_ref, slope_ref, received_ref, kept_one_ref, received_one_ref, both_ref
):
    nodes, hidden_width = slope_ref.shape
    tile = 256
    start = core_ref[0] * nodes

    def weight_grads(t, carry):
        left = rows_ref[pl.ds(pl.multiple_of(start, nodes), nodes), lanes_at(t, tile)]
        product = across(left, slope_ref[...])
        for c in range(tile // 16):
            chunk = t * (tile // 16) + c
            for lane in range(hidden_width // LANES):
                at = slice(lane * 16, (lane + 1) * 16)
                mine = product[c * 16 : (c + 1) * 16, lane * LANES : (lane + 1) * LANES]
                other = received_ref[chunk, at, :].astype(jnp.float32)
                both_ref[chunk, at, :] = (mine + other).astype(jnp.bfloat16)
            mine = kept_one_ref[chunk].astype(jnp.float32)
            other = received_one_ref[chunk].astype(jnp.float32)
            both_ref[chunk, LANES:, :] = (mine + other).astype(jnp.bfloat16)
        return carry

    lax.fori_loop(0, hidden_width // tile, weight_grads, 0)


def backward_kernel(
    core_ref, slope_ref, root_ref, near_ref, count_ref, flip_ref, hidden_ref, inputs_flip_ref,
    bias_two_ref, kept_ref, sent_ref, back, bias_grads,
):
    core = core_ref[0]
    nodes, hidden_width = slope_ref.shape
    tile = 256
    bias_grads[0:1, :] = bias_two_ref[0:1, :]
    inverse = 1.0 / count_ref[...].astype(jnp.float32)

    def backward(t, carry):
        cols = lanes_at(t, tile)
        back[:nodes, cols] = along(slope_ref[...], root_ref[cols, :]).astype(jnp.bfloat16)
        near = along(slope_ref[...], near_ref[cols, :])
        back[nodes:, cols] = (near * inverse).astype(jnp.bfloat16)
        return carry

    lax.fori_loop(0, hidden_width // tile, backward, 0)

    def first_grads(t, carry):
        cols = lanes_at(t, tile)
        table_grad = matmul(flip_ref[...], back[:, cols])
        grad = table_grad * (1.0 - jnp.exp(-hidden_ref[:, cols].astype(jnp.float32)))
        grad = grad.astype(jnp.bfloat16)
        bias_grads[1:2, cols] = jnp.sum(grad.astype(jnp.float32), axis=0, keepdims=True)
        product = matmul(inputs_flip_ref[...], grad).astype(jnp.bfloat16)
        low, high = product[:LANES], product[LANES:]
        mine, partner = jnp.where(core == 0, low, high), jnp.where(core == 0, high, low)
        for to_ref, product in ((kept_ref, mine), (sent_ref, partner)):
            for c in range(8):
                for lane in range(tile // LANES):
                    chunk = c * 8 + t * (tile // LANES) + lane
                    to_ref[chunk, 0:16, :] = product[
                        c * 16 : (c + 1) * 16, lane * LANES : (lane + 1) * LANES
                    ]
        return carry

    lax.fori_loop(0, hidden_width // tile, first_grads, 0)
    for place, to_ref in enumerate((kept_ref, sent_ref)):
        which = core ^ place
        to_ref[:, 16:, :] = jnp.zeros((to_ref.shape[0], 8, LANES), jnp.bfloat16)
        for lane in range(8):
            cols = slice(lane * LANES, (lane + 1) * LANES)
            row = jnp.where(which == 0, bias_grads[0:1, cols], bias_grads[1:2, cols])
            to_ref[lane, 16:, :] = jnp.broadcast_to(row, (8, LANES)).astype(jnp.bfloat16)


def shaped(*shape, dtype=jnp.bfloat16):
    return jax.ShapeDtypeStruct(shape, dtype)


def widen(from_ref, wide, root_hbm, near_hbm, to_root, sent):
    tiles = wide.shape[0] // LANES

    def copy(t, target):
        return pltpu.make_async_copy(wide.at[lanes_at(t)], target.at[lanes_at(t)], sent.at[t])

    def one_tile(t, carry):
        for c in range(8):
            at = pl.ds(pl.multiple_of(t * LANES + c * 16, 16), 16)
            for lane in range(8):
                piece = from_ref[t * 8 + c, lane * 16 : (lane + 1) * 16, :]
                wide[at, lane * LANES : (lane + 1) * LANES] = piece.astype(jnp.float32)

        @pl.when(to_root)
        def _():
            copy(t, root_hbm).start()

        @pl.when(jnp.logical_not(to_root))
        def _():
            copy(t, near_hbm).start()

        return carry

    lax.fori_loop(0, tiles, one_tile, 0)

    def finish():
        @pl.when(to_root)
        def _():
            for t in range(tiles):
                copy(t, root_hbm).wait()

        @pl.when(jnp.logical_not(to_root))
        def _():
            for t in range(tiles):
                copy(t, near_hbm).wait()

    return finish


def own_half_kernel(core_ref, kept_ref, root_hbm, near_hbm, wide, sent):
    widen(kept_ref, wide, root_hbm, near_hbm, core_ref[0] == 0, sent)()


def other_half_kernel(
    core_ref, z_ref, kept_ref, other_ref, root_in, near_in, root_hbm, near_hbm, first_root_ref,
    first_near_ref, bias_two_ref, bias_one_ref, wide, sent,
):
    del root_in, near_in
    core, z = core_ref[0], z_ref[0]
    even = core == 0
    finish = widen(other_ref, wide, root_hbm, near_hbm, core != 0, sent)
    here = lax.shift_right_logical(z, 1) == core
    base = lax.bitwise_and(z, 1) * 4
    for j, to_ref in enumerate((first_root_ref, first_near_ref)):
        for i in range(2):
            for lane in range(8):
                chunk = (base + 2 * j + i) * 8 + lane
                kept = kept_ref[chunk, LANES : LANES + 16, :].astype(jnp.float32)
                other = other_ref[chunk, LANES : LANES + 16, :].astype(jnp.float32)
                at, cols = slice(i * 16, (i + 1) * 16), slice(lane * LANES, (lane + 1) * LANES)
                to_ref[at, cols] = jnp.where(here, kept, other)
    for lane in range(8):
        kept = kept_ref[lane, LANES + 16 :, :].astype(jnp.float32)[0:1, :]
        other = other_ref[lane, LANES + 16 :, :].astype(jnp.float32)[0:1, :]
        cols = slice(lane * LANES, (lane + 1) * LANES)
        bias_two_ref[:, cols] = jnp.where(even, kept, other)
        bias_one_ref[:, cols] = jnp.where(even, other, kept)
    finish()


def spread(core, z, kept, hidden_width):
    f32 = jnp.float32
    square = shaped(hidden_width, hidden_width, dtype=f32)
    slab = shaped(32, hidden_width, dtype=f32)
    line = shaped(1, hidden_width, dtype=f32)
    scratch = [pltpu.VMEM(square.shape, f32), pltpu.SemaphoreType.DMA((hidden_width // LANES,))]
    other = lax.ppermute(kept, "core", [(0, 1), (1, 0)])
    root, near = pl.pallas_call(
        own_half_kernel,
        out_shape=(square, square),
        in_specs=[SMEM, VMEM],
        out_specs=(HBM, HBM),
        scratch_shapes=scratch,
        name="own_half",
        compiler_params=pltpu.CompilerParams(vmem_limit_bytes=8 << 20),
        cost_estimate=pl.CostEstimate(flops=1_000_000, bytes_accessed=7_000_000, transcendentals=0),
    )(core, kept)
    return pl.pallas_call(
        other_half_kernel,
        out_shape=(square, square, slab, slab, line, line),
        in_specs=[SMEM, SMEM, VMEM, VMEM, HBM, HBM],
        out_specs=(HBM, HBM) + (VMEM,) * 4,
        scratch_shapes=scratch,
        input_output_aliases={4: 0, 5: 1},
        name="other_half",
        compiler_params=pltpu.CompilerParams(vmem_limit_bytes=8 << 20),
        cost_estimate=pl.CostEstimate(flops=1_000_000, bytes_accessed=9_000_000, transcendentals=0),
    )(core, z, kept, other, root, near)


def weights_of_pair(own, z):
    first = lax.ppermute(own, "z", [(0, 1), (1, 0), (2, 3), (3, 2)])
    odd = lax.bitwise_and(z, 1) == 1
    return jnp.concatenate([jnp.where(odd, first, own), jnp.where(odd, own, first)], axis=0)


def weights_of_others(pair):
    return lax.ppermute(pair, "z", [(0, 3), (3, 0), (1, 2), (2, 1)])


def exchange(value, axes):
    return lax.all_to_all(value, axes, split_axis=0, concat_axis=0, tiled=True)


def step(
    features,
    first_adjacent,
    first_center,
    first_count,
    owner_map,
    first_root,
    first_near,
    first_bias,
    second_adjacent,
    second_center,
    second_count,
    second_root,
    second_near,
    second_bias,
    upstream,
):
    owners = 128
    hidden_width = first_root.shape[1]
    z = lax.axis_index("z")
    core = lax.axis_index("core")[None]
    pair = weights_of_pair(jnp.concatenate([first_root, first_near], axis=0), z)
    columns = jnp.concatenate([first_center[:, None], first_adjacent], axis=1).T
    packed = aggregate(features, columns, first_count[None], owner_map[None], owners)
    packed, pair = lax.optimization_barrier((packed, pair))
    other_pair = weights_of_others(pair)
    arrived = exchange(packed, AXES)
    count = second_count[:, None]
    picked, flipped = picks(second_adjacent, second_center[:, None], count, owners * 8)
    slots, depth = picked.shape[1], 2 * pair.shape[0]
    nodes = upstream.shape[0]
    layer_output, sent_two, hidden, rows, slope, inputs_flip, bias_grad = call(
        forward_kernel,
        (
            shaped(nodes, hidden_width),
            shaped(64, LANES, LANES),
            shaped(slots, hidden_width),
            shaped(2 * nodes, hidden_width),
            shaped(nodes, hidden_width),
            shaped(depth, slots),
            shaped(8, hidden_width, dtype=jnp.float32),
        ),
        12,
        smem=2,
        hbm=4,
        scratch=[
            pltpu.VMEM((slots, depth), jnp.bfloat16),
            pltpu.VMEM(picked.shape, jnp.bfloat16),
            pltpu.VMEM(second_root.shape, jnp.bfloat16),
            pltpu.VMEM(second_near.shape, jnp.bfloat16),
            pltpu.VMEM(upstream.shape, jnp.bfloat16),
            pltpu.SemaphoreType.DMA((4,)),
        ],
        limit=24,
        flops=6_000_000_000,
        moved=18_000_000,
        exps=3_000_000,
    )(
        core, z[None], arrived, pair, other_pair, first_bias[None], count, second_bias[None],
        in_hbm(picked), in_hbm(second_root), in_hbm(second_near), in_hbm(upstream),
    )
    received = lax.ppermute(sent_two, "core", [(0, 1), (1, 0)])
    kept_one, sent_one = call(
        backward_kernel, (shaped(64, 24, LANES), shaped(64, 24, LANES)), 9, smem=1,
        scratch=[
            pltpu.VMEM((2 * nodes, hidden_width), jnp.bfloat16),
            pltpu.VMEM((8, hidden_width), jnp.float32),
        ],
        limit=24, flops=4_700_000_000, moved=12_000_000, exps=1_000_000,
    )(core, slope, second_root, second_near, count, flipped, hidden, inputs_flip, bias_grad)
    received_one = lax.ppermute(sent_one, "core", [(0, 1), (1, 0)])
    (both,) = call(
        kept_kernel, (shaped(64, CHUNK, LANES),), 6, smem=1, limit=20,
        flops=1_000_000_000, moved=7_000_000,
    )(core, rows, slope, received, kept_one, received_one)
    terms = exchange(both, CHIPS)
    total = jnp.sum(terms.astype(jnp.float32), axis=0).astype(jnp.bfloat16)
    mine = exchange(jnp.broadcast_to(total[None], terms.shape), CHIPS)
    root_two, near_two, root_one, near_one, bias_two, bias_one = spread(
        core, z[None], mine, hidden_width
    )
    return (layer_output, root_two, near_two, bias_two[0], root_one, near_one, bias_one[0])


def solution(mesh):
    chips = Mesh(mesh.devices.reshape(4, 4, 4, 2), AXES)
    trainer = ("x", "y", "core")
    return jax.shard_map(
        step,
        mesh=chips,
        in_specs=(
            P("z", trainer),
            P(trainer, None),
            P(trainer),
            P(trainer),
            P(trainer),
            P("z", None),
            P("z", None),
            P(),
            P(AXES, None),
            P(AXES),
            P(AXES),
            P(),
            P(),
            P(),
            P(AXES, None),
        ),
        out_specs=(
            P(AXES, None),
            P(),
            P(),
            P(),
            P("z", None),
            P("z", None),
            P(),
        ),
        check_vma=False,
    )
```

```python
import jax
import jax.numpy as jnp
from jax import lax
from jax.experimental import pallas as pl
from jax.experimental.pallas import tpu as pltpu
from jax.sharding import Mesh, PartitionSpec as P


CAP = 32
LANES = 128
AXES = ("z", "x", "y", "core")
CHIPS = ("z", "x", "y")
CHUNK = 152
VMEM = pl.BlockSpec(memory_space=pltpu.VMEM)
ALONG_LANES = lax.GatherDimensionNumbers(
    offset_dims=(),
    collapsed_slice_dims=(1,),
    start_index_map=(1,),
    operand_batching_dims=(0,),
    start_indices_batching_dims=(0,),
)
SMEM = pl.BlockSpec(memory_space=pltpu.SMEM)
HBM = pl.BlockSpec(memory_space=pltpu.HBM)


def lanes_at(at, size=LANES):
    if isinstance(at, int):
        return slice(at * size, (at + 1) * size)
    return pl.ds(pl.multiple_of(at * size, size), size)


def across(left, right):
    return lax.dot_general(
        left, right, (((0,), (0,)), ((), ())), preferred_element_type=jnp.float32
    )


def along(left, right):
    return lax.dot_general(
        left, right, (((1,), (1,)), ((), ())), preferred_element_type=jnp.float32
    )


def matmul(left, right):
    return jnp.dot(left, right, preferred_element_type=jnp.float32)


def take_lanes(rows, index):
    return lax.gather(
        rows, index[..., None], ALONG_LANES, (1, 1), mode=lax.GatherScatterMode.PROMISE_IN_BOUNDS
    )


def find(load, high, low, chunks, parts):
    bits = [lax.bitwise_and(high, jnp.int16(1 << b)) != jnp.int16(0) for b in range(5)]

    def among(start, size, bit):
        if size == 1:
            return [take_lanes(load(start, v), low) for v in range(parts)]
        first = among(start, size // 2, bit - 1)
        last = among(start + size // 2, size // 2, bit - 1)
        return [jnp.where(bits[bit], q, p) for p, q in zip(first, last)]

    return among(0, chunks, chunks.bit_length() - 2)


def aggregate_kernel(
    adj_ref, feat_hbm, count_hbm, owner_hbm, out_ref, index, counts, rows, places, stage, wide,
    feat_ref, count_ref, owner_ref, arrivals,
):
    copies = [
        pltpu.make_async_copy(source, target, arrivals.at[number])
        for number, (source, target) in enumerate(
            ((count_hbm, count_ref), (owner_hbm, owner_ref), (feat_hbm, feat_ref))
        )
    ]
    for copy in copies:
        copy.start()
    copies[0].wait()
    width, inputs = feat_ref.shape
    nodes = owner_ref.shape[1]
    owners = out_ref.shape[0]
    fan = adj_ref.shape[0] - 1
    chunks = inputs // LANES
    groups = nodes // LANES
    parts = width // 16
    steps = (fan + 1) // 4
    i16, i32, bf16, f32 = jnp.int16, jnp.int32, jnp.bfloat16, jnp.float32
    span = 256
    before = (
        lax.broadcasted_iota(i32, (span, span), 0) < lax.broadcasted_iota(i32, (span, span), 1)
    ).astype(bf16)

    def ones(hit, axis):
        return jnp.sum(jnp.where(hit, 1.0, 0.0), axis=axis, keepdims=True)

    kinds = lax.broadcasted_iota(i32, (16, span), 0)
    blocks = [slice(b * span, (b + 1) * span) for b in range(nodes // span)]
    start = jnp.zeros((16, 1), f32)
    for at in blocks:
        start = start + ones(fan - count_ref[:, at] < kinds, 1)
    order, seen = [], start
    for at in blocks:
        hit = fan - count_ref[:, at] == kinds
        earlier = matmul(hit.astype(bf16), before) + seen
        order.append(jnp.sum(jnp.where(hit, earlier, 0.0), axis=0, keepdims=True).astype(i32))
        seen = seen + ones(hit, 1)
    node_at = jnp.zeros((2 * groups, LANES), f32)
    group_ids = lax.broadcasted_iota(i32, (groups, span), 0)
    lane_ids = lax.broadcasted_iota(i32, (LANES, span), 0)
    for b, place in enumerate(order):
        node = lax.broadcasted_iota(i32, (groups, span), 1) + b * span
        mine = group_ids == lax.shift_right_logical(place, 7)
        weights = jnp.concatenate(
            [
                jnp.where(mine, lax.shift_right_logical(node, 7), 0).astype(f32),
                jnp.where(mine, lax.bitwise_and(node, LANES - 1), 0).astype(f32),
            ],
            axis=0,
        ).astype(bf16)
        picked = (lane_ids == lax.bitwise_and(place, LANES - 1)).astype(bf16)
        node_at = node_at + along(weights, picked)
    node_at = node_at.astype(i32)
    for g in range(groups):
        high = jnp.broadcast_to(node_at[g : g + 1], (16, LANES)).astype(i16)
        low = jnp.broadcast_to(node_at[groups + g : groups + g + 1], (16, LANES)).astype(i16)
        (columns,) = find(
            lambda c, v: adj_ref[:, c * LANES : (c + 1) * LANES].astype(i16), high, low, groups, 1
        )
        columns = columns.astype(i32)
        for s in range(steps):
            index[g * steps + s, 0:4] = columns[s * 4 : s * 4 + 4]
        place = lax.broadcasted_iota(i32, (16, LANES), 1) + g * LANES
        counts[g] = (fan + 1) - ones(start.astype(i32) <= place, 0).astype(i32)

    copies[1].wait()
    copies[2].wait()

    def one_group(g, carry):
        count = counts[g]

        def four(s, total, first):
            total = list(total)
            for j in range(4):
                at = index[g * steps + s, j : j + 1, :]
                high = jnp.broadcast_to(lax.shift_right_logical(at, 7), (16, LANES)).astype(i16)
                low = jnp.broadcast_to(lax.bitwise_and(at, LANES - 1), (16, LANES)).astype(i16)
                found = find(
                    lambda c, v: feat_ref[v * 16 : (v + 1) * 16, c * LANES : (c + 1) * LANES],
                    high, low, chunks, parts,
                )
                if first and j == 0:
                    for v in range(parts):
                        rows[v * 16 : (v + 1) * 16, lanes_at(g)] = found[v]
                    continue
                valid = jnp.broadcast_to(s * 4 + j <= count, (16, LANES))
                for v in range(parts):
                    total[v] = total[v] + jnp.where(valid, found[v].astype(f32), 0.0)
            return tuple(total)

        total = four(0, (jnp.zeros((16, LANES), f32),) * parts, True)
        needed = lax.shift_right_logical(jnp.max(count) + 4, 2)
        total = lax.fori_loop(1, needed, lambda s, t: four(s, t, False), total)
        divisor = jnp.broadcast_to(count.astype(f32), (16, LANES))
        for v in range(parts):
            near = (total[v] / divisor).astype(bf16)
            rows[width + v * 16 : width + (v + 1) * 16, lanes_at(g)] = near
        return carry

    lax.fori_loop(0, groups, one_group, 0)

    owner_ids = lax.broadcasted_iota(i32, (owners, span), 0)
    ranks = lax.broadcasted_iota(i32, (CAP, span), 0)
    seen = jnp.zeros((owners, 1), f32)
    found_at = jnp.zeros((3 * CAP, owners), f32)
    for at, place in zip(blocks, order):
        hit = owner_ids == owner_ref[:, at]
        picked = hit.astype(bf16)
        earlier = matmul(picked, before) + seen
        rank = jnp.sum(jnp.where(hit, earlier, 0.0), axis=0, keepdims=True).astype(i32)
        seen = seen + ones(hit, 1)
        mine = ranks == rank
        weights = jnp.concatenate(
            [
                jnp.where(mine, lax.shift_right_logical(place, 7), 0).astype(f32),
                jnp.where(mine, lax.bitwise_and(place, LANES - 1), 0).astype(f32),
                jnp.where(mine, 1.0, 0.0),
            ],
            axis=0,
        ).astype(bf16)
        found_at = found_at + along(weights, picked)
    found_at = found_at.astype(i32)
    for q in range(CAP // 4):
        for kind in range(3):
            at = kind * CAP + q * 4
            places[q, kind * 4 : (kind + 1) * 4] = found_at[at : at + 4]

    half = 2 * width

    def four_ranks(q, carry):
        for j in range(4):
            high = jnp.broadcast_to(places[q, j : j + 1, :], (16, owners)).astype(i16)
            low = jnp.broadcast_to(places[q, 4 + j : 5 + j, :], (16, owners)).astype(i16)
            filled = jnp.broadcast_to(places[q, 8 + j : 9 + j, :], (16, owners)) > 0
            found = find(
                lambda c, v: rows[v * 16 : (v + 1) * 16, c * LANES : (c + 1) * LANES],
                high, low, groups, half // 16,
            )
            for v in range(half // 16):
                at = (j % 2) * half + v * 16
                stage[j // 2, at : at + 16, :] = jnp.where(filled, found[v].astype(f32), 0.0)
        for pair in range(2):
            wide[pl.ds(q * 2 + pair, owners, stride=16), :] = stage[pair].T
        return carry

    lax.fori_loop(0, CAP // 4, four_ranks, 0)

    def finish(t, carry):
        at = pl.ds(pl.multiple_of(t * 8, 8), 8)
        out_ref[at] = wide[lanes_at(t), :].astype(bf16).reshape(8, 16, LANES)
        return carry

    lax.fori_loop(0, owners // 8, finish, 0)


def aggregate(features, adjacent, count, owner, owners):
    width, _ = features.shape
    nodes = owner.shape[1]
    return pl.pallas_call(
        aggregate_kernel,
        out_shape=jax.ShapeDtypeStruct((owners, 16, LANES), jnp.bfloat16),
        in_specs=[VMEM] + [HBM] * 3,
        out_specs=VMEM,
        scratch_shapes=[
            pltpu.VMEM((nodes // LANES * 4, 4, LANES), jnp.int32),
            pltpu.VMEM((nodes // LANES, 1, LANES), jnp.int32),
            pltpu.VMEM((2 * width, nodes), jnp.bfloat16),
            pltpu.VMEM((CAP // 4, 12, LANES), jnp.int32),
            pltpu.VMEM((2, 4 * width, owners), jnp.float32),
            pltpu.VMEM((16 * owners, LANES), jnp.float32),
            pltpu.VMEM(features.shape, jnp.bfloat16),
            pltpu.VMEM(count.shape, jnp.int32),
            pltpu.VMEM(owner.shape, jnp.int32),
            pltpu.SemaphoreType.DMA((3,)),
        ],
        name="aggregate",
        compiler_params=pltpu.CompilerParams(vmem_limit_bytes=12 << 20),
        cost_estimate=pl.CostEstimate(flops=40_000_000, bytes_accessed=3_000_000, transcendentals=0),
    )(adjacent, in_hbm(features), in_hbm(count), in_hbm(owner))


def picks_kernel(adj_ref, center_ref, count_ref, out_ref, flip_ref):
    nodes, fan = adj_ref.shape
    slots = out_ref.shape[1]

    def table_row(slot):
        odd = lax.shift_left(lax.bitwise_and(slot, 1), 4)
        pair = lax.bitwise_and(lax.shift_right_logical(slot, 1), 15)
        return lax.bitwise_and(slot, -CAP) + odd + pair

    def one_tile(t, carry):
        at = pl.ds(pl.multiple_of(t * 16, 16), 16)
        number = lax.broadcasted_iota(jnp.int32, (16, fan), 1)
        adjacent = jnp.where(number < count_ref[at, :], table_row(adj_ref[at, :]), -1)
        center = jnp.broadcast_to(table_row(center_ref[at, :]), (16, LANES))
        spread = [jnp.broadcast_to(adjacent[:, k : k + 1], (16, LANES)) for k in range(fan)]
        for c in range(slots // LANES):
            ids = lax.broadcasted_iota(jnp.int32, (16, LANES), 1) + c * LANES
            total = jnp.zeros((16, LANES), jnp.float32)
            for k in range(fan):
                total = total + jnp.where(spread[k] == ids, 1.0, 0.0)
            out_ref[at, c * LANES : (c + 1) * LANES] = jnp.where(center == ids, 1.0, 0.0).astype(
                out_ref.dtype
            )
            low = pl.ds(pl.multiple_of(nodes + t * 16, 16), 16)
            out_ref[low, c * LANES : (c + 1) * LANES] = total.astype(out_ref.dtype)
        return carry

    lax.fori_loop(0, nodes // 16, one_tile, 0)

    def one_flip(t, carry):
        flip_ref[:, lanes_at(t)] = out_ref[lanes_at(t), :].T
        return carry

    lax.fori_loop(0, 2 * nodes // LANES, one_flip, 0)


def picks(adjacent, center, count, slots):
    nodes = adjacent.shape[0]
    return pl.pallas_call(
        picks_kernel,
        out_shape=(
            jax.ShapeDtypeStruct((2 * nodes, slots), jnp.bfloat16),
            jax.ShapeDtypeStruct((slots, 2 * nodes), jnp.bfloat16),
        ),
        in_specs=[VMEM] * 3,
        out_specs=(VMEM, VMEM),
        name="picks",
        compiler_params=pltpu.CompilerParams(vmem_limit_bytes=12 << 20),
        cost_estimate=pl.CostEstimate(flops=20_000_000, bytes_accessed=5_000_000, transcendentals=0),
    )(adjacent, center, count)


def call(kernel, outs, ins, smem=0, hbm=0, scratch=(), limit=16, flops=0, moved=0, exps=0):
    return pl.pallas_call(
        kernel,
        out_shape=outs,
        in_specs=[SMEM] * smem + [VMEM] * (ins - smem - hbm) + [HBM] * hbm,
        out_specs=(VMEM,) * len(outs),
        scratch_shapes=scratch,
        compiler_params=pltpu.CompilerParams(vmem_limit_bytes=limit << 20),
        cost_estimate=pl.CostEstimate(flops=flops, bytes_accessed=moved, transcendentals=exps),
    )


def in_hbm(value):
    return pltpu.with_memory_space_constraint(value, pltpu.HBM)


def put_chunks(to_ref, t, product):
    for c in range(product.shape[0] // 16):
        for lane in range(product.shape[1] // LANES):
            to_ref[t * (product.shape[0] // 16) + c, lane * 16 : (lane + 1) * 16, :] = product[
                c * 16 : (c + 1) * 16, lane * LANES : (lane + 1) * LANES
            ]


def forward_kernel(
    core_ref, z_ref, arrived_ref, pair_ref, other_pair_ref, bias_one_ref, count_ref, bias_two_ref,
    picks_hbm, root_hbm, near_hbm, upstream_hbm, out_ref, sent_ref, hidden, rows, slope,
    inputs_flip, bias_grad, inputs, picks_ref, root_ref, near_ref, upstream_ref, arrivals,
):
    copies = [
        pltpu.make_async_copy(source, target, arrivals.at[number])
        for number, (source, target) in enumerate(
            (
                (picks_hbm, picks_ref),
                (root_hbm, root_ref),
                (near_hbm, near_ref),
                (upstream_hbm, upstream_ref),
            )
        )
    ]
    for copy in copies:
        copy.start()
    slots, depth = inputs.shape
    hidden_width = hidden.shape[1]
    nodes = slope.shape[0]
    quarter = depth // 4
    sources = slots // CAP
    tile = 256

    def one_source(t, carry):
        for e in range(2):
            pieces = [
                arrived_ref[f * sources + t, :, e * quarter : (e + 1) * quarter] for f in range(4)
            ]
            at = pl.ds(pl.multiple_of(t * CAP + e * 16, 16), 16)
            inputs[at, :] = jnp.concatenate(pieces, axis=1)
        return carry

    lax.fori_loop(0, sources, one_source, 0)
    for t in range(slots // tile):
        inputs_flip[:, t * tile : (t + 1) * tile] = inputs[t * tile : (t + 1) * tile, :].T

    late = z_ref[0] >= 2

    def first_layer(t, carry):
        cols = lanes_at(t, tile)
        pair, other = pair_ref[:, cols], other_pair_ref[:, cols]
        pre = matmul(inputs[:, : depth // 2], jnp.where(late, other, pair))
        pre = pre + matmul(inputs[:, depth // 2 :], jnp.where(late, pair, other))
        pre = pre + bias_one_ref[:, cols]
        value = jnp.maximum(pre, 0.0) + jnp.log1p(jnp.exp(-jnp.abs(pre)))
        hidden[:, cols] = value.astype(jnp.bfloat16)
        return carry

    inverse = 1.0 / count_ref[...].astype(jnp.float32)

    def select(t, carry):
        cols = lanes_at(t, tile)
        rows[:nodes, cols] = matmul(picks_ref[:nodes, :], hidden[:, cols]).astype(jnp.bfloat16)
        total = matmul(picks_ref[nodes:, :], hidden[:, cols])
        rows[nodes:, cols] = (total * inverse).astype(jnp.bfloat16)
        return carry

    first_layer(0, 0)
    copies[0].wait()
    for t in range(1, hidden_width // tile):
        first_layer(t, 0)
        select(t - 1, 0)
    select(hidden_width // tile - 1, 0)
    for copy in copies[1:]:
        copy.wait()

    def second_layer(t, carry):
        cols = lanes_at(t, tile)
        pre = matmul(rows[:nodes, :], root_ref[:, cols]) + matmul(rows[nodes:, :], near_ref[:, cols])
        pre = pre + bias_two_ref[:, cols]
        gate = jax.nn.sigmoid(pre)
        out_ref[:, cols] = (pre * gate).astype(jnp.bfloat16)
        grad = upstream_ref[:, cols].astype(jnp.float32) * gate * (1.0 + pre * (1.0 - gate))
        grad = grad.astype(jnp.bfloat16)
        slope[:, cols] = grad
        bias_grad[0:1, cols] = jnp.sum(grad.astype(jnp.float32), axis=0, keepdims=True)
        return carry

    for t in range(hidden_width // tile):
        second_layer(t, 0)
    start = (core_ref[0] ^ 1) * nodes

    def weight_grads(t, carry):
        left = rows[pl.ds(pl.multiple_of(start, nodes), nodes), lanes_at(t, tile)]
        put_chunks(sent_ref, t, across(left, slope[...]).astype(jnp.bfloat16))
        return carry

    lax.fori_loop(0, hidden_width // tile, weight_grads, 0)


def kept_kernel(
    core_ref, rows_ref, slope_ref, received_ref, kept_one_ref, received_one_ref, both_ref
):
    nodes, hidden_width = slope_ref.shape
    tile = 256
    start = core_ref[0] * nodes

    def weight_grads(t, carry):
        left = rows_ref[pl.ds(pl.multiple_of(start, nodes), nodes), lanes_at(t, tile)]
        product = across(left, slope_ref[...])
        for c in range(tile // 16):
            chunk = t * (tile // 16) + c
            for lane in range(hidden_width // LANES):
                at = slice(lane * 16, (lane + 1) * 16)
                mine = product[c * 16 : (c + 1) * 16, lane * LANES : (lane + 1) * LANES]
                other = received_ref[chunk, at, :].astype(jnp.float32)
                both_ref[chunk, at, :] = (mine + other).astype(jnp.bfloat16)
            mine = kept_one_ref[chunk].astype(jnp.float32)
            other = received_one_ref[chunk].astype(jnp.float32)
            both_ref[chunk, LANES:, :] = (mine + other).astype(jnp.bfloat16)
        return carry

    lax.fori_loop(0, hidden_width // tile, weight_grads, 0)


def backward_kernel(
    core_ref, slope_ref, root_ref, near_ref, count_ref, flip_ref, hidden_ref, inputs_flip_ref,
    bias_two_ref, kept_ref, sent_ref, back, bias_grads,
):
    core = core_ref[0]
    nodes, hidden_width = slope_ref.shape
    tile = 256
    bias_grads[0:1, :] = bias_two_ref[0:1, :]
    inverse = 1.0 / count_ref[...].astype(jnp.float32)

    def backward(t, carry):
        cols = lanes_at(t, tile)
        back[:nodes, cols] = along(slope_ref[...], root_ref[cols, :]).astype(jnp.bfloat16)
        near = along(slope_ref[...], near_ref[cols, :])
        back[nodes:, cols] = (near * inverse).astype(jnp.bfloat16)
        return carry

    lax.fori_loop(0, hidden_width // tile, backward, 0)

    def first_grads(t, carry):
        cols = lanes_at(t, tile)
        table_grad = matmul(flip_ref[...], back[:, cols])
        grad = table_grad * (1.0 - jnp.exp(-hidden_ref[:, cols].astype(jnp.float32)))
        grad = grad.astype(jnp.bfloat16)
        bias_grads[1:2, cols] = jnp.sum(grad.astype(jnp.float32), axis=0, keepdims=True)
        product = matmul(inputs_flip_ref[...], grad).astype(jnp.bfloat16)
        low, high = product[:LANES], product[LANES:]
        mine, partner = jnp.where(core == 0, low, high), jnp.where(core == 0, high, low)
        for to_ref, product in ((kept_ref, mine), (sent_ref, partner)):
            for c in range(8):
                for lane in range(tile // LANES):
                    chunk = c * 8 + t * (tile // LANES) + lane
                    to_ref[chunk, 0:16, :] = product[
                        c * 16 : (c + 1) * 16, lane * LANES : (lane + 1) * LANES
                    ]
        return carry

    lax.fori_loop(0, hidden_width // tile, first_grads, 0)
    for place, to_ref in enumerate((kept_ref, sent_ref)):
        which = core ^ place
        to_ref[:, 16:, :] = jnp.zeros((to_ref.shape[0], 8, LANES), jnp.bfloat16)
        for lane in range(8):
            cols = slice(lane * LANES, (lane + 1) * LANES)
            row = jnp.where(which == 0, bias_grads[0:1, cols], bias_grads[1:2, cols])
            to_ref[lane, 16:, :] = jnp.broadcast_to(row, (8, LANES)).astype(jnp.bfloat16)


def shaped(*shape, dtype=jnp.bfloat16):
    return jax.ShapeDtypeStruct(shape, dtype)


def widen(from_ref, wide, root_hbm, near_hbm, to_root, sent):
    tiles = wide.shape[0] // LANES

    def copy(t, target):
        return pltpu.make_async_copy(wide.at[lanes_at(t)], target.at[lanes_at(t)], sent.at[t])

    def one_tile(t, carry):
        for c in range(8):
            at = pl.ds(pl.multiple_of(t * LANES + c * 16, 16), 16)
            for lane in range(8):
                piece = from_ref[t * 8 + c, lane * 16 : (lane + 1) * 16, :]
                wide[at, lane * LANES : (lane + 1) * LANES] = piece.astype(jnp.float32)

        @pl.when(to_root)
        def _():
            copy(t, root_hbm).start()

        @pl.when(jnp.logical_not(to_root))
        def _():
            copy(t, near_hbm).start()

        return carry

    lax.fori_loop(0, tiles, one_tile, 0)

    def finish():
        @pl.when(to_root)
        def _():
            for t in range(tiles):
                copy(t, root_hbm).wait()

        @pl.when(jnp.logical_not(to_root))
        def _():
            for t in range(tiles):
                copy(t, near_hbm).wait()

    return finish


def own_half_kernel(core_ref, kept_ref, root_hbm, near_hbm, wide, sent):
    widen(kept_ref, wide, root_hbm, near_hbm, core_ref[0] == 0, sent)()


def other_half_kernel(
    core_ref, z_ref, kept_ref, other_ref, root_in, near_in, root_hbm, near_hbm, first_root_ref,
    first_near_ref, bias_two_ref, bias_one_ref, wide, sent,
):
    del root_in, near_in
    core, z = core_ref[0], z_ref[0]
    even = core == 0
    finish = widen(other_ref, wide, root_hbm, near_hbm, core != 0, sent)
    here = lax.shift_right_logical(z, 1) == core
    base = lax.bitwise_and(z, 1) * 4
    for j, to_ref in enumerate((first_root_ref, first_near_ref)):
        for i in range(2):
            for lane in range(8):
                chunk = (base + 2 * j + i) * 8 + lane
                kept = kept_ref[chunk, LANES : LANES + 16, :].astype(jnp.float32)
                other = other_ref[chunk, LANES : LANES + 16, :].astype(jnp.float32)
                at, cols = slice(i * 16, (i + 1) * 16), slice(lane * LANES, (lane + 1) * LANES)
                to_ref[at, cols] = jnp.where(here, kept, other)
    for lane in range(8):
        kept = kept_ref[lane, LANES + 16 :, :].astype(jnp.float32)[0:1, :]
        other = other_ref[lane, LANES + 16 :, :].astype(jnp.float32)[0:1, :]
        cols = slice(lane * LANES, (lane + 1) * LANES)
        bias_two_ref[:, cols] = jnp.where(even, kept, other)
        bias_one_ref[:, cols] = jnp.where(even, other, kept)
    finish()


def spread(core, z, kept, hidden_width):
    f32 = jnp.float32
    square = shaped(hidden_width, hidden_width, dtype=f32)
    slab = shaped(32, hidden_width, dtype=f32)
    line = shaped(1, hidden_width, dtype=f32)
    scratch = [pltpu.VMEM(square.shape, f32), pltpu.SemaphoreType.DMA((hidden_width // LANES,))]
    other = lax.ppermute(kept, "core", [(0, 1), (1, 0)])
    root, near = pl.pallas_call(
        own_half_kernel,
        out_shape=(square, square),
        in_specs=[SMEM, VMEM],
        out_specs=(HBM, HBM),
        scratch_shapes=scratch,
        name="own_half",
        compiler_params=pltpu.CompilerParams(vmem_limit_bytes=8 << 20),
        cost_estimate=pl.CostEstimate(flops=1_000_000, bytes_accessed=7_000_000, transcendentals=0),
    )(core, kept)
    return pl.pallas_call(
        other_half_kernel,
        out_shape=(square, square, slab, slab, line, line),
        in_specs=[SMEM, SMEM, VMEM, VMEM, HBM, HBM],
        out_specs=(HBM, HBM) + (VMEM,) * 4,
        scratch_shapes=scratch,
        input_output_aliases={4: 0, 5: 1},
        name="other_half",
        compiler_params=pltpu.CompilerParams(vmem_limit_bytes=8 << 20),
        cost_estimate=pl.CostEstimate(flops=1_000_000, bytes_accessed=9_000_000, transcendentals=0),
    )(core, z, kept, other, root, near)


def weights_of_pair(own, z):
    first = lax.ppermute(own, "z", [(0, 1), (1, 0), (2, 3), (3, 2)])
    odd = lax.bitwise_and(z, 1) == 1
    return jnp.concatenate([jnp.where(odd, first, own), jnp.where(odd, own, first)], axis=0)


def weights_of_others(pair):
    return lax.ppermute(pair, "z", [(0, 3), (3, 0), (1, 2), (2, 1)])


def exchange(value, axes):
    return lax.all_to_all(value, axes, split_axis=0, concat_axis=0, tiled=True)


def step(
    features,
    first_adjacent,
    first_center,
    first_count,
    owner_map,
    first_root,
    first_near,
    first_bias,
    second_adjacent,
    second_center,
    second_count,
    second_root,
    second_near,
    second_bias,
    upstream,
):
    owners = 128
    hidden_width = first_root.shape[1]
    z = lax.axis_index("z")
    core = lax.axis_index("core")[None]
    pair = weights_of_pair(jnp.concatenate([first_root, first_near], axis=0), z)
    columns = jnp.concatenate([first_center[:, None], first_adjacent], axis=1).T
    packed = aggregate(features, columns, first_count[None], owner_map[None], owners)
    packed, pair = lax.optimization_barrier((packed, pair))
    other_pair = weights_of_others(pair)
    arrived = exchange(packed, AXES)
    count = second_count[:, None]
    picked, flipped = picks(second_adjacent, second_center[:, None], count, owners * 8)
    slots, depth = picked.shape[1], 2 * pair.shape[0]
    nodes = upstream.shape[0]
    layer_output, sent_two, hidden, rows, slope, inputs_flip, bias_grad = call(
        forward_kernel,
        (
            shaped(nodes, hidden_width),
            shaped(64, LANES, LANES),
            shaped(slots, hidden_width),
            shaped(2 * nodes, hidden_width),
            shaped(nodes, hidden_width),
            shaped(depth, slots),
            shaped(8, hidden_width, dtype=jnp.float32),
        ),
        12,
        smem=2,
        hbm=4,
        scratch=[
            pltpu.VMEM((slots, depth), jnp.bfloat16),
            pltpu.VMEM(picked.shape, jnp.bfloat16),
            pltpu.VMEM(second_root.shape, jnp.bfloat16),
            pltpu.VMEM(second_near.shape, jnp.bfloat16),
            pltpu.VMEM(upstream.shape, jnp.bfloat16),
            pltpu.SemaphoreType.DMA((4,)),
        ],
        limit=24,
        flops=6_000_000_000,
        moved=18_000_000,
        exps=3_000_000,
    )(
        core, z[None], arrived, pair, other_pair, first_bias[None], count, second_bias[None],
        in_hbm(picked), in_hbm(second_root), in_hbm(second_near), in_hbm(upstream),
    )
    received = lax.ppermute(sent_two, "core", [(0, 1), (1, 0)])
    kept_one, sent_one = call(
        backward_kernel, (shaped(64, 24, LANES), shaped(64, 24, LANES)), 9, smem=1,
        scratch=[
            pltpu.VMEM((2 * nodes, hidden_width), jnp.bfloat16),
            pltpu.VMEM((8, hidden_width), jnp.float32),
        ],
        limit=24, flops=4_700_000_000, moved=12_000_000, exps=1_000_000,
    )(core, slope, second_root, second_near, count, flipped, hidden, inputs_flip, bias_grad)
    received_one = lax.ppermute(sent_one, "core", [(0, 1), (1, 0)])
    (both,) = call(
        kept_kernel, (shaped(64, CHUNK, LANES),), 6, smem=1, limit=20,
        flops=1_000_000_000, moved=7_000_000,
    )(core, rows, slope, received, kept_one, received_one)
    terms = exchange(both, CHIPS)
    total = jnp.sum(terms.astype(jnp.float32), axis=0).astype(jnp.bfloat16)
    mine = exchange(jnp.broadcast_to(total[None], terms.shape), CHIPS)
    root_two, near_two, root_one, near_one, bias_two, bias_one = spread(
        core, z[None], mine, hidden_width
    )
    return (layer_output, root_two, near_two, bias_two[0], root_one, near_one, bias_one[0])


def solution(mesh):
    chips = Mesh(mesh.devices.reshape(4, 4, 4, 2), AXES)
    trainer = ("x", "y", "core")
    return jax.shard_map(
        step,
        mesh=chips,
        in_specs=(
            P("z", trainer),
            P(trainer, None),
            P(trainer),
            P(trainer),
            P(trainer),
            P("z", None),
            P("z", None),
            P(),
            P(AXES, None),
            P(AXES),
            P(AXES),
            P(),
            P(),
            P(),
            P(AXES, None),
        ),
        out_specs=(
            P(AXES, None),
            P(),
            P(),
            P(),
            P("z", None),
            P("z", None),
            P(),
        ),
        check_vma=False,
    )
```
